32 devices in a mesh: dp: 8 (over z, x), tensor: 4 (over y, core).
Axes of the slice: x: 2, y: 2, z: 4, core: 2. Of those that a mesh axis runs over, the one named last changes fastest.
Arguments:
- inputs: float32 [4, 8192, 768], P(None, ('dp', 'tensor')), may hold values from -6 to 6
- w_qkv: float32 [3, 768, 768], P(None, None, 'tensor'), may hold values from -0.21875 to 0.21875
- w_out: float32 [768, 768], P('tensor'), may hold values from -3 to 3
- w_gate_up: float32 [2, 768, 2048], P(None, None, 'tensor'), may hold values from -0.21875 to 0.21875
- w_down: float32 [2048, 768], P('tensor'), may hold values from -0.125 to 0.125
- gain_attn: float32 [768], replicated, may hold values from 0.5 to 1.5
- gain_mlp: float32 [768], replicated, may hold values from 0.5 to 1.5
- piece_starts: int32 [4, 8, 2], P(None, 'dp'), may hold values from 0 to 768, as said below
- out_grad: float32 [4, 8192, 768], P(None, ('dp', 'tensor')), may hold values from -6 to 6
Outputs:
- outputs: float32 [4, 8192, 768], P(None, ('dp', 'tensor'))
- input_grad: float32 [4, 8192, 768], P(None, ('dp', 'tensor'))
- grad_qkv: float32 [3, 768, 768], P(None, None, 'tensor')
- grad_out: float32 [768, 768], P('tensor')
- grad_gate_up: float32 [2, 768, 2048], P(None, None, 'tensor')
- grad_down: float32 [2048, 768], P('tensor')
- grad_gain_attn: float32 [768], replicated
- grad_gain_mlp: float32 [768], replicated
The draws below stay inside these ranges and needn't reach their ends.
Inputs may be any that keep to these rules, and one draw needn't show every extreme that they name: `piece_starts`: each sequence has 2 image pieces of 256 tokens; the k-th lies wholly inside the k-th of 2 equal parts of the sequence, so pieces never intersect.
All inputs are finite; a program needn't handle non-finite values.
Results may differ from the reference program's by a relative error of at most 0.02.
The reference program's roundings to bfloat16 on the way count: a program that leaves them out, or rounds other values in their place, can miss the bound.
Values may be sent and summed in bfloat16 or wider, within the bound.
No kernel may reach another device: no remote copies, remote signals or barrier semaphores. Data moves between devices by JAX's collectives and lax.ppermute only.
A program may use at most 320 MiB of HBM per device.

```python
import jax
import jax.numpy as jnp
from jax import lax

D = 768
HEADS = 12
HD = 64
FF = 2048
LEN = 1024
PIECE = 256
NPIECE = 2
MICRO = 4
SEQ_MB = 1
SEQ_ALL = 8
ROWS = 8192
N_DP = 8
N_TENSOR = 4


def draw_piece_starts(key, part):
    span_len = LEN // NPIECE
    shape_all = (MICRO, SEQ_ALL, NPIECE)
    offsets = jax.random.randint(key, shape_all, 0, span_len - PIECE + 1)
    piece_index = lax.broadcasted_iota(jnp.int32, shape_all, 2)
    micro_index = lax.broadcasted_iota(jnp.int32, shape_all, 0)
    seq_index = lax.broadcasted_iota(jnp.int32, shape_all, 1)
    starts = offsets + piece_index * span_len
    corner = (micro_index == 0) & (seq_index == 0)
    starts = jnp.where(corner & (piece_index == 0), 0, starts)
    starts = jnp.where(corner & (piece_index == NPIECE - 1), LEN - PIECE, starts)
    return starts.astype(jnp.int32)


def block_scale(rng, shape, split, low, largest):
    def one(dim, shards_of):
        draws = jax.random.uniform(jax.random.fold_in(jax.random.fold_in(rng, 6), dim), (shards_of,), jnp.float32, low / len(split), largest / len(split))
        return jnp.repeat(jnp.exp(draws), shape[dim] // shards_of).reshape((-1,) + (1,) * (len(shape) - dim - 1))

    loudness = one(*split[0])
    for cut in split[1:]:
        loudness = loudness * one(*cut)
    return loudness


def normal_values(stream_key, dims, scale, most, shards=(), held_as=jnp.bfloat16):
    level = block_scale(stream_key, dims, shards, -0.22, 0.18) if shards else 1.0
    result = jax.random.normal(stream_key, dims, jnp.float32) * scale * level
    return jnp.minimum(jnp.maximum(result, -most), most).astype(held_as)


def setup_inputs(seed: int = 0) -> dict:
    seeds = jax.random.split(jax.random.key(seed), 10)
    return {
        "inputs": normal_values(seeds[0], (MICRO, ROWS, D), 1.0, 6.0, ((1, 32),), jnp.float32),
        "w_qkv": normal_values(seeds[1], (3, D, HEADS * HD), D ** -0.5, 0.21875, ((2, 4),), jnp.float32),
        "w_out": normal_values(seeds[2], (HEADS * HD, D), (HD // 16) ** -0.5, 3.0, ((0, 4),), jnp.float32),
        "w_gate_up": normal_values(seeds[3], (2, D, FF), D ** -0.5, 0.21875, ((2, 4),), jnp.float32),
        "w_down": normal_values(seeds[4], (FF, D), FF ** -0.5, 0.125, ((0, 4),), jnp.float32),
        "gain_attn": jnp.clip(1.0 + 0.1 * jax.random.normal(seeds[5], (D,), jnp.float32), 0.5, 1.5),
        "gain_mlp": jnp.clip(1.0 + 0.1 * jax.random.normal(seeds[6], (D,), jnp.float32), 0.5, 1.5),
        "piece_starts": draw_piece_starts(jax.random.fold_in(seeds[9], 71), 0),
        "out_grad": normal_values(seeds[8], (MICRO, ROWS, D), 1.0, 6.0, ((1, 32),), jnp.float32),
    }


epsilon = 1e-06
highest = lax.Precision.HIGHEST

@jax.custom_vjp
def low(v):
    return lax.optimization_barrier(v.astype(jnp.bfloat16)).astype(jnp.float32)

@jax.custom_vjp
def low_back(v):
    return v

def low_keep(v):
    return (low(v), None)

def low_pass(kept, grad):
    return (grad,)

def back_keep(v):
    return (v, None)

def back_low(kept, grad):
    return (low(grad),)
low.defvjp(low_keep, low_pass)
low_back.defvjp(back_keep, back_low)

def rope_tables(length, width):
    halfway = width // 2
    inverse = 10000.0 ** (-jnp.arange(halfway, dtype=jnp.float32) * 2.0 / width)
    angles = jnp.arange(length, dtype=jnp.float32)[:, None] * inverse[None, :]
    return (jnp.cos(angles)[:, None, :], jnp.sin(angles)[:, None, :])

def rotate(vector, cosine, sine):
    halfway = vector.shape[-1] // 2
    first = vector[..., :halfway]
    second = vector[..., halfway:]
    return jnp.concatenate([first * cosine - second * sine, second * cosine + first * sine], axis=-1)

def piece_mask(starts, length, piece_len):
    position = jnp.arange(length, dtype=jnp.int32)
    inside = (position[:, None] >= starts[None, :]) & (position[:, None] < starts[None, :] + piece_len)
    numbers = jnp.arange(1, starts.shape[0] + 1, dtype=jnp.int32)
    labels = lax.optimization_barrier(jnp.sum(inside.astype(jnp.int32) * numbers[None, :], axis=1))
    causal = position[None, :] <= position[:, None]
    same_piece = (labels[:, None] == labels[None, :]) & (labels[:, None] > 0)
    return causal | same_piece

def rms_norm(tokens_mb, gain):
    return tokens_mb * lax.rsqrt(lax.optimization_barrier(jnp.mean(tokens_mb * tokens_mb, axis=-1, keepdims=True)) + epsilon) * gain

def attend(queries, keys_rot, values_seq, allowed):
    factor = queries.shape[-1] ** (-0.5)
    scores = jnp.einsum('qhd,khd->hqk', queries, keys_rot, precision=highest) * factor
    scores = low_back(scores)
    scores = jnp.where(allowed[None], scores, -jnp.inf)
    weights_soft = low(jax.nn.softmax(scores, axis=-1))
    return jnp.einsum('hqk,khd->qhd', weights_soft, values_seq, precision=highest)

def group_layer(weights, tokens_mb, starts):
    w_proj, w_mix, w_pair, w_last, gain_one, gain_two = weights
    heads_local = HEADS // N_TENSOR
    width_local = heads_local * HD
    hidden_local = FF // N_TENSOR
    span_rows = tokens_mb.shape[0]
    seq_count = starts.shape[0]
    cosine, sine = rope_tables(LEN, HD)
    allowed = jax.vmap(lambda row_starts: piece_mask(row_starts, LEN, PIECE))(starts)
    normed = low(rms_norm(tokens_mb, gain_one))
    branch_parts = []
    for rank in range(N_TENSOR):
        shard_in = low_back(normed)
        columns = slice(rank * width_local, (rank + 1) * width_local)
        projected = jnp.einsum('gd,cdk->cgk', shard_in, w_proj[:, :, columns], precision=highest)
        projected = low_back(projected).reshape(3, seq_count, LEN, heads_local, HD)
        queries = low(rotate(projected[0], cosine, sine))
        keys_rot = low(rotate(projected[1], cosine, sine))
        values_seq = low(projected[2])
        mixed = jax.vmap(attend)(queries, keys_rot, values_seq, allowed)
        mixed = low_back(low(mixed.reshape(span_rows, width_local)))
        branch_parts.append(low(jnp.dot(mixed, w_mix[columns, :], precision=highest)))
    after = tokens_mb + low_back(sum(branch_parts))
    normed_two = low(rms_norm(after, gain_two))
    mlp_parts = []
    for rank in range(N_TENSOR):
        shard_in = low_back(normed_two)
        columns = slice(rank * hidden_local, (rank + 1) * hidden_local)
        gate_up = low_back(jnp.einsum('gd,cdf->cgf', shard_in, w_pair[:, :, columns], precision=highest))
        hidden = low(jax.nn.silu(gate_up[0]) * gate_up[1])
        mlp_parts.append(low(jnp.dot(hidden, w_last[columns, :], precision=highest)))
    return after + low_back(sum(mlp_parts))

def reference(inputs, w_qkv, w_out, w_gate_up, w_down, gain_attn, gain_mlp, piece_starts, out_grad):
    groups = MICRO * N_DP
    span_rows = SEQ_MB * LEN

    def forward(inputs, w_qkv, w_out, w_gate_up, w_down, gain_attn, gain_mlp):
        weights = (low(w_qkv), low(w_out), low(w_gate_up), low(w_down), gain_attn, gain_mlp)
        tokens_all = inputs.reshape(groups, span_rows, D)
        starts_all = piece_starts.reshape(groups, SEQ_MB, NPIECE)
        stepper = jax.checkpoint(lambda operands: group_layer(weights, operands[0], operands[1]))
        return lax.map(stepper, (tokens_all, starts_all)).reshape(inputs.shape)
    outputs, pullback = jax.vjp(forward, inputs, w_qkv, w_out, w_gate_up, w_down, gain_attn, gain_mlp)
    grads = pullback(out_grad)
    return (outputs, grads[0], grads[1], grads[2], grads[3], grads[4], grads[5], grads[6])
```

```python
import functools
import jax
import jax.numpy as jnp
import numpy as np
from jax import lax
from jax.experimental import pallas as pl
from jax.experimental.pallas import tpu as pltpu
from jax.sharding import PartitionSpec as P

HD = 64
LEN = 1024
PIECE = 256
HALF = 512
EPS = 1e-06
F32 = jnp.float32
BF16 = jnp.bfloat16
VMEM_LIMIT = 60 * 1024 * 1024


def nn(a, b):
    return lax.dot_general(a, b, (((1,), (0,)), ((), ())), preferred_element_type=F32)


def nt(a, b):
    return lax.dot_general(a, b, (((1,), (1,)), ((), ())), preferred_element_type=F32)


def call(body, name, out_shape, args, flops, trans=0, **kw):
    read = sum(int(np.prod(a.shape)) * a.dtype.itemsize for a in args)
    made = sum(int(np.prod(o.shape)) * np.dtype(o.dtype).itemsize for o in out_shape)
    return pl.pallas_call(
        body,
        name=name,
        out_shape=out_shape,
        compiler_params=pltpu.CompilerParams(vmem_limit_bytes=VMEM_LIMIT),
        cost_estimate=pl.CostEstimate(
            flops=int(flops), bytes_accessed=read + made, transcendentals=int(trans)
        ),
        **kw,
    )(*args)


def struct(shape, dtype):
    return jax.ShapeDtypeStruct(shape, dtype)


def project(n1_ref, weights, cos_ref, sin_ref, q_ref, k_ref, v_ref):
    step = 256
    for block in range(LEN // step):
        cols = slice(block * step, (block + 1) * step)
        rows = n1_ref[cols, :]
        cosine = cos_ref[:, cols]
        sine = sin_ref[:, cols]
        for slot, w_ref in enumerate(weights):
            for part, ref in ((0, q_ref), (1, k_ref), (2, v_ref)):
                made = nt(w_ref[part], rows)
                for head in range(3):
                    low = made[head * HD : head * HD + HD // 2]
                    high = made[head * HD + HD // 2 : (head + 1) * HD]
                    if part < 2:
                        low, high = low * cosine - high * sine, high * cosine + low * sine
                    if part == 0:
                        low, high = low * HD**-0.5, high * HD**-0.5
                    at = slot * HD
                    ref[head, at : at + HD // 2, cols] = low.astype(BF16)
                    ref[head, at + HD // 2 : at + HD, cols] = high.astype(BF16)


def in_order(here, pieces, ref):
    step = ref.shape[0] // 4
    for quarter in range(4):
        for slot, piece in enumerate(pieces):

            @pl.when((here ^ slot) == quarter)
            def _():
                ref[quarter * step : (quarter + 1) * step, :] = piece[...]


def project_first_body(meta_ref, p0, p1, p2, p3, gain_ref, w0, w1, cos_ref, sin_ref, x_ref, n1_ref, q_ref, k_ref, v_ref):
    step = 256
    gain = gain_ref[...]
    in_order(meta_ref[2], (p0, p1, p2, p3), x_ref)
    for block in range(LEN // step):
        rows = slice(block * step, (block + 1) * step)
        x = x_ref[rows, :].astype(F32)
        scale = lax.rsqrt(jnp.mean(x * x, axis=-1, keepdims=True) + EPS)
        n1_ref[rows, :] = (x * scale * gain).astype(BF16)
    project(n1_ref, (w0, w1), cos_ref, sin_ref, q_ref, k_ref, v_ref)


def project_next_body(n1_ref, w0, w1, cos_ref, sin_ref, q_ref, k_ref, v_ref):
    project(n1_ref, (w0, w1), cos_ref, sin_ref, q_ref, k_ref, v_ref)


HEADS3 = (3, 2 * HD, LEN)


VM = pl.BlockSpec(memory_space=pltpu.VMEM)
SM = pl.BlockSpec(memory_space=pltpu.SMEM)


def project_first(meta, pieces, gain, w0, w1, cosine, sine):
    width = gain.shape[1]
    out = [struct((LEN, width), BF16)] * 2 + [struct(HEADS3, BF16)] * 3
    args = (meta, *pieces, gain, w0, w1, cosine, sine)
    return call(
        project_first_body,
        "project_first",
        out,
        args,
        2 * LEN * width * 18 * HD,
        in_specs=[SM] + [VM] * (len(args) - 1),
        out_specs=[VM] * len(out),
    )


def project_next(n1, w0, w1, cosine, sine):
    width = n1.shape[1]
    out = [struct(HEADS3, BF16)] * 3
    return call(project_next_body, "project_next", out, (n1, w0, w1, cosine, sine), 2 * LEN * width * 18 * HD)


def limits(starts_ref):
    pos = lax.broadcasted_iota(jnp.int32, (1, LEN), 1)
    lim = pos
    for piece in range(2):
        first = starts_ref[piece]
        lim = jnp.where((pos >= first) & (pos < first + PIECE), first + PIECE - 1, lim)
    return lim


def one_head(block, head):
    zero = jnp.zeros((HD, block.shape[1]), block.dtype)
    part = block[head * HD : (head + 1) * HD]
    return jnp.concatenate([part, zero] if head == 0 else [zero, part], axis=0)


NEG = -1e30


def attend_body(qb, starts_ref, q_ref, k_ref, v_ref, mt_ref, m_ref, lse_ref):
    lim = limits(starts_ref)
    k_rows = k_ref[0].T
    for head in range(2):
        q_one = one_head(q_ref[0], head)
        v_one = v_ref[0, head * HD : (head + 1) * HD, :]
        for block in range(LEN // qb):
            cols = slice(block * qb, (block + 1) * qb)
            keys = HALF if (block + 1) * qb <= HALF else LEN
            scores = nn(k_rows[:keys], q_one[:, cols])
            edge = scores[keys - HALF :]
            pos = lax.broadcasted_iota(jnp.int32, (HALF, qb), 0) + (keys - HALF)
            edge = jnp.where(pos <= lim[:, cols], edge, NEG)
            most = jnp.max(edge, axis=0, keepdims=True)
            if keys > HALF:
                body = scores[:HALF]
                most = jnp.maximum(most, jnp.max(body, axis=0, keepdims=True))
            soft = jnp.exp(edge - most)
            total = jnp.sum(soft, axis=0, keepdims=True)
            mixed = nn(v_one[:, keys - HALF : keys], soft.astype(BF16))
            if keys > HALF:
                soft = jnp.exp(body - most)
                total = total + jnp.sum(soft, axis=0, keepdims=True)
                mixed = mixed + nn(v_one[:, :HALF], soft.astype(BF16))
            mt_ref[0, head * HD : (head + 1) * HD, cols] = (mixed * (1.0 / total)).astype(BF16)
            lse_ref[0, head : head + 1, cols] = most + jnp.log(total)
    m_ref[...] = mt_ref[0].T


def attend(starts, q, k, v, qb=256):
    block = pl.BlockSpec((1, 2 * HD, LEN), lambda i: (i, 0, 0))
    out = [struct(HEADS3, BF16), struct((LEN, 6 * HD), BF16), struct((3, 2, LEN), F32)]
    return call(
        functools.partial(attend_body, qb),
        "attend",
        out,
        (starts, q, k, v),
        6 * 2 * LEN * LEN * 256 * 2 * 0.75,
        6 * LEN * LEN * 0.75,
        grid=(3,),
        in_specs=[pl.BlockSpec(memory_space=pltpu.SMEM), block, block, block],
        out_specs=[
            block,
            pl.BlockSpec((LEN, 2 * HD), lambda i: (0, i)),
            pl.BlockSpec((1, 2, LEN), lambda i: (i, 0, 0)),
        ],
    )


def attend_back_body(qb, starts_ref, cos_ref, sin_ref, n1_ref, *refs):
    sets = (refs[0:5], refs[5:10])
    do_ref = refs[10]
    dt_ref, dw_ref, acc_ref = refs[11:]
    lim = limits(starts_ref)
    for which, (q_ref, k_ref, v_ref, mt_ref, lse_ref) in enumerate(sets):
        q = q_ref[0]
        k = k_ref[0]
        v = v_ref[0]
        do = do_ref[which * 2 * HD : (which + 1) * 2 * HD, :]
        k_rows = k.T
        v_rows = v.T
        both = do.astype(F32) * mt_ref[0].astype(F32)
        for head in range(2):
            mine = slice(head * HD, (head + 1) * HD)
            inner = jnp.sum(both[mine], axis=0, keepdims=True)
            q_one = one_head(q, head)
            do_one = one_head(do, head)
            lse = lse_ref[0, head : head + 1, :]
            for block in range(LEN // qb):
                cols = slice(block * qb, (block + 1) * qb)
                wide = (block + 1) * qb > HALF
                dq = None
                for part in range(2 if wide else 1):
                    keys = slice(part * HALF, (part + 1) * HALF)
                    scores = nn(k_rows[keys], q_one[:, cols])
                    if part == (1 if wide else 0):
                        pos = lax.broadcasted_iota(jnp.int32, (HALF, qb), 0) + part * HALF
                        scores = jnp.where(pos <= lim[:, cols], scores, NEG)
                    soft = jnp.exp(scores - lse[:, cols])
                    grad = nn(v_rows[keys], do_one[:, cols])
                    grad = (soft * (grad - inner[:, cols])).astype(BF16)
                    more = nn(k[mine, keys], grad)
                    dq = more if dq is None else dq + more
                    dk = nt(q[mine, cols], grad)
                    dv = nt(do[mine, cols], soft.astype(BF16))
                    fresh = block == (0 if part == 0 else HALF // qb)
                    if fresh:
                        acc_ref[1, mine, keys] = dk
                        acc_ref[2, mine, keys] = dv
                    else:
                        acc_ref[1, mine, keys] += dk
                        acc_ref[2, mine, keys] += dv
                acc_ref[0, mine, cols] = dq * HD**-0.5
        cosine = cos_ref[...]
        sine = sin_ref[...]
        for part in range(3):
            for head in range(2):
                at = head * HD
                low = acc_ref[part, at : at + HD // 2, :]
                high = acc_ref[part, at + HD // 2 : at + HD, :]
                if part < 2:
                    low, high = low * cosine + high * sine, high * cosine - low * sine
                to = which * 2 * HD + at
                dt_ref[part, to : to + HD // 2, :] = low.astype(BF16)
                dt_ref[part, to + HD // 2 : to + HD, :] = high.astype(BF16)
    for part in range(3):
        made = nn(dt_ref[part], n1_ref[...])
        for slot in range(4):
            dw_ref[slot, part] = made[slot * HD : (slot + 1) * HD].astype(BF16)


def attend_back(turn, starts, cosine, sine, n1, sets, do, qb=256):
    width = n1.shape[1]
    head = pl.BlockSpec((1, 2 * HD, LEN), lambda i: (turn, 0, 0))
    full = lambda a: pl.BlockSpec(a.shape, lambda i, n=a.ndim: (0,) * n)
    lse = pl.BlockSpec((1, 2, LEN), lambda i: (turn, 0, 0))
    args = (starts, cosine, sine, n1, *sets[0], *sets[1], do)
    out = [struct((3, 4 * HD, LEN), BF16), struct((4, 3, HD, width), BF16)]
    return call(
        functools.partial(attend_back_body, qb),
        "attend_back",
        out,
        args,
        4 * 5 * LEN * LEN * 256 * 2 * 0.75 + 2 * LEN * width * 12 * HD,
        4 * LEN * LEN * 0.75,
        grid=(1,),
        in_specs=[pl.BlockSpec(memory_space=pltpu.SMEM), full(cosine), full(sine), full(n1)]
        + [head, head, head, head, lse] * 2
        + [pl.BlockSpec((4 * HD, LEN), lambda i: (turn, 0))],
        out_specs=[full(o) for o in out],
        scratch_shapes=[pltpu.VMEM((3, 2 * HD, LEN), F32)],
    )


def turn_rows(w_refs):
    return jnp.concatenate(
        [w[turn * HD : (turn + 1) * HD, :] for turn in range(3) for w in w_refs], axis=0
    )


def after_body(
    meta_ref, x_ref, ma_ref, mb_ref, w0, w1, w2, w3, gain_ref, g0, g1, g2, g3,
    after_ref, n2_ref, n2t_ref, g_ref, gt_ref,
):
    slot = pl.program_id(0) ^ meta_ref[2]
    for which, piece in enumerate((g0, g1, g2, g3)):

        @pl.when(slot == which)
        def _():
            g_ref[...] = piece[...]

    first = turn_rows((w0, w1))
    second = turn_rows((w2, w3))
    after = x_ref[...].astype(F32) + nn(ma_ref[...], first) + nn(mb_ref[...], second)
    after_ref[...] = after
    scale = lax.rsqrt(jnp.mean(after * after, axis=-1, keepdims=True) + EPS)
    normed = (after * scale * gain_ref[...]).astype(BF16)
    n2_ref[...] = normed
    n2t_ref[...] = normed.T
    gt_ref[...] = g_ref[...].T


def after_attention(meta, x, mixed_a, mixed_b, wo, gain, g):
    width = x.shape[1]
    step = 256
    rows = lambda n: pl.BlockSpec((step, n), lambda i: (i, 0))
    cols = pl.BlockSpec((width, step), lambda i: (0, i))
    full = lambda a: pl.BlockSpec(a.shape, lambda i, n=a.ndim: (0,) * n)
    args = (meta, x, mixed_a, mixed_b, *wo, gain, *g)
    out = [
        struct((LEN, width), F32),
        struct((LEN, width), BF16),
        struct((width, LEN), BF16),
        struct((LEN, width), BF16),
        struct((width, LEN), BF16),
    ]
    return call(
        after_body,
        "after_attention",
        out,
        args,
        2 * LEN * width * width,
        grid=(LEN // step,),
        in_specs=[SM, rows(width), rows(6 * HD), rows(6 * HD)]
        + [full(w) for w in wo]
        + [full(gain)]
        + [full(p) for p in g],
        out_specs=[rows(width), rows(width), cols, rows(width), cols],
    )


def mlp_body(split, meta_ref, n2_ref, n2t_ref, g_ref, gt_ref, *refs):
    block = 256
    step = 256
    if split:
        gua0, gub0, gua1, gub1, wda0, wdb0, wda1, wdb1 = refs[:8]
        out_ref, back_ref, dw0, dw1, hid, dga, dup, gus, wds = refs[8:]
        bit = meta_ref[3]
        for slot, (one, two) in enumerate(((gua0, gub0), (gua1, gub1))):
            gus[slot, bit] = one[0]
            gus[slot, 1 - bit] = two[0]
        for slot, (one, two) in enumerate(((wda0, wdb0), (wda1, wdb1))):
            wds[slot, bit] = one[0]
            wds[slot, 1 - bit] = two[0]
        take_gu = lambda slot, which, cols: gus[slot, which, :, cols]
        take_wd = lambda slot, part: wds[slot, part]
    else:
        gu0, gu1, wd0, wd1 = refs[:4]
        out_ref, back_ref, dw0, dw1, hid, dga, dup = refs[4:]
        take_gu = lambda slot, which, cols: (gu0, gu1)[slot][which, :, cols]
        take_wd = lambda slot, part: (wd0, wd1)[slot][part]
    out_ref[...] = jnp.zeros_like(out_ref)
    back_ref[...] = jnp.zeros_like(back_ref)
    for slot, dw_ref in ((1, dw1), (0, dw0)):
        for part in range(2):
            cols = slice(part * block, (part + 1) * block)
            wg = take_gu(slot, 0, cols)
            wu = take_gu(slot, 1, cols)
            wl = take_wd(slot, part)

            @pl.loop(0, LEN // step)
            def _(turn):
                rows = pl.ds(pl.multiple_of(turn * step, step), step)
                n2 = n2_ref[rows, :]
                gate = nn(n2, wg)
                up = nn(n2, wu)
                grad = nt(g_ref[rows, :], wl)
                sigma = 1.0 / (1.0 + jnp.exp(-gate))
                silu = gate * sigma
                hidden = (silu * up).astype(BF16)
                grad_up = (grad * silu).astype(BF16)
                grad_gate = (grad * up * (sigma * (1.0 + gate * (1.0 - sigma)))).astype(BF16)
                hid[rows, :] = hidden
                dga[rows, :] = grad_gate
                dup[rows, :] = grad_up
                out_ref[rows, :] += nn(hidden, wl)
                back_ref[rows, :] += nt(grad_gate, wg) + nt(grad_up, wu)

            dw_ref[0, :, cols] = nn(n2t_ref[...], dga[...]).astype(BF16)
            dw_ref[1, :, cols] = nn(n2t_ref[...], dup[...]).astype(BF16)
            dw_ref[2, :, cols] = nn(gt_ref[...], hid[...]).astype(BF16)


def mlp(meta, n2, n2t, g, gt, weights):
    width = n2.shape[1]
    split = len(weights) == 8
    units = 512
    out = [
        struct((LEN, width), F32),
        struct((LEN, width), F32),
        struct((3, width, units), BF16),
        struct((3, width, units), BF16),
    ]
    args = (meta, n2, n2t, g, gt, *weights)
    scratch = [pltpu.VMEM((LEN, 256), BF16)] * 3
    if split:
        scratch += [pltpu.VMEM((2, 2, width, units), BF16), pltpu.VMEM((2, 2, units // 2, width), BF16)]
    return call(
        functools.partial(mlp_body, split),
        "mlp",
        out,
        args,
        2 * LEN * width * units * 2 * 9,
        LEN * units * 2,
        in_specs=[SM] + [VM] * (len(args) - 1),
        out_specs=[VM] * 4,
        scratch_shapes=scratch,
    )


def norm_back(grad, value, gain):
    scale = lax.rsqrt(jnp.mean(value * value, axis=-1, keepdims=True) + EPS)
    unit = value * scale
    gain_grad = jnp.sum(grad * unit, axis=0, keepdims=True)
    e = grad * gain
    return scale * (e - unit * jnp.mean(e * unit, axis=-1, keepdims=True)), gain_grad


def give(meta_ref, value, refs):
    slot = pl.program_id(0) ^ meta_ref[2]
    for which, ref in enumerate(refs):

        @pl.when(slot == which)
        def _():
            ref[...] = value


def middle_body(
    meta_ref, x_ref, after_ref, oa_ref, ob_ref, ba_ref, bb_ref, g_ref, gain_ref, mta_ref, mtb_ref,
    w0, w1, w2, w3, e0, e1, e2, e3, da_ref, do_ref, dwo_ref, gain_out, acc,
):
    step = pl.program_id(0)
    after = after_ref[...]
    delta = (after - x_ref[...].astype(F32) + oa_ref[...] + ob_ref[...]).astype(BF16)
    give(meta_ref, delta, (e0, e1, e2, e3))
    back, gain_grad = norm_back(ba_ref[...] + bb_ref[...], after, gain_ref[...])
    grad_after = g_ref[...].astype(F32) + back
    da_ref[...] = grad_after
    low = grad_after.astype(BF16)

    @pl.when(step == 0)
    def _():
        gain_out[...] = jnp.zeros_like(gain_out)
        acc[...] = jnp.zeros_like(acc)

    gain_out[...] += gain_grad
    weights = turn_rows((w0, w1, w2, w3))
    do_ref[...] = nt(weights, low).astype(BF16)
    for turn in range(3):
        for which, mt in enumerate((mta_ref, mtb_ref)):
            acc[turn, which] += nn(mt[turn], low)

    @pl.when(step == pl.num_programs(0) - 1)
    def _():
        for turn in range(3):
            for slot in range(4):
                at = (slot % 2) * HD
                dwo_ref[slot, turn] = acc[turn, slot // 2, at : at + HD, :].astype(BF16)


def middle(meta, x, after, outs, backs, g, gain, mts, wo):
    width = x.shape[1]
    step = 256
    rows = pl.BlockSpec((step, width), lambda i: (i, 0))
    full = lambda a: pl.BlockSpec(a.shape, lambda i, n=a.ndim: (0,) * n)
    heads = pl.BlockSpec((3, 2 * HD, step), lambda i: (0, 0, i))
    args = (meta, x, after, *outs, *backs, g, gain, *mts, *wo)
    out = [struct((step, width), BF16)] * 4 + [
        struct((LEN, width), F32),
        struct((12 * HD, LEN), BF16),
        struct((4, 3, HD, width), BF16),
        struct((1, width), F32),
    ]
    return call(
        middle_body,
        "middle",
        out,
        args,
        4 * LEN * width * width,
        grid=(LEN // step,),
        in_specs=[SM] + [rows] * 7 + [full(gain), heads, heads] + [full(w) for w in wo],
        out_specs=[full(o) for o in out[:4]]
        + [rows, pl.BlockSpec((12 * HD, step), lambda i: (0, i)), full(out[6]), full(out[7])],
        scratch_shapes=[pltpu.VMEM((3, 2, 2 * HD, width), F32)],
    )


def token_grad_body(turns, last, *refs):
    dts = refs[: len(turns)]
    weights = refs[len(turns) : len(turns) + 4]
    rest = refs[len(turns) + 4 :]
    step = pl.program_id(0)
    total = None
    for turn, dt in zip(turns, dts):
        for part in range(3):
            w = jnp.concatenate([w[part, turn * HD : (turn + 1) * HD, :] for w in weights], axis=0)
            more = nn(dt[part].T, w)
            total = more if total is None else total + more
    if not last:
        rest[0][...] = total
        return
    meta_ref, before_ref, x_ref, da_ref, g_ref, gain_ref, e0, e1, e2, e3, gain_out = rest
    total = total + before_ref[...]
    back, gain_grad = norm_back(total, x_ref[...].astype(F32), gain_ref[...])
    give(meta_ref, (da_ref[...] - g_ref[...].astype(F32) + back).astype(BF16), (e0, e1, e2, e3))

    @pl.when(step == 0)
    def _():
        gain_out[...] = jnp.zeros_like(gain_out)

    gain_out[...] += gain_grad


def token_grad(turns, dts, weights, rest=None):
    width = weights[0].shape[2]
    step = 256
    rows = pl.BlockSpec((step, width), lambda i: (i, 0))
    full = lambda a: pl.BlockSpec(a.shape, lambda i, n=a.ndim: (0,) * n)
    cols = pl.BlockSpec((3, 4 * HD, step), lambda i: (0, 0, i))
    specs = [cols] * len(dts) + [full(w) for w in weights]
    args = (*dts, *weights)
    if rest is None:
        out = [struct((LEN, width), F32)]
        out_specs = [rows]
    else:
        out = [struct((step, width), BF16)] * 4 + [struct((1, width), F32)]
        out_specs = [full(o) for o in out]
        specs = specs + [SM] + [rows] * 4 + [full(rest[5])]
        args = args + tuple(rest)
    return call(
        functools.partial(token_grad_body, turns, rest is not None),
        "token_grad",
        out,
        args,
        2 * LEN * width * 12 * HD * len(turns),
        grid=(LEN // step,),
        in_specs=specs,
        out_specs=out_specs,
    )


def rope_tables(length, width):
    halfway = width // 2
    inverse = 10000.0 ** (-jnp.arange(halfway, dtype=F32) * 2.0 / width)
    angles = inverse[:, None] * jnp.arange(length, dtype=F32)[None, :]
    return jnp.cos(angles), jnp.sin(angles)


def swap(value, axis, size, mask):
    return lax.ppermute(value, axis, [(i, i ^ mask) for i in range(size)])


def sum_split_body(n, count, index_ref, *refs):
    ins, outs = refs[:count], refs[count:]
    total = ins[0][0].astype(F32)
    for ref in ins[1:]:
        total = total + ref[0].astype(F32)
    total = total.astype(BF16)
    slot = pl.program_id(0) ^ index_ref[0]
    for which, ref in enumerate(outs):

        @pl.when(slot == which)
        def _():
            ref[...] = total


def sum_split(addends, n, index):
    rows, cols = addends[0].shape
    parts = [a.reshape(n, rows // n, cols) for a in addends]
    out = [struct((rows // n, cols), BF16)] * n
    full = pl.BlockSpec((rows // n, cols), lambda i: (0, 0))
    return call(
        functools.partial(sum_split_body, n, len(addends)),
        "sum_split",
        out,
        (index.reshape(1), *parts),
        rows * cols * len(addends),
        grid=(n,),
        in_specs=[SM] + [pl.BlockSpec((1, rows // n, cols), lambda i: (i, 0, 0))] * len(addends),
        out_specs=[full] * n,
    )


def join_body(index_ref, *refs):
    slot = pl.program_id(0) ^ index_ref[0]
    for which, ref in enumerate(refs[:-1]):

        @pl.when(slot == which)
        def _():
            refs[-1][0] = ref[...]


def join(pieces, index):
    n = len(pieces)
    rows, cols = pieces[0].shape
    full = pl.BlockSpec((rows, cols), lambda i: (0, 0))
    made = call(
        join_body,
        "join",
        [struct((n, rows, cols), BF16)],
        (index.reshape(1), *pieces),
        rows * cols * n,
        grid=(n,),
        in_specs=[SM] + [full] * n,
        out_specs=[pl.BlockSpec((1, rows, cols), lambda i: (i, 0, 0))],
    )[0]
    return made.reshape(n * rows, cols)


def stages_of(size, widths):
    bits = size.bit_length() - 1
    out = []
    shift = 0
    for width in widths:
        width = min(width, bits - shift)
        if width > 0:
            out.append((shift, 1 << width))
            shift += width
    while shift < bits:
        width = min(widths[-1], bits - shift)
        out.append((shift, 1 << width))
        shift += width
    return out


def scatter_sum(addends, stages, here, size, keep_last=False):
    for shift, n in stages:
        index = (here >> shift) & (n - 1)
        pieces = sum_split(addends, n, index)
        addends = [pieces[0]] + [swap(pieces[j], "dp", size, j << shift) for j in range(1, n)]
    return sum_split(addends, 1, jnp.zeros_like(here))[0]


def gather_stage(piece, stage, here, size):
    shift, n = stage
    return [piece] + [swap(piece, "dp", size, j << shift) for j in range(1, n)]


def gather_all(piece, stages, here, size):
    for shift, n in reversed(stages):
        index = (here >> shift) & (n - 1)
        piece = join(gather_stage(piece, (shift, n), here, size), index)
    return piece


def add_home_body(meta_ref, in_ref, p0, p1, p2, p3, out_ref):
    slot = pl.program_id(0) ^ meta_ref[2]
    for which, piece in enumerate((p0, p1, p2, p3)):

        @pl.when(slot == which)
        def _():
            out_ref[0] = in_ref[0] + piece[...].astype(F32)


def add_home(meta, base, pieces):
    count, rows, width = base.shape
    block = pl.BlockSpec((1, rows, width), lambda i: (i, 0, 0))
    full = pl.BlockSpec((rows, width), lambda i: (0, 0))
    return call(
        add_home_body,
        "add_home",
        [struct(base.shape, F32)],
        (meta, base, *pieces),
        base.size,
        grid=(count,),
        in_specs=[SM, block] + [full] * 4,
        out_specs=[block],
    )[0]


def mlp_out_body(pair_ref, last_ref, gu_ref, wd_ref):
    step = pl.program_id(0)

    @pl.when(step < 4)
    def _():
        gu_ref[...] = pair_ref[...].astype(F32)

    @pl.when(step >= 4)
    def _():
        wd_ref[...] = last_ref[...].astype(F32).T


def mlp_out(whole, width, units):
    rows = width // 2
    return call(
        mlp_out_body,
        "mlp_out",
        [struct((2 * width, units), F32), struct((units, width), F32)],
        (whole, whole),
        whole.size,
        grid=(6,),
        in_specs=[
            pl.BlockSpec((rows, units), lambda i: (jnp.minimum(i, 3), 0)),
            pl.BlockSpec((rows, units), lambda i: (jnp.maximum(i, 4), 0)),
        ],
        out_specs=[
            pl.BlockSpec((rows, units), lambda i: (jnp.minimum(i, 3), 0)),
            pl.BlockSpec((units, rows), lambda i: (0, jnp.maximum(i - 4, 0))),
        ],
    )


def attn_out_body(early_ref, late_ref, qkv_ref, wo_ref):
    wo_ref[...] = early_ref[: 3 * HD, :].astype(F32)
    for part in range(3):
        at = part * HD
        parts = [early_ref[3 * HD + at : 3 * HD + at + HD, :], early_ref[6 * HD + at : 6 * HD + at + HD, :]]
        parts.append(late_ref[at : at + HD, :])
        qkv_ref[part] = jnp.concatenate(parts, axis=0).astype(F32).T


def attn_out(early, late):
    width = early.shape[1]
    return call(
        attn_out_body,
        "attn_out",
        [struct((3, width, 3 * HD), F32), struct((3 * HD, width), F32)],
        (early, late),
        early.size,
    )


def sum_all_body(count, index_ref, *refs):
    hold = refs[-1]
    for which in range(count):
        hold[index_ref[0] ^ which] = refs[which][...]
    total = hold[0]
    for which in range(1, count):
        total = total + hold[which]
    refs[count][...] = total


def sum_all(value, axis, size, stages, here):
    for shift, n in stages:
        index = (here >> shift) & (n - 1)
        pieces = [value] + [swap(value, axis, size, j << shift) for j in range(1, n)]
        value = call(
            functools.partial(sum_all_body, n),
            "sum_all",
            [struct(value.shape, F32)],
            (index.reshape(1), *pieces),
            value.size * n,
            in_specs=[SM] + [VM] * n,
            out_specs=[VM],
            scratch_shapes=[pltpu.VMEM((n,) + value.shape, F32)],
        )[0]
    return value


def send_home(pieces, size):
    return [pieces[0]] + [swap(pieces[k], "tensor", size, k) for k in range(1, 4)]


def local(n_dp, inputs, w_qkv, w_out, w_gate_up, w_down, gain_attn, gain_mlp, piece_starts, out_grad):
    width = inputs.shape[2]
    units = w_down.shape[0]
    here = lax.axis_index("tensor").astype(jnp.int32)
    row = lax.axis_index("dp").astype(jnp.int32)
    bit = row & 1
    mine = lax.dynamic_index_in_dim(piece_starts, here, 0, keepdims=False)[0]
    meta = jnp.concatenate([mine, jnp.stack([here, bit])])
    one = gain_attn[None]
    two = gain_mlp[None]
    cosine, sine = rope_tables(LEN, HD)
    tensor = functools.partial(swap, axis="tensor", size=4)

    def quarters(whole):
        picks = [
            lax.dynamic_index_in_dim(whole, here ^ k, 0, keepdims=False).astype(BF16) for k in range(4)
        ]
        return [picks[0]] + [tensor(picks[k], mask=k) for k in range(1, 4)]

    xs = quarters(inputs)
    wq0 = jnp.swapaxes(w_qkv, 1, 2).astype(BF16)
    wq1 = tensor(wq0, mask=1)
    wq2 = tensor(wq0, mask=2)
    wq3 = tensor(wq2, mask=1)
    wo0 = w_out.astype(BF16)
    wo1 = tensor(wo0, mask=1)
    wo2 = tensor(wo0, mask=2)
    wo3 = tensor(wo2, mask=1)
    gs = quarters(out_grad)
    wq = (wq0, wq1, wq2, wq3)
    wo = (wo0, wo1, wo2, wo3)
    gu0 = w_gate_up.astype(BF16)
    wd0 = w_down.astype(BF16).reshape(2, units // 2, width)
    gu1 = tensor(gu0, mask=1)
    wd1 = tensor(wd0, mask=1)

    def far(shard):
        half = lax.dynamic_slice_in_dim(shard, bit, 1, 0)
        direct = tensor(half, mask=2)
        round_about = swap(direct, "dp", n_dp, 1)
        return direct, round_about, tensor(direct, mask=1), tensor(round_about, mask=1)

    gu_far = far(gu0)
    wd_far = far(wd0)

    x, n1, qa, ka, va = project_first(meta, xs, one, wq0, wq1, cosine, sine)
    mta, ma, la = attend(meta, qa, ka, va)
    qb, kb, vb = project_next(n1, wq2, wq3, cosine, sine)
    mtb, mb, lb = attend(meta, qb, kb, vb)
    after, n2, n2t, g, gt = after_attention(meta, x, ma, mb, wo, two, gs)
    oa, ba, dw0, dw1 = mlp(meta, n2, n2t, g, gt, (gu0, gu1, wd0, wd1))
    in1 = tensor(dw1, mask=1)
    ob, bb, dw2, dw3 = mlp(meta, n2, n2t, g, gt, gu_far + wd_far)
    in3 = tensor(dw3, mask=1)
    middle_out = middle(meta, x, after, (oa, ob), (ba, bb), g, two, (mta, mtb), wo)
    back_home = send_home(middle_out[:4], 4)
    da, do, dwo, gain_two = middle_out[4:]
    flat = lambda a: a.reshape(-1, a.shape[-1])
    zero = jnp.zeros((), jnp.int32)
    wide = stages_of(n_dp, (1, 2))
    tall = stages_of(n_dp, (3, 3))
    low = sum_split([flat(dw2), flat(in3)], 1, zero)[0]
    piece = scatter_sum([flat(dw0), flat(in1), tensor(low, mask=2)], wide, row, n_dp)
    grad_pair, grad_down = mlp_out(gather_all(piece, wide, row, n_dp), width, units)
    sets = ((qa, ka, va, mta, la), (qb, kb, vb, mtb, lb))
    dts = []
    dws = []
    for turn in range(3):
        dt, dw = attend_back(turn, meta, cosine, sine, n1, sets, do)
        dts.append(dt)
        dws.append(dw)

    def core_sum(parts, stages):
        slots = [jnp.concatenate([flat(p[s]) for p in parts]) if len(parts) > 1 else flat(parts[0][s]) for s in range(4)]
        in1 = tensor(slots[1], mask=1)
        in3 = tensor(slots[3], mask=1)
        low = sum_split([slots[2], in3], 1, zero)[0]
        piece = scatter_sum([slots[0], in1, tensor(low, mask=2)], stages, row, n_dp)
        return gather_all(piece, stages, row, n_dp)

    early = core_sum((dwo, dws[0], dws[1]), wide)
    (before,) = token_grad((0, 1), dts[:2], wq)
    late = core_sum((dws[2],), tall)
    *grads, gain_one = token_grad((2,), dts[2:], wq, (meta, before, x, da, g, one))
    grad_home = send_home(grads, 4)
    gains = jnp.concatenate([gain_one, gain_two])
    gains = sum_all(gains, "tensor", 4, [(0, 4)], here)
    gains = sum_all(gains, "dp", n_dp, tall, row)
    grad_qkv, grad_out = attn_out(early, late)
    return (
        add_home(meta, inputs, back_home),
        add_home(meta, out_grad, grad_home),
        grad_qkv,
        grad_out,
        grad_pair.reshape(2, width, units),
        grad_down,
        gains[0],
        gains[1],
    )


def solution(mesh):
    rows = P(None, ("dp", "tensor"), None)
    weights = (P(None, None, "tensor"), P("tensor", None), P(None, None, "tensor"), P("tensor", None))
    return jax.shard_map(
        functools.partial(local, mesh.shape["dp"]),
        mesh=mesh,
        in_specs=(rows, *weights, P(), P(), P(None, "dp", None), rows),
        out_specs=(rows, rows, *weights, P(), P()),
        check_vma=False,
    )
```

```python
import functools
import jax
import jax.numpy as jnp
import numpy as np
from jax import lax
from jax.experimental import pallas as pl
from jax.experimental.pallas import tpu as pltpu
from jax.sharding import PartitionSpec as P

HD = 64
LEN = 1024
PIECE = 256
HALF = 512
EPS = 1e-06
F32 = jnp.float32
BF16 = jnp.bfloat16
MIB = 1024 * 1024


def nn(a, b):
    return lax.dot_general(a, b, (((1,), (0,)), ((), ())), preferred_element_type=F32)


def nt(a, b):
    return lax.dot_general(a, b, (((1,), (1,)), ((), ())), preferred_element_type=F32)


def call(body, name, out_shape, args, vmem, cost=1e6, **kw):
    return pl.pallas_call(
        body,
        name=name,
        out_shape=out_shape,
        compiler_params=pltpu.CompilerParams(vmem_limit_bytes=vmem * MIB),
        cost_estimate=pl.CostEstimate(flops=int(cost), bytes_accessed=int(cost) // 100, transcendentals=0),
        **kw,
    )(*args)


def struct(shape, dtype):
    return jax.ShapeDtypeStruct(shape, dtype)


def project(n1_ref, weights, cos_ref, sin_ref, q_ref, k_ref, v_ref):
    step = 256
    for block in range(LEN // step):
        cols = slice(block * step, (block + 1) * step)
        rows = n1_ref[cols, :]
        cosine = cos_ref[:, cols]
        sine = sin_ref[:, cols]
        for slot, w_ref in enumerate(weights):
            for part, ref in ((0, q_ref), (1, k_ref), (2, v_ref)):
                made = nt(w_ref[part], rows)
                for head in range(3):
                    low = made[head * HD : head * HD + HD // 2]
                    high = made[head * HD + HD // 2 : (head + 1) * HD]
                    if part < 2:
                        low, high = low * cosine - high * sine, high * cosine + low * sine
                    if part == 0:
                        low, high = low * HD**-0.5, high * HD**-0.5
                    at = slot * HD
                    ref[head, at : at + HD // 2, cols] = low.astype(BF16)
                    ref[head, at + HD // 2 : at + HD, cols] = high.astype(BF16)


def in_order(here, pieces, ref):
    step = ref.shape[0] // 4
    for quarter in range(4):
        for slot, piece in enumerate(pieces):

            @pl.when((here ^ slot) == quarter)
            def _():
                ref[quarter * step : (quarter + 1) * step, :] = piece[...]


def project_first_body(meta_ref, p0, p1, p2, p3, gain_ref, w0, w1, cos_ref, sin_ref, x_ref, n1_ref, q_ref, k_ref, v_ref):
    step = 256
    gain = gain_ref[...]
    in_order(meta_ref[2], (p0, p1, p2, p3), x_ref)
    for block in range(LEN // step):
        rows = slice(block * step, (block + 1) * step)
        x = x_ref[rows, :].astype(F32)
        scale = lax.rsqrt(jnp.mean(x * x, axis=-1, keepdims=True) + EPS)
        n1_ref[rows, :] = (x * scale * gain).astype(BF16)
    project(n1_ref, (w0, w1), cos_ref, sin_ref, q_ref, k_ref, v_ref)


def project_next_body(
    meta_ref, n1_ref, d2, r2, d3, r3, cos_ref, sin_ref, q_ref, k_ref, v_ref, w2_ref, w3_ref
):
    bit = meta_ref[3]
    for direct, other, ref in ((d2, r2, w2_ref), (d3, r3, w3_ref)):
        for part in range(2):
            ref[2 * bit + part] = direct[part]
            ref[2 * (1 - bit) + part] = other[part]
    project(n1_ref, (w2_ref, w3_ref), cos_ref, sin_ref, q_ref, k_ref, v_ref)


HEADS3 = (3, 2 * HD, LEN)


VM = pl.BlockSpec(memory_space=pltpu.VMEM)
SM = pl.BlockSpec(memory_space=pltpu.SMEM)


def project_first(meta, pieces, gain, w0, w1, cosine, sine):
    width = gain.shape[1]
    out = [struct((LEN, width), BF16)] * 2 + [struct(HEADS3, BF16)] * 3
    args = (meta, *pieces, gain, w0, w1, cosine, sine)
    return call(
        project_first_body,
        "project_first",
        out,
        args,
        24,
        in_specs=[SM] + [VM] * (len(args) - 1),
        out_specs=[VM] * len(out),
    )


def project_next(meta, n1, far, cosine, sine):
    out = [struct(HEADS3, BF16)] * 3 + [struct((4,) + far[0].shape[1:], BF16)] * 2
    args = (meta, n1, *far, cosine, sine)
    return call(
        project_next_body,
        "project_next",
        out,
        args,
        24,
        in_specs=[SM] + [VM] * (len(args) - 1),
        out_specs=[VM] * len(out),
    )


def limits(starts_ref):
    pos = lax.broadcasted_iota(jnp.int32, (1, LEN), 1)
    lim = pos
    for piece in range(2):
        first = starts_ref[piece]
        lim = jnp.where((pos >= first) & (pos < first + PIECE), first + PIECE - 1, lim)
    return lim


def one_head(block, head):
    zero = jnp.zeros((HD, block.shape[1]), block.dtype)
    part = block[head * HD : (head + 1) * HD]
    return jnp.concatenate([part, zero] if head == 0 else [zero, part], axis=0)


NEG = -1e30


def attend_body(qb, starts_ref, q_ref, k_ref, v_ref, mt_ref, m_ref, lse_ref):
    lim = limits(starts_ref)
    k_rows = k_ref[0].T
    for head in range(2):
        q_one = one_head(q_ref[0], head)
        v_one = v_ref[0, head * HD : (head + 1) * HD, :]
        for block in range(LEN // qb):
            cols = slice(block * qb, (block + 1) * qb)
            keys = HALF if (block + 1) * qb <= HALF else LEN
            scores = nn(k_rows[:keys], q_one[:, cols])
            edge = scores[keys - HALF :]
            pos = lax.broadcasted_iota(jnp.int32, (HALF, qb), 0) + (keys - HALF)
            edge = jnp.where(pos <= lim[:, cols], edge, NEG)
            most = jnp.max(edge, axis=0, keepdims=True)
            if keys > HALF:
                body = scores[:HALF]
                most = jnp.maximum(most, jnp.max(body, axis=0, keepdims=True))
            soft = jnp.exp(edge - most)
            total = jnp.sum(soft, axis=0, keepdims=True)
            mixed = nn(v_one[:, keys - HALF : keys], soft.astype(BF16))
            if keys > HALF:
                soft = jnp.exp(body - most)
                total = total + jnp.sum(soft, axis=0, keepdims=True)
                mixed = mixed + nn(v_one[:, :HALF], soft.astype(BF16))
            mt_ref[0, head * HD : (head + 1) * HD, cols] = (mixed * (1.0 / total)).astype(BF16)
            lse_ref[0, head : head + 1, cols] = most + jnp.log(total)
    m_ref[...] = mt_ref[0].T


def attend(starts, q, k, v, qb=512):
    block = pl.BlockSpec((1, 2 * HD, LEN), lambda i: (i, 0, 0))
    out = [struct(HEADS3, BF16), struct((LEN, 6 * HD), BF16), struct((3, 2, LEN), F32)]
    return call(
        functools.partial(attend_body, qb),
        "attend",
        out,
        (starts, q, k, v),
        24,
        grid=(3,),
        in_specs=[pl.BlockSpec(memory_space=pltpu.SMEM), block, block, block],
        out_specs=[
            block,
            pl.BlockSpec((LEN, 2 * HD), lambda i: (0, i)),
            pl.BlockSpec((1, 2, LEN), lambda i: (i, 0, 0)),
        ],
    )


def attend_back_body(qb, starts_ref, cos_ref, sin_ref, n1_ref, *refs):
    sets = (refs[0:5], refs[5:10])
    do_ref = refs[10]
    dt_ref, even_ref, odd_ref, acc_ref = refs[11:]
    lim = limits(starts_ref)
    for which, (q_ref, k_ref, v_ref, mt_ref, lse_ref) in enumerate(sets):
        q = q_ref[0]
        k = k_ref[0]
        v = v_ref[0]
        do = do_ref[which * 2 * HD : (which + 1) * 2 * HD, :]
        k_rows = k.T
        v_rows = v.T
        both = do.astype(F32) * mt_ref[0].astype(F32)
        for head in range(2):
            mine = slice(head * HD, (head + 1) * HD)
            inner = jnp.sum(both[mine], axis=0, keepdims=True)
            q_one = one_head(q, head)
            do_one = one_head(do, head)
            lse = lse_ref[0, head : head + 1, :]
            for block in range(LEN // qb):
                cols = slice(block * qb, (block + 1) * qb)
                wide = (block + 1) * qb > HALF
                dq = None
                for part in range(2 if wide else 1):
                    keys = slice(part * HALF, (part + 1) * HALF)
                    scores = nn(k_rows[keys], q_one[:, cols])
                    if part == (1 if wide else 0):
                        pos = lax.broadcasted_iota(jnp.int32, (HALF, qb), 0) + part * HALF
                        scores = jnp.where(pos <= lim[:, cols], scores, NEG)
                    soft = jnp.exp(scores - lse[:, cols])
                    grad = nn(v_rows[keys], do_one[:, cols])
                    grad = (soft * (grad - inner[:, cols])).astype(BF16)
                    more = nn(k[mine, keys], grad)
                    dq = more if dq is None else dq + more
                    dk = nt(q[mine, cols], grad)
                    dv = nt(do[mine, cols], soft.astype(BF16))
                    fresh = block == (0 if part == 0 else HALF // qb)
                    if fresh:
                        acc_ref[1, mine, keys] = dk
                        acc_ref[2, mine, keys] = dv
                    else:
                        acc_ref[1, mine, keys] += dk
                        acc_ref[2, mine, keys] += dv
                acc_ref[0, mine, cols] = dq * HD**-0.5
        cosine = cos_ref[...]
        sine = sin_ref[...]
        for part in range(3):
            for head in range(2):
                at = head * HD
                low = acc_ref[part, at : at + HD // 2, :]
                high = acc_ref[part, at + HD // 2 : at + HD, :]
                if part < 2:
                    low, high = low * cosine + high * sine, high * cosine - low * sine
                to = which * 2 * HD + at
                dt_ref[part, to : to + HD // 2, :] = low.astype(BF16)
                dt_ref[part, to + HD // 2 : to + HD, :] = high.astype(BF16)
    for part in range(3):
        made = nn(dt_ref[part], n1_ref[...])
        for slot in range(4):
            ref = odd_ref if slot % 2 else even_ref
            ref[slot // 2, part * HD : (part + 1) * HD, :] = made[slot * HD : (slot + 1) * HD].astype(BF16)


def attend_back(turn, starts, cosine, sine, n1, sets, do, qb=512):
    width = n1.shape[1]
    head = pl.BlockSpec((1, 2 * HD, LEN), lambda i: (turn, 0, 0))
    full = lambda a: pl.BlockSpec(a.shape, lambda i, n=a.ndim: (0,) * n)
    lse = pl.BlockSpec((1, 2, LEN), lambda i: (turn, 0, 0))
    args = (starts, cosine, sine, n1, *sets[0], *sets[1], do)
    out = [struct((3, 4 * HD, LEN), BF16)] + [struct((2, 3 * HD, width), BF16)] * 2
    return call(
        functools.partial(attend_back_body, qb),
        "attend_back",
        out,
        args,
        40,
        grid=(1,),
        in_specs=[pl.BlockSpec(memory_space=pltpu.SMEM), full(cosine), full(sine), full(n1)]
        + [head, head, head, head, lse] * 2
        + [pl.BlockSpec((4 * HD, LEN), lambda i: (turn, 0))],
        out_specs=[full(o) for o in out],
        scratch_shapes=[pltpu.VMEM((3, 2 * HD, LEN), F32)],
    )


def turn_rows(w_refs):
    return jnp.concatenate(
        [w[3, turn * HD : (turn + 1) * HD, :] for turn in range(3) for w in w_refs], axis=0
    )


def after_body(
    meta_ref, x_ref, ma_ref, mb_ref, w0, w1, w2, w3, gain_ref, g0, g1, g2, g3,
    after_ref, n2_ref, n2t_ref, g_ref, gt_ref,
):
    slot = pl.program_id(0) ^ meta_ref[2]
    for which, piece in enumerate((g0, g1, g2, g3)):

        @pl.when(slot == which)
        def _():
            g_ref[...] = piece[...]

    first = turn_rows((w0, w1))
    second = turn_rows((w2, w3))
    after = x_ref[...].astype(F32) + nn(ma_ref[...], first) + nn(mb_ref[...], second)
    after_ref[...] = after
    scale = lax.rsqrt(jnp.mean(after * after, axis=-1, keepdims=True) + EPS)
    normed = (after * scale * gain_ref[...]).astype(BF16)
    n2_ref[...] = normed
    n2t_ref[...] = normed.T
    gt_ref[...] = g_ref[...].T


def after_attention(meta, x, mixed_a, mixed_b, wo, gain, g):
    width = x.shape[1]
    step = 256
    rows = lambda n: pl.BlockSpec((step, n), lambda i: (i, 0))
    cols = pl.BlockSpec((width, step), lambda i: (0, i))
    full = lambda a: pl.BlockSpec(a.shape, lambda i, n=a.ndim: (0,) * n)
    args = (meta, x, mixed_a, mixed_b, *wo, gain, *g)
    out = [
        struct((LEN, width), F32),
        struct((LEN, width), BF16),
        struct((width, LEN), BF16),
        struct((LEN, width), BF16),
        struct((width, LEN), BF16),
    ]
    return call(
        after_body,
        "after_attention",
        out,
        args,
        30,
        grid=(LEN // step,),
        in_specs=[SM, rows(width), rows(6 * HD), rows(6 * HD)]
        + [full(w) for w in wo]
        + [full(gain)]
        + [full(p) for p in g],
        out_specs=[rows(width), rows(width), cols, rows(width), cols],
    )


def mlp_body(layout, first, meta_ref, n2_ref, n2t_ref, g_ref, gt_ref, *refs):
    block = 256
    refs = list(refs)
    sources = [[refs.pop(0) for _ in range(kind)] for kind in layout]
    if not first:
        out_in, back_in = refs.pop(0), refs.pop(0)
    out_ref, back_ref = refs.pop(0), refs.pop(0)
    made = [refs.pop(0) for _ in layout]
    hid, dga, dup = refs[:3]
    if first:
        out_ref[...] = jnp.zeros_like(out_ref)
        back_ref[...] = jnp.zeros_like(back_ref)
    else:
        out_ref[...] = out_in[...]
        back_ref[...] = back_in[...]
    width = n2_ref.shape[1]
    half = 3 * width // 2
    for source, dw_ref in zip(sources, made):
        if len(source) == 2:
            hold = refs[3]
            hold[meta_ref[3]] = source[0][...]
            hold[1 - meta_ref[3]] = source[1][...]

            def take(part, cols, hold=hold):
                if part == 0:
                    return hold[0, :width, cols]
                if part == 2:
                    return hold[1, half - width :, cols]
                return jnp.concatenate([hold[0, width:, cols], hold[1, : half - width, cols]], axis=0)
        else:

            def take(part, cols, hold=source[0]):
                return hold[part, :, cols]

        for part in range(2):
            cols = slice(part * block, (part + 1) * block)
            wg = take(0, cols)
            wu = take(1, cols)
            wl = take(2, cols)
            n2 = n2_ref[...]
            gate = nn(n2, wg)
            up = nn(n2, wu)
            grad = nn(g_ref[...], wl)
            sigma = 1.0 / (1.0 + jnp.exp(-gate))
            silu = gate * sigma
            hid[...] = (silu * up).astype(BF16)
            dup[...] = (grad * silu).astype(BF16)
            dga[...] = (grad * up * (sigma * (1.0 + gate * (1.0 - sigma)))).astype(BF16)
            out_ref[...] += nt(hid[...], wl)
            back_ref[...] += nt(dga[...], wg) + nt(dup[...], wu)
            dw_ref[0, :, cols] = nn(n2t_ref[...], dga[...]).astype(BF16)
            dw_ref[1, :, cols] = nn(n2t_ref[...], dup[...]).astype(BF16)
            dw_ref[2, :, cols] = nn(gt_ref[...], hid[...]).astype(BF16)


def mlp(meta, n2, n2t, g, gt, weights, before=()):
    width = n2.shape[1]
    units = 512
    layout = tuple(len(w) for w in weights)
    out = [struct((LEN, width), F32)] * 2 + [struct((3, width, units), BF16)] * len(weights)
    args = (meta, n2, n2t, g, gt, *[a for w in weights for a in w], *before)
    scratch = [pltpu.VMEM((LEN, 256), BF16)] * 3
    if 2 in layout:
        scratch.append(pltpu.VMEM((2, 3 * width // 2, units), BF16))
    aliases = {len(args) - 2: 0, len(args) - 1: 1} if before else {}
    return call(
        functools.partial(mlp_body, layout, not before),
        "mlp",
        out,
        args,
        50,
        in_specs=[SM] + [VM] * (len(args) - 1),
        out_specs=[VM] * len(out),
        scratch_shapes=scratch,
        input_output_aliases=aliases,
    )


def norm_back(grad, value, gain):
    scale = lax.rsqrt(jnp.mean(value * value, axis=-1, keepdims=True) + EPS)
    unit = value * scale
    gain_grad = jnp.sum(grad * unit, axis=0, keepdims=True)
    e = grad * gain
    return scale * (e - unit * jnp.mean(e * unit, axis=-1, keepdims=True)), gain_grad


def give(meta_ref, value, refs):
    slot = pl.program_id(0) ^ meta_ref[2]
    for which, ref in enumerate(refs):

        @pl.when(slot == which)
        def _():
            ref[...] = value


def middle_body(
    meta_ref, x_ref, after_ref, sum_ref, back_ref, g_ref, gain_ref, mta_ref, mtb_ref,
    w0, w1, w2, w3, e0, e1, e2, e3, da_ref, do_ref, even_ref, odd_ref, gain_out, acc,
):
    step = pl.program_id(0)
    after = after_ref[...]
    delta = (after - x_ref[...].astype(F32) + sum_ref[...]).astype(BF16)
    give(meta_ref, delta, (e0, e1, e2, e3))
    back, gain_grad = norm_back(back_ref[...], after, gain_ref[...])
    grad_after = g_ref[...].astype(F32) + back
    da_ref[...] = grad_after
    low = grad_after.astype(BF16)

    @pl.when(step == 0)
    def _():
        gain_out[...] = jnp.zeros_like(gain_out)
        acc[...] = jnp.zeros_like(acc)

    gain_out[...] += gain_grad
    weights = turn_rows((w0, w1, w2, w3))
    do_ref[...] = nt(weights, low).astype(BF16)
    for turn in range(3):
        for which, mt in enumerate((mta_ref, mtb_ref)):
            acc[turn, which] += nn(mt[turn], low)

    @pl.when(step == pl.num_programs(0) - 1)
    def _():
        for turn in range(3):
            for slot in range(4):
                at = (slot % 2) * HD
                ref = odd_ref if slot % 2 else even_ref
                ref[slot // 2, turn * HD : (turn + 1) * HD, :] = acc[turn, slot // 2, at : at + HD, :].astype(BF16)


def middle(meta, x, after, total, back, g, gain, mts, wo):
    width = x.shape[1]
    step = 256
    rows = pl.BlockSpec((step, width), lambda i: (i, 0))
    full = lambda a: pl.BlockSpec(a.shape, lambda i, n=a.ndim: (0,) * n)
    heads = pl.BlockSpec((3, 2 * HD, step), lambda i: (0, 0, i))
    args = (meta, x, after, total, back, g, gain, *mts, *wo)
    out = [struct((step, width), BF16)] * 4 + [
        struct((LEN, width), F32),
        struct((12 * HD, LEN), BF16),
        struct((2, 3 * HD, width), BF16),
        struct((2, 3 * HD, width), BF16),
        struct((1, width), F32),
    ]
    return call(
        middle_body,
        "middle",
        out,
        args,
        40,
        grid=(LEN // step,),
        in_specs=[SM] + [rows] * 5 + [full(gain), heads, heads] + [full(w) for w in wo],
        out_specs=[full(o) for o in out[:4]]
        + [rows, pl.BlockSpec((12 * HD, step), lambda i: (0, i)), full(out[6]), full(out[7]), full(out[8])],
        scratch_shapes=[pltpu.VMEM((3, 2, 2 * HD, width), F32)],
    )


def token_grad_body(turns, last, meta_ref, *refs):
    dts = refs[: len(turns)]
    weights = refs[len(turns) : len(turns) + 4]
    rest = refs[len(turns) + 4 :]
    step = pl.program_id(0)
    total = None
    for turn, dt in zip(turns, dts):
        for part in range(3):
            w = jnp.concatenate([w[part, turn * HD : (turn + 1) * HD, :] for w in weights], axis=0)
            more = nn(dt[part].T, w)
            total = more if total is None else total + more
    if not last:
        rest[0][...] = total
        return
    before_ref, x_ref, da_ref, g_ref, gain_ref, e0, e1, e2, e3, gain_out = rest
    total = total + before_ref[...]
    back, gain_grad = norm_back(total, x_ref[...].astype(F32), gain_ref[...])
    give(meta_ref, (da_ref[...] - g_ref[...].astype(F32) + back).astype(BF16), (e0, e1, e2, e3))

    @pl.when(step == 0)
    def _():
        gain_out[...] = jnp.zeros_like(gain_out)

    gain_out[...] += gain_grad


def token_grad(meta, turns, dts, weights, rest=None):
    width = weights[0].shape[2]
    step = 256
    rows = pl.BlockSpec((step, width), lambda i: (i, 0))
    full = lambda a: pl.BlockSpec(a.shape, lambda i, n=a.ndim: (0,) * n)
    cols = pl.BlockSpec((3, 4 * HD, step), lambda i: (0, 0, i))
    specs = [SM] + [cols] * len(dts) + [full(w) for w in weights]
    args = (meta, *dts, *weights)
    if rest is None:
        out = [struct((LEN, width), F32)]
        out_specs = [rows]
    else:
        out = [struct((step, width), BF16)] * 4 + [struct((1, width), F32)]
        out_specs = [full(o) for o in out]
        specs = specs + [rows] * 4 + [full(rest[4])]
        args = args + tuple(rest)
    return call(
        functools.partial(token_grad_body, turns, rest is not None),
        "token_grad",
        out,
        args,
        30,
        grid=(LEN // step,),
        in_specs=specs,
        out_specs=out_specs,
    )


def rope_tables(length, width):
    halfway = width // 2
    inverse = 10000.0 ** (-jnp.arange(halfway, dtype=F32) * 2.0 / width)
    angles = inverse[:, None] * jnp.arange(length, dtype=F32)[None, :]
    return jnp.cos(angles), jnp.sin(angles)


def swap(value, axis, size, mask):
    return lax.ppermute(value, axis, [(i, i ^ mask) for i in range(size)])


def added(*refs):
    total = refs[0].astype(F32)
    for ref in refs[1:]:
        total = total + ref.astype(F32)
    return total.astype(BF16)


def put(cond, ref, at, value):
    @pl.when(cond)
    def _():
        if at is None:
            ref[...] = value
        else:
            ref[at] = value


def start_body(meta_ref, a0, b0, a2, b2, keep_p, send_p, keep_q, send_q):
    step = pl.program_id(0)
    bit = meta_ref[3]
    two = meta_ref[4]
    for slot, (a, b) in enumerate(((a0, b0), (a2, b2))):
        value = added(a[0], b[0])
        put(step == bit, keep_p, slot, value)
        put(step == 1 - bit, send_p, slot, value)
        put(step == 2 + two, keep_q, slot, value)
        put(step == 3 - two, send_q, slot, value)


def start_sums(meta, dw0, in1, dw2, in3):
    rows = dw0.shape[0] * dw0.shape[1] // 4
    cols = dw0.shape[2]
    parts = [a.reshape(4, rows, cols) for a in (dw0, in1, dw2, in3)]
    out = [struct((2, rows, cols), BF16)] * 4
    return call(
        start_body,
        "start_sums",
        out,
        (meta, *parts),
        16,
        grid=(4,),
        in_specs=[SM] + [pl.BlockSpec((1, rows, cols), lambda i: (i, 0, 0))] * 4,
        out_specs=[pl.BlockSpec((2, rows, cols), lambda i: (0, 0, 0))] * 4,
    )


def second_body(meta_ref, kp, rp, kq, rq, keep, send):
    for which, (k, r) in enumerate(((kp, rp), (kq, rq))):
        keep[which] = added(k[0], r[0])
        send[which] = added(k[1], r[1])


def second_sums(meta, kp, rp, kq, rq):
    _, rows, cols = kp.shape
    block = pl.BlockSpec((2, rows // 2, cols), lambda i: (0, i, 0))
    return call(
        second_body,
        "second_sums",
        [struct((2, rows, cols), BF16)] * 2,
        (meta, kp, rp, kq, rq),
        16,
        grid=(2,),
        in_specs=[SM] + [block] * 4,
        out_specs=[block] * 2,
    )


def third_body(meta_ref, a, b, keep, send_p, send_q):
    step = pl.program_id(0)
    two = meta_ref[4]
    bit = meta_ref[3]
    value = added(a[0, 0], b[0, 0])
    put(step == two, keep, 0, value)
    put(step == 1 - two, send_p, None, value)
    value = added(a[1, 0], b[1, 0])
    put(step == bit, keep, 1, value)
    put(step == 1 - bit, send_q, None, value)


def third_sums(meta, a, b):
    _, rows, cols = a.shape
    half = rows // 2
    views = [v.reshape(2, 2, half, cols) for v in (a, b)]
    return call(
        third_body,
        "third_sums",
        [struct((2, half, cols), BF16)] + [struct((half, cols), BF16)] * 2,
        (meta, *views),
        12,
        grid=(2,),
        in_specs=[SM] + [pl.BlockSpec((2, 1, half, cols), lambda i: (0, i, 0, 0))] * 2,
        out_specs=[pl.BlockSpec((2, half, cols), lambda i: (0, 0, 0))]
        + [pl.BlockSpec((half, cols), lambda i: (0, 0))] * 2,
    )


def halve_body(bit_ref, a, b0, b1, keep, send):
    bit = bit_ref[0]
    step = pl.program_id(0)
    for which, b in enumerate((b0, b1)):
        value = added(a[which, 0], b[0])
        put(step == bit, keep, which, value)
        put(step != bit, send, which, value)


def halve_sums(bit, a, b0, b1):
    _, rows, cols = a.shape
    half = rows // 2
    return call(
        halve_body,
        "halve_sums",
        [struct((2, half, cols), BF16)] * 2,
        (bit.reshape(1), a.reshape(2, 2, half, cols), b0.reshape(2, half, cols), b1.reshape(2, half, cols)),
        12,
        grid=(2,),
        in_specs=[SM, pl.BlockSpec((2, 1, half, cols), lambda i: (0, i, 0, 0))]
        + [pl.BlockSpec((1, half, cols), lambda i: (i, 0, 0))] * 2,
        out_specs=[pl.BlockSpec((2, half, cols), lambda i: (0, 0, 0))] * 2,
    )


def plain_body(tie_ref, a, b, out):
    out[...] = added(a[...], b[...])


def plain_sum(tie, a, b):
    return call(plain_body, "plain_sum", [struct(a.shape, BF16)], (tie, a, b), 12, in_specs=[SM, VM, VM], out_specs=[VM])[0]


def pair_body(bit_ref, a, b, out):
    bit = bit_ref[0]
    for which in range(2):
        out[which, bit] = a[which]
        out[which, 1 - bit] = b[which]


def pair_join(bit, a, b):
    _, rows, cols = a.shape
    made = call(
        pair_body,
        "pair_join",
        [struct((2, 2, rows, cols), BF16)],
        (bit.reshape(1), a, b),
        12,
        in_specs=[SM, VM, VM],
        out_specs=[VM],
    )[0]
    return made.reshape(2, 2 * rows, cols)


def cross_body(meta_ref, a, bp, bq, out_p, out_q):
    two = meta_ref[4]
    bit = meta_ref[3]
    out_p[two] = a[0]
    out_p[1 - two] = bp[...]
    out_q[bit] = a[1]
    out_q[1 - bit] = bq[...]


def cross_join(meta, a, bp, bq):
    _, rows, cols = a.shape
    made = call(
        cross_body,
        "cross_join",
        [struct((2, rows, cols), BF16)] * 2,
        (meta, a, bp, bq),
        12,
        in_specs=[SM, VM, VM, VM],
        out_specs=[VM, VM],
    )
    return [m.reshape(2 * rows, cols) for m in made]


def mlp_out_body(meta_ref, p, rp, q, rq, gu_ref, wd_ref, hold):
    bit = meta_ref[3]
    two = meta_ref[4]
    hold[bit] = p[...]
    hold[1 - bit] = rp[...]
    hold[2 + two] = q[...]
    hold[3 - two] = rq[...]
    rows = hold.shape[1]
    pair = gu_ref.shape[0]
    for which in range(2):
        gu_ref[which * rows : (which + 1) * rows, :] = hold[which].astype(F32)
    rest = pair - 2 * rows
    gu_ref[2 * rows :, :] = hold[2, :rest, :].astype(F32)
    wd_ref[:, : rows - rest] = hold[2, rest:, :].astype(F32).T
    wd_ref[:, rows - rest :] = hold[3].astype(F32).T


def mlp_out(meta, p, rp, q, rq, width):
    rows, units = p.shape
    return call(
        mlp_out_body,
        "mlp_out",
        [struct((2 * width, units), F32), struct((units, width), F32)],
        (meta, p, rp, q, rq),
        24,
        in_specs=[SM] + [VM] * 4,
        out_specs=[VM] * 2,
        scratch_shapes=[pltpu.VMEM((4, rows, units), BF16)],
    )


def core_body(count, meta_ref, *refs):
    evens, ins = refs[:count], refs[count : 2 * count]
    keep, send = refs[2 * count :]
    rows = evens[0].shape[1]
    for which, (a, b) in enumerate(zip(evens, ins)):
        keep[which * rows : (which + 1) * rows, :] = added(a[0], b[0])
        send[which * rows : (which + 1) * rows, :] = added(a[1], b[1])


def core_sums(meta, evens, ins):
    count = len(evens)
    _, rows, cols = evens[0].shape
    args = (meta, *evens, *ins)
    return call(
        functools.partial(core_body, count),
        "core_sums",
        [struct((count * rows, cols), BF16)] * 2,
        args,
        16,
        in_specs=[SM] + [VM] * (2 * count),
        out_specs=[VM] * 2,
    )


def spread_body(tie_ref, in_ref, out_ref):
    total = in_ref[0].astype(F32)
    for which in range(1, in_ref.shape[0]):
        total = total + in_ref[which].astype(F32)
    total = total.astype(BF16)
    for which in range(in_ref.shape[0]):
        out_ref[which] = total


def spread_sum(tie, pieces):
    return call(spread_body, "spread_sum", [struct(pieces.shape, BF16)], (tie, pieces), 16, in_specs=[SM, VM], out_specs=[VM])[0]


def exchange(value):
    return lax.all_to_all(value, "dp", 0, 0)


def attn_out_body(tie_ref, early_ref, late_ref, qkv_ref, wo_ref):
    wo_ref[...] = early_ref[: 3 * HD, :].astype(F32)
    for part in range(3):
        at = part * HD
        parts = [early_ref[3 * HD + at : 3 * HD + at + HD, :], early_ref[6 * HD + at : 6 * HD + at + HD, :]]
        parts.append(late_ref[at : at + HD, :])
        qkv_ref[part] = jnp.concatenate(parts, axis=0).astype(F32).T


def attn_out(tie, early, late):
    width = early.shape[1]
    return call(
        attn_out_body,
        "attn_out",
        [struct((3, width, 3 * HD), F32), struct((3 * HD, width), F32)],
        (tie, early, late),
        20,
        in_specs=[SM, VM, VM],
        out_specs=[VM, VM],
    )


def add_home_body(meta_ref, in_ref, p0, p1, p2, p3, out_ref):
    slot = pl.program_id(0) ^ meta_ref[2]
    for which, piece in enumerate((p0, p1, p2, p3)):

        @pl.when(slot == which)
        def _():
            out_ref[0] = in_ref[0] + piece[...].astype(F32)


def add_home(meta, base, pieces):
    count, rows, width = base.shape
    block = pl.BlockSpec((1, rows, width), lambda i: (i, 0, 0))
    full = pl.BlockSpec((rows, width), lambda i: (0, 0))
    return call(
        add_home_body,
        "add_home",
        [struct(base.shape, F32)],
        (meta, base, *pieces),
        16,
        grid=(count,),
        in_specs=[SM, block] + [full] * 4,
        out_specs=[block],
    )[0]


def tie(value, *after):
    return lax.optimization_barrier((value, *after))[0]


def local(n_dp, inputs, w_qkv, w_out, w_gate_up, w_down, gain_attn, gain_mlp, piece_starts, out_grad):
    width = inputs.shape[2]
    units = w_down.shape[0]
    here = lax.axis_index("tensor").astype(jnp.int32)
    row = lax.axis_index("dp").astype(jnp.int32)
    bit = row & 1
    bits = [(row >> s) & 1 for s in range(n_dp.bit_length() - 1)]
    mine = lax.dynamic_index_in_dim(piece_starts, here, 0, keepdims=False)[0]
    meta = jnp.concatenate([mine, jnp.stack([here, bits[0], bits[1]])])
    one = gain_attn[None]
    two = gain_mlp[None]
    cosine, sine = rope_tables(LEN, HD)
    tensor = functools.partial(swap, axis="tensor", size=4)
    dp = functools.partial(swap, axis="dp", size=n_dp)

    def picks(whole):
        return [lax.dynamic_index_in_dim(whole, here ^ k, 0, keepdims=False).astype(BF16) for k in range(4)]

    def around(pieces):
        return [pieces[0]] + [tensor(pieces[k], mask=k) for k in range(1, 4)]

    def far(half):
        direct = tensor(half, mask=2)
        other = dp(direct, mask=1)
        return direct, other, tensor(direct, mask=1), tensor(other, mask=1)

    x_mine = picks(inputs)
    xs = around(x_mine)
    wa0 = jnp.concatenate([jnp.swapaxes(w_qkv, 1, 2), w_out[None]]).astype(BF16)
    wa1 = tensor(wa0, mask=1)
    wa_far = far(lax.dynamic_slice_in_dim(wa0, 2 * bit, 2, 0))
    wm0 = jnp.concatenate([w_gate_up, w_down.T[None]]).astype(BF16)
    wm1 = tensor(wm0, mask=1)
    wm_far = far(lax.dynamic_slice_in_dim(wm0.reshape(3 * width, units), 3 * width // 2 * bit, 3 * width // 2, 0))
    gs = around(picks(out_grad))

    last = [meta]

    def run(kernel, first, *args, **kw):
        out = kernel(tie(first, last[0]), *args, **kw)
        last[0] = out[0] if isinstance(out, (list, tuple)) else out
        return out

    x, n1, qa, ka, va = run(project_first, meta, xs, one, wa0, wa1, cosine, sine)
    mta, ma, la = run(attend, meta, qa, ka, va)
    qb, kb, vb, wa2, wa3 = run(project_next, meta, n1, wa_far, cosine, sine)
    wa = (wa0, wa1, wa2, wa3)
    mtb, mb, lb = run(attend, meta, qb, kb, vb)
    after, n2, n2t, g, gt = run(after_attention, meta, x, ma, mb, wa, two, gs)
    acc_out, acc_back, dw1, dw0 = run(mlp, meta, n2, n2t, g, gt, ((wm1,), (wm0,)))
    in1 = tensor(dw1, mask=1)
    acc_out, acc_back, dw3 = run(mlp, meta, n2, n2t, g, gt, (wm_far[2:],), (acc_out, acc_back))
    in3 = tensor(dw3, mask=1)
    acc_out, acc_back, dw2 = run(mlp, meta, n2, n2t, g, gt, (wm_far[:2],), (acc_out, acc_back))
    keep_p, send_p, keep_q, send_q = run(start_sums, meta, dw0, in1, dw2, in3)
    recv_p = dp(send_p, mask=1)
    recv_q = dp(send_q, mask=2)
    middle_out = run(middle, meta, x, after, acc_out, acc_back, g, two, (mta, mtb), wa)
    home = around(middle_out[:4])
    da, do, even_o, odd_o, gain_two = middle_out[4:]
    in_o = tensor(odd_o, mask=1)
    sets = ((qa, ka, va, mta, la), (qb, kb, vb, mtb, lb))
    back = lambda turn: run(lambda m: attend_back(turn, m, cosine, sine, n1, sets, do), meta)
    dt0, even0, odd0 = back(0)
    in0 = tensor(odd0, mask=1)
    keep, send = run(second_sums, meta, keep_p, recv_p, keep_q, recv_q)
    recv = tensor(send, mask=2)
    dt1, even1, odd1 = back(1)
    in1_ = tensor(odd1, mask=1)
    outputs = run(add_home, meta, inputs, home)
    early, early_send = run(core_sums, meta, (even_o, even0, even1), (in_o, in0, in1_))
    early_recv = tensor(early_send, mask=2)
    keep, send_p, send_q = run(third_sums, meta, keep, recv)
    recv_p = dp(send_p, mask=2)
    recv_q = dp(send_q, mask=1)
    (before,) = run(lambda m: token_grad(m, (0, 1), (dt0, dt1), wa), meta)
    pieces = (recv_p, recv_q)
    for shift in range(2, len(bits)):
        keep, send = run(halve_sums, bits[shift], keep, *pieces)
        pieces = dp(send, mask=1 << shift)
    dt2, even2, odd2 = back(2)
    in2 = tensor(odd2, mask=1)
    piece = run(plain_sum, meta, keep, pieces)
    other = dp(piece, mask=1 << (len(bits) - 1))
    early = run(plain_sum, meta, early, early_recv)
    early = exchange(early.reshape(n_dp, -1, width))
    late, late_send = run(core_sums, meta, (even2,), (in2,))
    late_recv = tensor(late_send, mask=2)
    *grads, gain_one = run(lambda m: token_grad(m, (2,), (dt2,), wa, (before, x, da, g, one)), meta)
    grads = around(grads)
    late = run(plain_sum, meta, late, late_recv)
    late = exchange(late.reshape(n_dp, -1, width))
    for shift in reversed(range(2, len(bits))):
        piece = run(pair_join, bits[shift], piece, other)
        if shift > 2:
            other = dp(piece, mask=1 << (shift - 1))
    recv_p = dp(piece[0], mask=2)
    recv_q = dp(piece[1], mask=1)
    early = exchange(run(spread_sum, meta, early))
    p, q = run(cross_join, meta, piece, recv_p, recv_q)
    recv_p = dp(p, mask=1)
    recv_q = dp(q, mask=2)
    gains = jnp.concatenate([gain_one, gain_two])
    gains = gains + tensor(gains, mask=1)
    gains = gains + tensor(gains, mask=2)
    for shift in range(len(bits)):
        gains = gains + dp(gains, mask=1 << shift)
    late = exchange(run(spread_sum, meta, late))
    input_grad = run(add_home, meta, out_grad, grads)
    grad_pair, grad_down = run(mlp_out, meta, p, recv_p, q, recv_q, width)
    grad_qkv, grad_out = run(attn_out, meta, early.reshape(9 * HD, width), late.reshape(3 * HD, width))
    return (
        outputs,
        input_grad,
        grad_qkv,
        grad_out,
        grad_pair.reshape(2, width, units),
        grad_down,
        gains[0],
        gains[1],
    )


def solution(mesh):
    rows = P(None, ("dp", "tensor"), None)
    weights = (P(None, None, "tensor"), P("tensor", None), P(None, None, "tensor"), P("tensor", None))
    return jax.shard_map(
        functools.partial(local, mesh.shape["dp"]),
        mesh=mesh,
        in_specs=(rows, *weights, P(), P(), P(None, "dp", None), rows),
        out_specs=(rows, rows, *weights, P(), P()),
        check_vma=False,
    )
```

```python
import functools
import jax
import jax.numpy as jnp
import numpy as np
from jax import lax
from jax.experimental import pallas as pl
from jax.experimental.pallas import tpu as pltpu
from jax.sharding import PartitionSpec as P

HD = 64
LEN = 1024
PIECE = 256
HALF = 512
EPS = 1e-06
F32 = jnp.float32
BF16 = jnp.bfloat16
MIB = 1024 * 1024


def nn(a, b):
    return lax.dot_general(a, b, (((1,), (0,)), ((), ())), preferred_element_type=F32)


def nt(a, b):
    return lax.dot_general(a, b, (((1,), (1,)), ((), ())), preferred_element_type=F32)


COST = {
    "project_first": 5,
    "project_next": 5,
    "attend": 10,
    "after_attention": 5,
    "mlp": 15,
    "middle": 10,
    "attend_back": 4,
    "token_grad": 1,
    "start_sums": 1,
    "add_home": 0.2,
    "mlp_out": 0.5,
}
RATE = 1e9


def call(body, name, out_shape, args, vmem, **kw):
    return pl.pallas_call(
        body,
        name=name,
        out_shape=out_shape,
        compiler_params=pltpu.CompilerParams(vmem_limit_bytes=vmem * MIB),
        cost_estimate=pl.CostEstimate(flops=int(COST.get(name, 0.3) * RATE), bytes_accessed=0, transcendentals=0),
        **kw,
    )(*args)


def struct(shape, dtype):
    return jax.ShapeDtypeStruct(shape, dtype)


def project(n1_ref, weights, cos_ref, sin_ref, q_ref, k_ref, v_ref):
    step = 256
    for block in range(LEN // step):
        cols = slice(block * step, (block + 1) * step)
        rows = n1_ref[cols, :]
        cosine = cos_ref[:, cols]
        sine = sin_ref[:, cols]
        for slot, w_ref in enumerate(weights):
            for part, ref in ((0, q_ref), (1, k_ref), (2, v_ref)):
                made = nt(w_ref[part], rows)
                for head in range(3):
                    low = made[head * HD : head * HD + HD // 2]
                    high = made[head * HD + HD // 2 : (head + 1) * HD]
                    if part < 2:
                        low, high = low * cosine - high * sine, high * cosine + low * sine
                    if part == 0:
                        low, high = low * HD**-0.5, high * HD**-0.5
                    at = slot * HD
                    ref[head, at : at + HD // 2, cols] = low.astype(BF16)
                    ref[head, at + HD // 2 : at + HD, cols] = high.astype(BF16)


def in_order(here, pieces, ref):
    step = ref.shape[0] // 4
    for quarter in range(4):
        for slot, piece in enumerate(pieces):

            @pl.when((here ^ slot) == quarter)
            def _():
                ref[quarter * step : (quarter + 1) * step, :] = piece[...]


def project_first_body(meta_ref, p0, p1, p2, p3, gain_ref, w0, w1, cos_ref, sin_ref, x_ref, n1_ref, q_ref, k_ref, v_ref):
    step = 256
    gain = gain_ref[...]
    in_order(meta_ref[2], (p0, p1, p2, p3), x_ref)
    for block in range(LEN // step):
        rows = slice(block * step, (block + 1) * step)
        x = x_ref[rows, :].astype(F32)
        scale = lax.rsqrt(jnp.mean(x * x, axis=-1, keepdims=True) + EPS)
        n1_ref[rows, :] = (x * scale * gain).astype(BF16)
    project(n1_ref, (w0, w1), cos_ref, sin_ref, q_ref, k_ref, v_ref)


def project_next_body(
    meta_ref, n1_ref, d2, r2, d3, r3, cos_ref, sin_ref, q_ref, k_ref, v_ref, w2_ref, w3_ref
):
    bit = meta_ref[3]
    for direct, other, ref in ((d2, r2, w2_ref), (d3, r3, w3_ref)):
        for part in range(2):
            ref[2 * bit + part] = direct[part]
            ref[2 * (1 - bit) + part] = other[part]
    project(n1_ref, (w2_ref, w3_ref), cos_ref, sin_ref, q_ref, k_ref, v_ref)


HEADS3 = (3, 2 * HD, LEN)


VM = pl.BlockSpec(memory_space=pltpu.VMEM)
SM = pl.BlockSpec(memory_space=pltpu.SMEM)


def project_first(meta, pieces, gain, w0, w1, cosine, sine):
    width = gain.shape[1]
    out = [struct((LEN, width), BF16)] * 2 + [struct(HEADS3, BF16)] * 3
    args = (meta, *pieces, gain, w0, w1, cosine, sine)
    return call(
        project_first_body,
        "project_first",
        out,
        args,
        24,
        in_specs=[SM] + [VM] * (len(args) - 1),
        out_specs=[VM] * len(out),
    )


def project_next(meta, n1, far, cosine, sine):
    out = [struct(HEADS3, BF16)] * 3 + [struct((4,) + far[0].shape[1:], BF16)] * 2
    args = (meta, n1, *far, cosine, sine)
    return call(
        project_next_body,
        "project_next",
        out,
        args,
        24,
        in_specs=[SM] + [VM] * (len(args) - 1),
        out_specs=[VM] * len(out),
    )


def limits(starts_ref):
    pos = lax.broadcasted_iota(jnp.int32, (1, LEN), 1)
    lim = pos
    for piece in range(2):
        first = starts_ref[piece]
        lim = jnp.where((pos >= first) & (pos < first + PIECE), first + PIECE - 1, lim)
    return lim


def one_head(block, head):
    zero = jnp.zeros((HD, block.shape[1]), block.dtype)
    part = block[head * HD : (head + 1) * HD]
    return jnp.concatenate([part, zero] if head == 0 else [zero, part], axis=0)


NEG = -1e30


def attend_body(qb, starts_ref, q_ref, k_ref, v_ref, mt_ref, m_ref, lse_ref):
    lim = limits(starts_ref)
    k_rows = k_ref[0].T
    for head in range(2):
        q_one = one_head(q_ref[0], head)
        v_one = v_ref[0, head * HD : (head + 1) * HD, :]
        for block in range(LEN // qb):
            cols = slice(block * qb, (block + 1) * qb)
            keys = HALF if (block + 1) * qb <= HALF else LEN
            scores = nn(k_rows[:keys], q_one[:, cols])
            edge = scores[keys - HALF :]
            pos = lax.broadcasted_iota(jnp.int32, (HALF, qb), 0) + (keys - HALF)
            edge = jnp.where(pos <= lim[:, cols], edge, NEG)
            most = jnp.max(edge, axis=0, keepdims=True)
            if keys > HALF:
                body = scores[:HALF]
                most = jnp.maximum(most, jnp.max(body, axis=0, keepdims=True))
            soft = jnp.exp(edge - most)
            total = jnp.sum(soft, axis=0, keepdims=True)
            mixed = nn(v_one[:, keys - HALF : keys], soft.astype(BF16))
            if keys > HALF:
                soft = jnp.exp(body - most)
                total = total + jnp.sum(soft, axis=0, keepdims=True)
                mixed = mixed + nn(v_one[:, :HALF], soft.astype(BF16))
            mt_ref[0, head * HD : (head + 1) * HD, cols] = (mixed * (1.0 / total)).astype(BF16)
            lse_ref[0, head : head + 1, cols] = most + jnp.log(total)
    m_ref[...] = mt_ref[0].T


def attend(starts, q, k, v, qb=512):
    block = pl.BlockSpec((1, 2 * HD, LEN), lambda i: (i, 0, 0))
    out = [struct(HEADS3, BF16), struct((LEN, 6 * HD), BF16), struct((3, 2, LEN), F32)]
    return call(
        functools.partial(attend_body, qb),
        "attend",
        out,
        (starts, q, k, v),
        24,
        grid=(3,),
        in_specs=[pl.BlockSpec(memory_space=pltpu.SMEM), block, block, block],
        out_specs=[
            block,
            pl.BlockSpec((LEN, 2 * HD), lambda i: (0, i)),
            pl.BlockSpec((1, 2, LEN), lambda i: (i, 0, 0)),
        ],
    )


def attend_back_body(qb, starts_ref, cos_ref, sin_ref, n1_ref, *refs):
    sets = (refs[0:5], refs[5:10])
    do_ref = refs[10]
    dt_ref, even_ref, odd_ref, acc_ref = refs[11:]
    lim = limits(starts_ref)
    for which, (q_ref, k_ref, v_ref, mt_ref, lse_ref) in enumerate(sets):
        q = q_ref[0]
        k = k_ref[0]
        v = v_ref[0]
        do = do_ref[which * 2 * HD : (which + 1) * 2 * HD, :]
        k_rows = k.T
        v_rows = v.T
        both = do.astype(F32) * mt_ref[0].astype(F32)
        for head in range(2):
            mine = slice(head * HD, (head + 1) * HD)
            inner = jnp.sum(both[mine], axis=0, keepdims=True)
            q_one = one_head(q, head)
            do_one = one_head(do, head)
            lse = lse_ref[0, head : head + 1, :]
            for block in range(LEN // qb):
                cols = slice(block * qb, (block + 1) * qb)
                wide = (block + 1) * qb > HALF
                dq = None
                for part in range(2 if wide else 1):
                    keys = slice(part * HALF, (part + 1) * HALF)
                    scores = nn(k_rows[keys], q_one[:, cols])
                    if part == (1 if wide else 0):
                        pos = lax.broadcasted_iota(jnp.int32, (HALF, qb), 0) + part * HALF
                        scores = jnp.where(pos <= lim[:, cols], scores, NEG)
                    soft = jnp.exp(scores - lse[:, cols])
                    grad = nn(v_rows[keys], do_one[:, cols])
                    grad = (soft * (grad - inner[:, cols])).astype(BF16)
                    more = nn(k[mine, keys], grad)
                    dq = more if dq is None else dq + more
                    dk = nt(q[mine, cols], grad)
                    dv = nt(do[mine, cols], soft.astype(BF16))
                    fresh = block == (0 if part == 0 else HALF // qb)
                    if fresh:
                        acc_ref[1, mine, keys] = dk
                        acc_ref[2, mine, keys] = dv
                    else:
                        acc_ref[1, mine, keys] += dk
                        acc_ref[2, mine, keys] += dv
                acc_ref[0, mine, cols] = dq * HD**-0.5
        cosine = cos_ref[...]
        sine = sin_ref[...]
        for part in range(3):
            for head in range(2):
                at = head * HD
                low = acc_ref[part, at : at + HD // 2, :]
                high = acc_ref[part, at + HD // 2 : at + HD, :]
                if part < 2:
                    low, high = low * cosine + high * sine, high * cosine - low * sine
                to = which * 2 * HD + at
                dt_ref[part, to : to + HD // 2, :] = low.astype(BF16)
                dt_ref[part, to + HD // 2 : to + HD, :] = high.astype(BF16)
    for part in range(3):
        made = nn(dt_ref[part], n1_ref[...])
        for slot in range(4):
            ref = odd_ref if slot % 2 else even_ref
            ref[slot // 2, part * HD : (part + 1) * HD, :] = made[slot * HD : (slot + 1) * HD].astype(BF16)


def attend_back(turn, starts, cosine, sine, n1, sets, do, qb=512):
    width = n1.shape[1]
    head = pl.BlockSpec((1, 2 * HD, LEN), lambda i: (turn, 0, 0))
    full = lambda a: pl.BlockSpec(a.shape, lambda i, n=a.ndim: (0,) * n)
    lse = pl.BlockSpec((1, 2, LEN), lambda i: (turn, 0, 0))
    args = (starts, cosine, sine, n1, *sets[0], *sets[1], do)
    out = [struct((3, 4 * HD, LEN), BF16)] + [struct((2, 3 * HD, width), BF16)] * 2
    return call(
        functools.partial(attend_back_body, qb),
        "attend_back",
        out,
        args,
        40,
        grid=(1,),
        in_specs=[pl.BlockSpec(memory_space=pltpu.SMEM), full(cosine), full(sine), full(n1)]
        + [head, head, head, head, lse] * 2
        + [pl.BlockSpec((4 * HD, LEN), lambda i: (turn, 0))],
        out_specs=[full(o) for o in out],
        scratch_shapes=[pltpu.VMEM((3, 2 * HD, LEN), F32)],
    )


def turn_rows(w_refs):
    return jnp.concatenate(
        [w[3, turn * HD : (turn + 1) * HD, :] for turn in range(3) for w in w_refs], axis=0
    )


def after_body(
    meta_ref, x_ref, ma_ref, mb_ref, w0, w1, w2, w3, gain_ref, g0, g1, g2, g3,
    after_ref, n2_ref, n2t_ref, g_ref, gt_ref,
):
    slot = pl.program_id(0) ^ meta_ref[2]
    for which, piece in enumerate((g0, g1, g2, g3)):

        @pl.when(slot == which)
        def _():
            g_ref[...] = piece[...]

    first = turn_rows((w0, w1))
    second = turn_rows((w2, w3))
    after = x_ref[...].astype(F32) + nn(ma_ref[...], first) + nn(mb_ref[...], second)
    after_ref[...] = after
    scale = lax.rsqrt(jnp.mean(after * after, axis=-1, keepdims=True) + EPS)
    normed = (after * scale * gain_ref[...]).astype(BF16)
    n2_ref[...] = normed
    n2t_ref[...] = normed.T
    gt_ref[...] = g_ref[...].T


def after_attention(meta, x, mixed_a, mixed_b, wo, gain, g):
    width = x.shape[1]
    step = 256
    rows = lambda n: pl.BlockSpec((step, n), lambda i: (i, 0))
    cols = pl.BlockSpec((width, step), lambda i: (0, i))
    full = lambda a: pl.BlockSpec(a.shape, lambda i, n=a.ndim: (0,) * n)
    args = (meta, x, mixed_a, mixed_b, *wo, gain, *g)
    out = [
        struct((LEN, width), F32),
        struct((LEN, width), BF16),
        struct((width, LEN), BF16),
        struct((LEN, width), BF16),
        struct((width, LEN), BF16),
    ]
    return call(
        after_body,
        "after_attention",
        out,
        args,
        30,
        grid=(LEN // step,),
        in_specs=[SM, rows(width), rows(6 * HD), rows(6 * HD)]
        + [full(w) for w in wo]
        + [full(gain)]
        + [full(p) for p in g],
        out_specs=[rows(width), rows(width), cols, rows(width), cols],
    )


def mlp_body(layout, first, meta_ref, n2_ref, n2t_ref, g_ref, gt_ref, *refs):
    block = 256
    refs = list(refs)
    sources = [[refs.pop(0) for _ in range(kind)] for kind in layout]
    if not first:
        out_in, back_in = refs.pop(0), refs.pop(0)
    out_ref, back_ref = refs.pop(0), refs.pop(0)
    made = [refs.pop(0) for _ in layout]
    hid, dga, dup = refs[:3]
    if first:
        out_ref[...] = jnp.zeros_like(out_ref)
        back_ref[...] = jnp.zeros_like(back_ref)
    else:
        out_ref[...] = out_in[...]
        back_ref[...] = back_in[...]
    width = n2_ref.shape[1]
    half = 3 * width // 2
    for source, dw_ref in zip(sources, made):
        if len(source) == 2:
            hold = refs[3]
            hold[meta_ref[3]] = source[0][...]
            hold[1 - meta_ref[3]] = source[1][...]

            def take(part, cols, hold=hold):
                if part == 0:
                    return hold[0, :width, cols]
                if part == 2:
                    return hold[1, half - width :, cols]
                return jnp.concatenate([hold[0, width:, cols], hold[1, : half - width, cols]], axis=0)
        else:

            def take(part, cols, hold=source[0]):
                return hold[part, :, cols]

        for part in range(2):
            cols = slice(part * block, (part + 1) * block)
            wg = take(0, cols)
            wu = take(1, cols)
            wl = take(2, cols)
            n2 = n2_ref[...]
            gate = nn(n2, wg)
            up = nn(n2, wu)
            grad = nn(g_ref[...], wl)
            sigma = 1.0 / (1.0 + jnp.exp(-gate))
            silu = gate * sigma
            hid[...] = (silu * up).astype(BF16)
            dup[...] = (grad * silu).astype(BF16)
            dga[...] = (grad * up * (sigma * (1.0 + gate * (1.0 - sigma)))).astype(BF16)
            out_ref[...] += nt(hid[...], wl)
            back_ref[...] += nt(dga[...], wg) + nt(dup[...], wu)
            dw_ref[0, :, cols] = nn(n2t_ref[...], dga[...]).astype(BF16)
            dw_ref[1, :, cols] = nn(n2t_ref[...], dup[...]).astype(BF16)
            dw_ref[2, :, cols] = nn(gt_ref[...], hid[...]).astype(BF16)


def mlp(meta, n2, n2t, g, gt, weights, before=()):
    width = n2.shape[1]
    units = 512
    layout = tuple(len(w) for w in weights)
    out = [struct((LEN, width), F32)] * 2 + [struct((3, width, units), BF16)] * len(weights)
    args = (meta, n2, n2t, g, gt, *[a for w in weights for a in w], *before)
    scratch = [pltpu.VMEM((LEN, 256), BF16)] * 3
    if 2 in layout:
        scratch.append(pltpu.VMEM((2, 3 * width // 2, units), BF16))
    aliases = {len(args) - 2: 0, len(args) - 1: 1} if before else {}
    return call(
        functools.partial(mlp_body, layout, not before),
        "mlp",
        out,
        args,
        50,
        in_specs=[SM] + [VM] * (len(args) - 1),
        out_specs=[VM] * len(out),
        scratch_shapes=scratch,
        input_output_aliases=aliases,
    )


def norm_back(grad, value, gain):
    scale = lax.rsqrt(jnp.mean(value * value, axis=-1, keepdims=True) + EPS)
    unit = value * scale
    gain_grad = jnp.sum(grad * unit, axis=0, keepdims=True)
    e = grad * gain
    return scale * (e - unit * jnp.mean(e * unit, axis=-1, keepdims=True)), gain_grad


def give(meta_ref, value, refs):
    slot = pl.program_id(0) ^ meta_ref[2]
    for which, ref in enumerate(refs[:2]):

        @pl.when(slot == which)
        def _():
            ref[...] = value

    for which in range(2):

        @pl.when(slot == 2 + which)
        def _():
            refs[2][which] = value


def middle_body(
    meta_ref, x_ref, after_ref, sum_ref, back_ref, g_ref, gain_ref, mta_ref, mtb_ref,
    w0, w1, w2, w3, e0, e1, e23, da_ref, do_ref, even_ref, odd_ref, gain_out, acc,
):
    step = pl.program_id(0)
    after = after_ref[...]
    delta = (after - x_ref[...].astype(F32) + sum_ref[...]).astype(BF16)
    give(meta_ref, delta, (e0, e1, e23))
    back, gain_grad = norm_back(back_ref[...], after, gain_ref[...])
    grad_after = g_ref[...].astype(F32) + back
    da_ref[...] = grad_after
    low = grad_after.astype(BF16)

    @pl.when(step == 0)
    def _():
        gain_out[...] = jnp.zeros_like(gain_out)
        acc[...] = jnp.zeros_like(acc)

    gain_out[...] += gain_grad
    weights = turn_rows((w0, w1, w2, w3))
    do_ref[...] = nt(weights, low).astype(BF16)
    for turn in range(3):
        for which, mt in enumerate((mta_ref, mtb_ref)):
            acc[turn, which] += nn(mt[turn], low)

    @pl.when(step == pl.num_programs(0) - 1)
    def _():
        for turn in range(3):
            for slot in range(4):
                at = (slot % 2) * HD
                ref = odd_ref if slot % 2 else even_ref
                ref[slot // 2, turn * HD : (turn + 1) * HD, :] = acc[turn, slot // 2, at : at + HD, :].astype(BF16)


def middle(meta, x, after, total, back, g, gain, mts, wo):
    width = x.shape[1]
    step = 256
    rows = pl.BlockSpec((step, width), lambda i: (i, 0))
    full = lambda a: pl.BlockSpec(a.shape, lambda i, n=a.ndim: (0,) * n)
    heads = pl.BlockSpec((3, 2 * HD, step), lambda i: (0, 0, i))
    args = (meta, x, after, total, back, g, gain, *mts, *wo)
    out = [struct((step, width), BF16)] * 2 + [
        struct((2, step, width), BF16),
        struct((LEN, width), F32),
        struct((12 * HD, LEN), BF16),
        struct((2, 3 * HD, width), BF16),
        struct((2, 3 * HD, width), BF16),
        struct((1, width), F32),
    ]
    return call(
        middle_body,
        "middle",
        out,
        args,
        40,
        grid=(LEN // step,),
        in_specs=[SM] + [rows] * 5 + [full(gain), heads, heads] + [full(w) for w in wo],
        out_specs=[full(o) for o in out[:3]]
        + [rows, pl.BlockSpec((12 * HD, step), lambda i: (0, i)), full(out[5]), full(out[6]), full(out[7])],
        scratch_shapes=[pltpu.VMEM((3, 2, 2 * HD, width), F32)],
    )


def token_grad_body(turns, last, meta_ref, *refs):
    dts = refs[: len(turns)]
    weights = refs[len(turns) : len(turns) + 4]
    rest = refs[len(turns) + 4 :]
    step = pl.program_id(0)
    total = None
    for turn, dt in zip(turns, dts):
        for part in range(3):
            w = jnp.concatenate([w[part, turn * HD : (turn + 1) * HD, :] for w in weights], axis=0)
            more = nn(dt[part].T, w)
            total = more if total is None else total + more
    if not last:
        rest[0][...] = total
        return
    before_ref, x_ref, da_ref, g_ref, gain_ref, e0, e1, e23, gain_out = rest
    total = total + before_ref[...]
    back, gain_grad = norm_back(total, x_ref[...].astype(F32), gain_ref[...])
    give(meta_ref, (da_ref[...] - g_ref[...].astype(F32) + back).astype(BF16), (e0, e1, e23))

    @pl.when(step == 0)
    def _():
        gain_out[...] = jnp.zeros_like(gain_out)

    gain_out[...] += gain_grad


def token_grad(meta, turns, dts, weights, rest=None):
    width = weights[0].shape[2]
    step = 256
    rows = pl.BlockSpec((step, width), lambda i: (i, 0))
    full = lambda a: pl.BlockSpec(a.shape, lambda i, n=a.ndim: (0,) * n)
    cols = pl.BlockSpec((3, 4 * HD, step), lambda i: (0, 0, i))
    specs = [SM] + [cols] * len(dts) + [full(w) for w in weights]
    args = (meta, *dts, *weights)
    if rest is None:
        out = [struct((LEN, width), F32)]
        out_specs = [rows]
    else:
        out = [struct((step, width), BF16)] * 2 + [struct((2, step, width), BF16), struct((1, width), F32)]
        out_specs = [full(o) for o in out]
        specs = specs + [rows] * 4 + [full(rest[4])]
        args = args + tuple(rest)
    return call(
        functools.partial(token_grad_body, turns, rest is not None),
        "token_grad",
        out,
        args,
        30,
        grid=(LEN // step,),
        in_specs=specs,
        out_specs=out_specs,
    )


def rope_tables(length, width):
    halfway = width // 2
    inverse = 10000.0 ** (-jnp.arange(halfway, dtype=F32) * 2.0 / width)
    angles = inverse[:, None] * jnp.arange(length, dtype=F32)[None, :]
    return jnp.cos(angles), jnp.sin(angles)


def swap(value, axis, size, mask):
    return lax.ppermute(value, axis, [(i, i ^ mask) for i in range(size)])


def added(*refs):
    total = refs[0].astype(F32)
    for ref in refs[1:]:
        total = total + ref.astype(F32)
    return total.astype(BF16)


def put(cond, ref, at, value):
    @pl.when(cond)
    def _():
        if at is None:
            ref[...] = value
        else:
            ref[at] = value


def start_body(meta_ref, a0, b0, a2, b2, keep_p, send_p, keep_q, send_q):
    step = pl.program_id(0)
    bit = meta_ref[3]
    two = meta_ref[4]
    for slot, (a, b) in enumerate(((a0, b0), (a2, b2))):
        value = added(a[0], b[0])
        put(step == bit, keep_p, slot, value)
        put(step == 1 - bit, send_p, slot, value)
        put(step == 2 + two, keep_q, slot, value)
        put(step == 3 - two, send_q, slot, value)


def start_sums(meta, dw0, in1, dw2, in3):
    rows = dw0.shape[0] * dw0.shape[1] // 4
    cols = dw0.shape[2]
    parts = [a.reshape(4, rows, cols) for a in (dw0, in1, dw2, in3)]
    out = [struct((2, rows, cols), BF16)] * 4
    return call(
        start_body,
        "start_sums",
        out,
        (meta, *parts),
        16,
        grid=(4,),
        in_specs=[SM] + [pl.BlockSpec((1, rows, cols), lambda i: (i, 0, 0))] * 4,
        out_specs=[pl.BlockSpec((2, rows, cols), lambda i: (0, 0, 0))] * 4,
    )


def second_body(meta_ref, kp, rp, kq, rq, keep, send_p, send_q):
    step = pl.program_id(0)
    for which, (k, r, send, bit) in enumerate(((kp, rp, send_p, meta_ref[4]), (kq, rq, send_q, meta_ref[3]))):
        for slot in range(2):
            value = added(k[slot, 0], r[slot, 0])
            put(step == bit, keep, (which, slot), value)
            put(step == 1 - bit, send, slot, value)


def second_sums(meta, *pieces):
    _, rows, cols = pieces[0].shape
    half = rows // 2
    full = lambda n: pl.BlockSpec((2,) * n + (half, cols), lambda i: (0,) * (n + 2))
    return call(
        second_body,
        "second_sums",
        [struct((2, 2, half, cols), BF16)] + [struct((2, half, cols), BF16)] * 2,
        (meta, *[p.reshape(2, 2, half, cols) for p in pieces]),
        20,
        grid=(2,),
        in_specs=[SM] + [pl.BlockSpec((2, 1, half, cols), lambda i: (0, i, 0, 0))] * 4,
        out_specs=[full(2), full(1), full(1)],
    )


def third_body(meta_ref, a, bp, bq, keep, send):
    which = pl.program_id(0)
    for part, b in enumerate((bp, bq)):

        @pl.when(which == part)
        def _():
            keep[0] = added(a[0, 0], b[0])
            send[0] = added(a[0, 1], b[1])


def third_sums(meta, a, bp, bq):
    _, _, rows, cols = a.shape
    whole = pl.BlockSpec((2, rows, cols), lambda i: (0, 0, 0))
    block = pl.BlockSpec((1, rows, cols), lambda i: (i, 0, 0))
    return call(
        third_body,
        "third_sums",
        [struct((2, rows, cols), BF16)] * 2,
        (meta, a, bp, bq),
        12,
        grid=(2,),
        in_specs=[SM, pl.BlockSpec((1, 2, rows, cols), lambda i: (i, 0, 0, 0)), whole, whole],
        out_specs=[block, block],
    )


def halve_body(bit_ref, a, b, keep, send):
    bit = bit_ref[0]
    step = pl.program_id(0)
    for which in range(2):
        value = added(a[which, 0], b[which, 0])
        put(step == bit, keep, which, value)
        put(step != bit, send, which, value)


def halve_sums(bit, a, b):
    _, rows, cols = a.shape
    half = rows // 2
    return call(
        halve_body,
        "halve_sums",
        [struct((2, half, cols), BF16)] * 2,
        (bit.reshape(1), a.reshape(2, 2, half, cols), b.reshape(2, 2, half, cols)),
        12,
        grid=(2,),
        in_specs=[SM] + [pl.BlockSpec((2, 1, half, cols), lambda i: (0, i, 0, 0))] * 2,
        out_specs=[pl.BlockSpec((2, half, cols), lambda i: (0, 0, 0))] * 2,
    )


def plain_body(tie_ref, a, b, out):
    out[...] = added(a[...], b[...])


def plain_sum(tie, a, b):
    return call(plain_body, "plain_sum", [struct(a.shape, BF16)], (tie, a, b), 12, in_specs=[SM, VM, VM], out_specs=[VM])[0]


def split_body(bit_ref, a, b, keep, send):
    bit = bit_ref[0]
    step = pl.program_id(0)
    value = added(a[0], b[0])
    put(step == bit, keep, None, value)
    put(step != bit, send, None, value)


def split_sums(bit, a, b):
    rows, cols = a.shape
    half = rows // 2
    return call(
        split_body,
        "split_sums",
        [struct((half, cols), BF16)] * 2,
        (bit.reshape(1), a.reshape(2, half, cols), b.reshape(2, half, cols)),
        12,
        grid=(2,),
        in_specs=[SM] + [pl.BlockSpec((1, half, cols), lambda i: (i, 0, 0))] * 2,
        out_specs=[pl.BlockSpec((half, cols), lambda i: (0, 0))] * 2,
    )


def merge_body(bit_ref, a, b, out):
    bit = bit_ref[0]
    out[bit] = a[...]
    out[1 - bit] = b[...]


def merge(bit, a, b):
    rows, cols = a.shape
    made = call(
        merge_body,
        "merge",
        [struct((2, rows, cols), BF16)],
        (bit.reshape(1), a, b),
        12,
        in_specs=[SM, VM, VM],
        out_specs=[VM],
    )[0]
    return made.reshape(2 * rows, cols)


def pair_body(bit_ref, a, b, out):
    bit = bit_ref[0]
    for which in range(2):
        out[which, bit] = a[which]
        out[which, 1 - bit] = b[which]


def pair_join(bit, a, b):
    _, rows, cols = a.shape
    made = call(
        pair_body,
        "pair_join",
        [struct((2, 2, rows, cols), BF16)],
        (bit.reshape(1), a, b),
        12,
        in_specs=[SM, VM, VM],
        out_specs=[VM],
    )[0]
    return made.reshape(2, 2 * rows, cols)


def cross_body(meta_ref, a, bp, bq, out_p, out_q):
    two = meta_ref[4]
    bit = meta_ref[3]
    out_p[two] = a[0]
    out_p[1 - two] = bp[...]
    out_q[bit] = a[1]
    out_q[1 - bit] = bq[...]


def cross_join(meta, a, bp, bq):
    _, rows, cols = a.shape
    made = call(
        cross_body,
        "cross_join",
        [struct((2, rows, cols), BF16)] * 2,
        (meta, a, bp, bq),
        12,
        in_specs=[SM, VM, VM, VM],
        out_specs=[VM, VM],
    )
    return [m.reshape(2 * rows, cols) for m in made]


def mlp_out_body(meta_ref, p, rp, q, rq, gu_ref, wd_ref, hold):
    bit = meta_ref[3]
    two = meta_ref[4]
    hold[bit] = p[...]
    hold[1 - bit] = rp[...]
    hold[2 + two] = q[...]
    hold[3 - two] = rq[...]
    rows = hold.shape[1]
    pair = gu_ref.shape[0]
    for which in range(2):
        gu_ref[which * rows : (which + 1) * rows, :] = hold[which].astype(F32)
    rest = pair - 2 * rows
    gu_ref[2 * rows :, :] = hold[2, :rest, :].astype(F32)
    wd_ref[:, : rows - rest] = hold[2, rest:, :].astype(F32).T
    wd_ref[:, rows - rest :] = hold[3].astype(F32).T


def mlp_out(meta, p, rp, q, rq, width):
    rows, units = p.shape
    return call(
        mlp_out_body,
        "mlp_out",
        [struct((2 * width, units), F32), struct((units, width), F32)],
        (meta, p, rp, q, rq),
        24,
        in_specs=[SM] + [VM] * 4,
        out_specs=[VM] * 2,
        scratch_shapes=[pltpu.VMEM((4, rows, units), BF16)],
    )


def core_body(count, meta_ref, *refs):
    evens, ins = refs[:count], refs[count : 2 * count]
    keep, send = refs[2 * count :]
    rows = evens[0].shape[1]
    for which, (a, b) in enumerate(zip(evens, ins)):
        keep[which * rows : (which + 1) * rows, :] = added(a[0], b[0])
        send[which * rows : (which + 1) * rows, :] = added(a[1], b[1])


def core_sums(meta, evens, ins):
    count = len(evens)
    _, rows, cols = evens[0].shape
    args = (meta, *evens, *ins)
    return call(
        functools.partial(core_body, count),
        "core_sums",
        [struct((count * rows, cols), BF16)] * 2,
        args,
        16,
        in_specs=[SM] + [VM] * (2 * count),
        out_specs=[VM] * 2,
    )


def spread_body(tie_ref, in_ref, out_ref):
    total = in_ref[0].astype(F32)
    for which in range(1, in_ref.shape[0]):
        total = total + in_ref[which].astype(F32)
    total = total.astype(BF16)
    for which in range(in_ref.shape[0]):
        out_ref[which] = total


def spread_sum(tie, pieces):
    return call(spread_body, "spread_sum", [struct(pieces.shape, BF16)], (tie, pieces), 16, in_specs=[SM, VM], out_specs=[VM])[0]


GAIN_ROWS = 8


def spread_gain_body(tie_ref, in_ref, gain_ref, out_ref):
    count, rows, width = in_ref.shape
    total = in_ref[0].astype(F32)
    for which in range(1, count):
        total = total + in_ref[which].astype(F32)
    total = total.astype(BF16)
    gains = gain_ref[...]
    high = gains.astype(BF16)
    low = (gains - high.astype(F32)).astype(BF16)
    head = jnp.concatenate([high, low, jnp.zeros((GAIN_ROWS - 4, width), BF16)], axis=0)
    for which in range(count):
        out_ref[which, :GAIN_ROWS, :] = head
        out_ref[which, GAIN_ROWS:, :] = total


def spread_gain_sum(tie, pieces, gains):
    count, rows, width = pieces.shape
    return call(
        spread_gain_body,
        "spread_sum",
        [struct((count, rows + GAIN_ROWS, width), BF16)],
        (tie, pieces, gains),
        16,
        in_specs=[SM, VM, VM],
        out_specs=[VM],
    )[0]


def exchange(value):
    return lax.all_to_all(value, "dp", 0, 0)


def attn_out_body(meta_ref, own_ref, other_ref, late_ref, qkv_ref, wo_ref, gain_ref, hold, hold_early):
    bit = meta_ref[3]
    hold_early[bit] = own_ref[...]
    hold_early[1 - bit] = other_ref[...]
    early = hold_early[...].reshape(9 * HD, hold.shape[1])
    wo_ref[...] = early[: 3 * HD, :].astype(F32)
    count = late_ref.shape[0]
    rows = late_ref.shape[1] - GAIN_ROWS
    gains = None
    for which in range(count):
        head = late_ref[which, :GAIN_ROWS, :].astype(F32)
        gains = head if gains is None else gains + head
        hold[which * rows : (which + 1) * rows, :] = late_ref[which, GAIN_ROWS:, :].astype(F32)
    gain_ref[...] = gains[0:2] + gains[2:4]
    for part in range(3):
        at = part * HD
        parts = [early[3 * HD + at : 3 * HD + at + HD, :], early[6 * HD + at : 6 * HD + at + HD, :]]
        parts = [p.astype(F32) for p in parts] + [hold[at : at + HD, :]]
        qkv_ref[part] = jnp.concatenate(parts, axis=0).T


def attn_out(meta, own, other, late):
    width = own.shape[1]
    return call(
        attn_out_body,
        "attn_out",
        [struct((3, width, 3 * HD), F32), struct((3 * HD, width), F32), struct((2, width), F32)],
        (meta, own, other, late),
        20,
        in_specs=[SM, VM, VM, VM],
        out_specs=[VM, VM, VM],
        scratch_shapes=[pltpu.VMEM((3 * HD, width), F32), pltpu.VMEM((2,) + own.shape, BF16)],
    )


def add_home_body(meta_ref, in_ref, p0, p1, p23, p3, out_ref):
    slot = pl.program_id(0) ^ meta_ref[2]
    for which, piece in enumerate((p0, p1, p23.at[0], p3)):

        @pl.when(slot == which)
        def _():
            out_ref[0] = in_ref[0] + piece[...].astype(F32)


def add_home(meta, base, pieces):
    count, rows, width = base.shape
    block = pl.BlockSpec((1, rows, width), lambda i: (i, 0, 0))
    full = lambda a: pl.BlockSpec(a.shape, lambda i, n=a.ndim: (0,) * n)
    return call(
        add_home_body,
        "add_home",
        [struct(base.shape, F32)],
        (meta, base, *pieces),
        16,
        grid=(count,),
        in_specs=[SM, block] + [full(p) for p in pieces],
        out_specs=[block],
    )[0]


def tie(value, *after):
    return lax.optimization_barrier((value, *after))[0]


def local(n_dp, inputs, w_qkv, w_out, w_gate_up, w_down, gain_attn, gain_mlp, piece_starts, out_grad):
    width = inputs.shape[2]
    units = w_down.shape[0]
    here = lax.axis_index("tensor").astype(jnp.int32)
    row = lax.axis_index("dp").astype(jnp.int32)
    bit = row & 1
    bits = [(row >> s) & 1 for s in range(n_dp.bit_length() - 1)]
    mine = lax.dynamic_index_in_dim(piece_starts, here, 0, keepdims=False)[0]
    meta = jnp.concatenate([mine, jnp.stack([here, bits[0], bits[1]])])
    one = gain_attn[None]
    two = gain_mlp[None]
    cosine, sine = rope_tables(LEN, HD)
    tensor = functools.partial(swap, axis="tensor", size=4)
    dp = functools.partial(swap, axis="dp", size=n_dp)

    def picks(whole):
        return [lax.dynamic_index_in_dim(whole, here ^ k, 0, keepdims=False).astype(BF16) for k in range(4)]

    def around(pieces):
        return [pieces[0]] + [tensor(pieces[k], mask=k) for k in range(1, 4)]

    def homeward(own, core, far):
        received = tensor(far, mask=2)
        return own, tensor(core, mask=1), received, tensor(received[1], mask=1)

    def far(half):
        direct = tensor(half, mask=2)
        other = dp(direct, mask=1)
        return direct, other, tensor(direct, mask=1), tensor(other, mask=1)

    x_mine = picks(inputs)
    xs = around(x_mine)
    wa0 = jnp.concatenate([jnp.swapaxes(w_qkv, 1, 2), w_out[None]]).astype(BF16)
    wa1 = tensor(wa0, mask=1)
    wa_far = far(tie(lax.dynamic_slice_in_dim(wa0, 2 * bit, 2, 0), xs[1]))
    wm0 = jnp.concatenate([w_gate_up, w_down.T[None]]).astype(BF16)
    wm1 = tensor(wm0, mask=1)
    wm_far = far(lax.dynamic_slice_in_dim(wm0.reshape(3 * width, units), 3 * width // 2 * bit, 3 * width // 2, 0))
    gs = around(picks(out_grad))

    last = [meta]

    def run(kernel, first, *args, **kw):
        out = kernel(tie(first, last[0]), *args, **kw)
        last[0] = out[0] if isinstance(out, (list, tuple)) else out
        return out

    x, n1, qa, ka, va = run(project_first, meta, xs, one, wa0, wa1, cosine, sine)
    mta, ma, la = run(attend, meta, qa, ka, va)
    qb, kb, vb, wa2, wa3 = run(project_next, meta, n1, wa_far, cosine, sine)
    wa = (wa0, wa1, wa2, wa3)
    mtb, mb, lb = run(attend, meta, qb, kb, vb)
    after, n2, n2t, g, gt = run(after_attention, meta, x, ma, mb, wa, two, gs)
    acc_out, acc_back, dw1, dw0 = run(mlp, meta, n2, n2t, g, gt, ((wm1,), (wm0,)))
    in1 = tensor(dw1, mask=1)
    acc_out, acc_back, dw3, dw2 = run(mlp, meta, n2, n2t, g, gt, (wm_far[2:], wm_far[:2]), (acc_out, acc_back))
    in3 = tensor(dw3, mask=1)
    middle_out = run(middle, meta, x, after, acc_out, acc_back, g, two, (mta, mtb), wa)
    home = homeward(*middle_out[:3])
    da, do, even_o, odd_o, gain_two = middle_out[3:]
    in_o = tensor(odd_o, mask=1)
    keep_p, send_p, keep_q, send_q = run(start_sums, meta, dw0, in1, dw2, in3)
    recv_p = dp(send_p, mask=1)
    recv_q = dp(send_q, mask=2)
    sets = ((qa, ka, va, mta, la), (qb, kb, vb, mtb, lb))
    back = lambda turn: run(lambda m: attend_back(turn, m, cosine, sine, n1, sets, do), meta)
    dt0, even0, odd0 = back(0)
    in0 = tensor(odd0, mask=1)
    dt1, even1, odd1 = back(1)
    in1_ = tensor(odd1, mask=1)
    keep, send_p, send_q = run(second_sums, tie(meta, home[2]), keep_p, recv_p, keep_q, recv_q)
    recv_p = dp(send_p, mask=2)
    recv_q = dp(send_q, mask=1)
    early, early_send = run(core_sums, meta, (even_o, even0, even1), (in_o, in0, in1_))
    early_recv = tensor(early_send, mask=2)
    dt2, even2, odd2 = back(2)
    in2 = tensor(odd2, mask=1)
    keep, send = run(third_sums, tie(meta, home[3]), keep, recv_p, recv_q)
    pieces = tensor(send, mask=2)
    late, late_send = run(core_sums, meta, (even2,), (in2,))
    late_recv = tensor(late_send, mask=2)
    (before,) = run(lambda m: token_grad(m, (0, 1), (dt0, dt1), wa), meta)
    early, early_send = run(split_sums, bits[0], early, early_recv)
    early_recv = dp(early_send, mask=1)
    *grads, gain_one = run(lambda m: token_grad(m, (2,), (dt2,), wa, (before, x, da, g, one)), meta)
    for shift in range(2, len(bits)):
        keep, send = run(halve_sums, bits[shift], keep, pieces)
        pieces = dp(send, mask=1 << shift)
    late = run(plain_sum, meta, late, late_recv)
    late = exchange(late.reshape(n_dp, -1, width))
    grads = homeward(grads[0], grads[1], tie(grads[2], late_recv))
    early, early_send = run(split_sums, bits[1], early, early_recv)
    early_recv = dp(early_send, mask=2)
    outputs = run(add_home, meta, inputs, home)
    gains = jnp.concatenate([gain_one, gain_two])
    gains = gains + tensor(gains, mask=1)
    gains = gains + tensor(gains, mask=2)
    for shift in range(2, len(bits)):
        early, early_send = run(split_sums, bits[shift], early, early_recv)
        early_recv = dp(early_send, mask=1 << shift)
    piece = run(plain_sum, meta, keep, pieces)
    other = dp(piece, mask=1 << (len(bits) - 1))
    early = run(plain_sum, meta, early, early_recv)
    early_recv = dp(early, mask=1 << (len(bits) - 1))
    late = exchange(run(spread_gain_sum, meta, late, gains))
    for shift in reversed(range(2, len(bits))):
        piece = run(pair_join, bits[shift], piece, other)
        if shift > 2:
            other = dp(piece, mask=1 << (shift - 1))
    recv_p = dp(piece[0], mask=2)
    recv_q = dp(piece[1], mask=1)
    for shift in reversed(range(1, len(bits))):
        early = run(merge, bits[shift], early, early_recv)
        early_recv = dp(early, mask=1 << (shift - 1))
        if shift == 2:
            input_grad = run(add_home, meta, out_grad, grads)
            p, q = run(cross_join, meta, piece, recv_p, recv_q)
            recv_p = dp(p, mask=1)
            recv_q = dp(q, mask=2)
    grad_qkv, grad_out, gains = run(attn_out, meta, early, early_recv, late)
    grad_pair, grad_down = run(mlp_out, meta, p, recv_p, q, recv_q, width)
    return (
        outputs,
        input_grad,
        grad_qkv,
        grad_out,
        grad_pair.reshape(2, width, units),
        grad_down,
        gains[0],
        gains[1],
    )


def solution(mesh):
    rows = P(None, ("dp", "tensor"), None)
    weights = (P(None, None, "tensor"), P("tensor", None), P(None, None, "tensor"), P("tensor", None))
    return jax.shard_map(
        functools.partial(local, mesh.shape["dp"]),
        mesh=mesh,
        in_specs=(rows, *weights, P(), P(), P(None, "dp", None), rows),
        out_specs=(rows, rows, *weights, P(), P()),
        check_vma=False,
    )
```

```python
import functools
import jax
import jax.numpy as jnp
import numpy as np
from jax import lax
from jax.experimental import pallas as pl
from jax.experimental.pallas import tpu as pltpu
from jax.sharding import PartitionSpec as P

HD = 64
LEN = 1024
PIECE = 256
HALF = 512
EPS = 1e-06
F32 = jnp.float32
BF16 = jnp.bfloat16
MIB = 1024 * 1024


def nn(a, b):
    return lax.dot_general(a, b, (((1,), (0,)), ((), ())), preferred_element_type=F32)


def nt(a, b):
    return lax.dot_general(a, b, (((1,), (1,)), ((), ())), preferred_element_type=F32)


COST = {
    "project_first": 5,
    "project_next": 5,
    "attend": 10,
    "after_attention": 5,
    "mlp": 15,
    "middle": 3,
    "attend_back": 2,
    "token_grad": 0.5,
    "start_sums": 1,
    "add_home": 0.1,
    "mlp_out": 0.1,
}
RATE = 1e9


def call(body, name, out_shape, args, vmem, **kw):
    return pl.pallas_call(
        body,
        name=name,
        out_shape=out_shape,
        compiler_params=pltpu.CompilerParams(vmem_limit_bytes=vmem * MIB),
        cost_estimate=pl.CostEstimate(flops=int(COST.get(name, 0.3) * RATE), bytes_accessed=0, transcendentals=0),
        **kw,
    )(*args)


def struct(shape, dtype):
    return jax.ShapeDtypeStruct(shape, dtype)


def project(n1_ref, weights, cos_ref, sin_ref, q_ref, k_ref, v_ref):
    step = 256
    for block in range(LEN // step):
        cols = slice(block * step, (block + 1) * step)
        rows = n1_ref[cols, :]
        cosine = cos_ref[:, cols]
        sine = sin_ref[:, cols]
        for slot, w_ref in enumerate(weights):
            for part, ref in ((0, q_ref), (1, k_ref), (2, v_ref)):
                made = nt(w_ref[part], rows)
                for head in range(3):
                    low = made[head * HD : head * HD + HD // 2]
                    high = made[head * HD + HD // 2 : (head + 1) * HD]
                    if part < 2:
                        low, high = low * cosine - high * sine, high * cosine + low * sine
                    if part == 0:
                        low, high = low * HD**-0.5, high * HD**-0.5
                    at = slot * HD
                    ref[head, at : at + HD // 2, cols] = low.astype(BF16)
                    ref[head, at + HD // 2 : at + HD, cols] = high.astype(BF16)


def in_order(here, pieces, ref):
    step = ref.shape[0] // 4
    for quarter in range(4):
        for slot, piece in enumerate(pieces):

            @pl.when((here ^ slot) == quarter)
            def _():
                ref[quarter * step : (quarter + 1) * step, :] = piece[...]


def project_first_body(meta_ref, p0, p1, p2, p3, gain_ref, w0, w1, cos_ref, sin_ref, x_ref, n1_ref, q_ref, k_ref, v_ref):
    step = 256
    gain = gain_ref[...]
    in_order(meta_ref[2], (p0, p1, p2, p3), x_ref)
    for block in range(LEN // step):
        rows = slice(block * step, (block + 1) * step)
        x = x_ref[rows, :].astype(F32)
        scale = lax.rsqrt(jnp.mean(x * x, axis=-1, keepdims=True) + EPS)
        n1_ref[rows, :] = (x * scale * gain).astype(BF16)
    project(n1_ref, (w0, w1), cos_ref, sin_ref, q_ref, k_ref, v_ref)


def project_next_body(
    meta_ref, n1_ref, d2, r2, d3, r3, cos_ref, sin_ref, q_ref, k_ref, v_ref, w2_ref, w3_ref
):
    bit = meta_ref[3]
    for direct, other, ref in ((d2, r2, w2_ref), (d3, r3, w3_ref)):
        for part in range(2):
            ref[2 * bit + part] = direct[part]
            ref[2 * (1 - bit) + part] = other[part]
    project(n1_ref, (w2_ref, w3_ref), cos_ref, sin_ref, q_ref, k_ref, v_ref)


HEADS3 = (3, 2 * HD, LEN)


VM = pl.BlockSpec(memory_space=pltpu.VMEM)
SM = pl.BlockSpec(memory_space=pltpu.SMEM)


def project_first(meta, pieces, gain, w0, w1, cosine, sine):
    width = gain.shape[1]
    out = [struct((LEN, width), BF16)] * 2 + [struct(HEADS3, BF16)] * 3
    args = (meta, *pieces, gain, w0, w1, cosine, sine)
    return call(
        project_first_body,
        "project_first",
        out,
        args,
        10,
        in_specs=[SM] + [VM] * (len(args) - 1),
        out_specs=[VM] * len(out),
    )


def project_next(meta, n1, far, cosine, sine):
    out = [struct(HEADS3, BF16)] * 3 + [struct((4,) + far[0].shape[1:], BF16)] * 2
    args = (meta, n1, *far, cosine, sine)
    return call(
        project_next_body,
        "project_next",
        out,
        args,
        10,
        in_specs=[SM] + [VM] * (len(args) - 1),
        out_specs=[VM] * len(out),
    )


def limits(starts_ref):
    pos = lax.broadcasted_iota(jnp.int32, (1, LEN), 1)
    lim = pos
    for piece in range(2):
        first = starts_ref[piece]
        lim = jnp.where((pos >= first) & (pos < first + PIECE), first + PIECE - 1, lim)
    return lim


def one_head(block, head):
    zero = jnp.zeros((HD, block.shape[1]), block.dtype)
    part = block[head * HD : (head + 1) * HD]
    return jnp.concatenate([part, zero] if head == 0 else [zero, part], axis=0)


NEG = -1e30


def attend_body(qb, starts_ref, q_ref, k_ref, v_ref, mt_ref, m_ref, lse_ref):
    lim = limits(starts_ref)
    k_rows = k_ref[0].T
    for head in range(2):
        q_one = one_head(q_ref[0], head)
        v_one = v_ref[0, head * HD : (head + 1) * HD, :]
        for block in range(LEN // qb):
            cols = slice(block * qb, (block + 1) * qb)
            keys = HALF if (block + 1) * qb <= HALF else LEN
            scores = nn(k_rows[:keys], q_one[:, cols])
            edge = scores[keys - HALF :]
            pos = lax.broadcasted_iota(jnp.int32, (HALF, qb), 0) + (keys - HALF)
            edge = jnp.where(pos <= lim[:, cols], edge, NEG)
            most = jnp.max(edge, axis=0, keepdims=True)
            if keys > HALF:
                body = scores[:HALF]
                most = jnp.maximum(most, jnp.max(body, axis=0, keepdims=True))
            soft = jnp.exp(edge - most)
            total = jnp.sum(soft, axis=0, keepdims=True)
            mixed = nn(v_one[:, keys - HALF : keys], soft.astype(BF16))
            if keys > HALF:
                soft = jnp.exp(body - most)
                total = total + jnp.sum(soft, axis=0, keepdims=True)
                mixed = mixed + nn(v_one[:, :HALF], soft.astype(BF16))
            mt_ref[0, head * HD : (head + 1) * HD, cols] = (mixed * (1.0 / total)).astype(BF16)
            lse_ref[0, head : head + 1, cols] = most + jnp.log(total)
    m_ref[...] = mt_ref[0].T


def attend(starts, q, k, v, qb=512):
    block = pl.BlockSpec((1, 2 * HD, LEN), lambda i: (i, 0, 0))
    out = [struct(HEADS3, BF16), struct((LEN, 6 * HD), BF16), struct((3, 2, LEN), F32)]
    return call(
        functools.partial(attend_body, qb),
        "attend",
        out,
        (starts, q, k, v),
        10,
        grid=(3,),
        in_specs=[pl.BlockSpec(memory_space=pltpu.SMEM), block, block, block],
        out_specs=[
            block,
            pl.BlockSpec((LEN, 2 * HD), lambda i: (0, i)),
            pl.BlockSpec((1, 2, LEN), lambda i: (i, 0, 0)),
        ],
    )


def attend_back_body(qb, starts_ref, cos_ref, sin_ref, n1_ref, *refs):
    sets = (refs[0:5], refs[5:10])
    do_ref = refs[10]
    dt_ref, even_ref, odd_ref, acc_ref = refs[11:]
    lim = limits(starts_ref)
    for which, (q_ref, k_ref, v_ref, mt_ref, lse_ref) in enumerate(sets):
        q = q_ref[0]
        k = k_ref[0]
        v = v_ref[0]
        do = do_ref[which * 2 * HD : (which + 1) * 2 * HD, :]
        k_rows = k.T
        v_rows = v.T
        both = do.astype(F32) * mt_ref[0].astype(F32)
        for head in range(2):
            mine = slice(head * HD, (head + 1) * HD)
            inner = jnp.sum(both[mine], axis=0, keepdims=True)
            q_one = one_head(q, head)
            do_one = one_head(do, head)
            lse = lse_ref[0, head : head + 1, :]
            for block in range(LEN // qb):
                cols = slice(block * qb, (block + 1) * qb)
                wide = (block + 1) * qb > HALF
                dq = None
                for part in range(2 if wide else 1):
                    keys = slice(part * HALF, (part + 1) * HALF)
                    scores = nn(k_rows[keys], q_one[:, cols])
                    if part == (1 if wide else 0):
                        pos = lax.broadcasted_iota(jnp.int32, (HALF, qb), 0) + part * HALF
                        scores = jnp.where(pos <= lim[:, cols], scores, NEG)
                    soft = jnp.exp(scores - lse[:, cols])
                    grad = nn(v_rows[keys], do_one[:, cols])
                    grad = (soft * (grad - inner[:, cols])).astype(BF16)
                    more = nn(k[mine, keys], grad)
                    dq = more if dq is None else dq + more
                    dk = nt(q[mine, cols], grad)
                    dv = nt(do[mine, cols], soft.astype(BF16))
                    fresh = block == (0 if part == 0 else HALF // qb)
                    if fresh:
                        acc_ref[1, mine, keys] = dk
                        acc_ref[2, mine, keys] = dv
                    else:
                        acc_ref[1, mine, keys] += dk
                        acc_ref[2, mine, keys] += dv
                acc_ref[0, mine, cols] = dq * HD**-0.5
        cosine = cos_ref[...]
        sine = sin_ref[...]
        for part in range(3):
            for head in range(2):
                at = head * HD
                low = acc_ref[part, at : at + HD // 2, :]
                high = acc_ref[part, at + HD // 2 : at + HD, :]
                if part < 2:
                    low, high = low * cosine + high * sine, high * cosine - low * sine
                to = which * 2 * HD + at
                dt_ref[part, to : to + HD // 2, :] = low.astype(BF16)
                dt_ref[part, to + HD // 2 : to + HD, :] = high.astype(BF16)
    for part in range(3):
        made = nn(dt_ref[part], n1_ref[...])
        for slot in range(4):
            ref = odd_ref if slot % 2 else even_ref
            ref[slot // 2, part * HD : (part + 1) * HD, :] = made[slot * HD : (slot + 1) * HD].astype(BF16)


def attend_back(turn, starts, cosine, sine, n1, sets, do, qb=512):
    width = n1.shape[1]
    head = pl.BlockSpec((1, 2 * HD, LEN), lambda i: (turn, 0, 0))
    full = lambda a: pl.BlockSpec(a.shape, lambda i, n=a.ndim: (0,) * n)
    lse = pl.BlockSpec((1, 2, LEN), lambda i: (turn, 0, 0))
    args = (starts, cosine, sine, n1, *sets[0], *sets[1], do)
    out = [struct((3, 4 * HD, LEN), BF16)] + [struct((2, 3 * HD, width), BF16)] * 2
    return call(
        functools.partial(attend_back_body, qb),
        "attend_back",
        out,
        args,
        16,
        grid=(1,),
        in_specs=[pl.BlockSpec(memory_space=pltpu.SMEM), full(cosine), full(sine), full(n1)]
        + [head, head, head, head, lse] * 2
        + [pl.BlockSpec((4 * HD, LEN), lambda i: (turn, 0))],
        out_specs=[full(o) for o in out],
        scratch_shapes=[pltpu.VMEM((3, 2 * HD, LEN), F32)],
    )


def turn_rows(w_refs):
    return jnp.concatenate(
        [w[3, turn * HD : (turn + 1) * HD, :] for turn in range(3) for w in w_refs], axis=0
    )


def after_body(
    meta_ref, x_ref, ma_ref, mb_ref, w0, w1, w2, w3, gain_ref, g0, g1, g2, g3,
    after_ref, n2_ref, n2t_ref, g_ref, gt_ref,
):
    slot = pl.program_id(0) ^ meta_ref[2]
    for which, piece in enumerate((g0, g1, g2, g3)):

        @pl.when(slot == which)
        def _():
            g_ref[...] = piece[...]

    first = turn_rows((w0, w1))
    second = turn_rows((w2, w3))
    after = x_ref[...].astype(F32) + nn(ma_ref[...], first) + nn(mb_ref[...], second)
    after_ref[...] = after
    scale = lax.rsqrt(jnp.mean(after * after, axis=-1, keepdims=True) + EPS)
    normed = (after * scale * gain_ref[...]).astype(BF16)
    n2_ref[...] = normed
    n2t_ref[...] = normed.T
    gt_ref[...] = g_ref[...].T


def after_attention(meta, x, mixed_a, mixed_b, wo, gain, g):
    width = x.shape[1]
    step = 256
    rows = lambda n: pl.BlockSpec((step, n), lambda i: (i, 0))
    cols = pl.BlockSpec((width, step), lambda i: (0, i))
    full = lambda a: pl.BlockSpec(a.shape, lambda i, n=a.ndim: (0,) * n)
    args = (meta, x, mixed_a, mixed_b, *wo, gain, *g)
    out = [
        struct((LEN, width), F32),
        struct((LEN, width), BF16),
        struct((width, LEN), BF16),
        struct((LEN, width), BF16),
        struct((width, LEN), BF16),
    ]
    return call(
        after_body,
        "after_attention",
        out,
        args,
        12,
        grid=(LEN // step,),
        in_specs=[SM, rows(width), rows(6 * HD), rows(6 * HD)]
        + [full(w) for w in wo]
        + [full(gain)]
        + [full(p) for p in g],
        out_specs=[rows(width), rows(width), cols, rows(width), cols],
    )


def mlp_body(layout, first, meta_ref, n2_ref, n2t_ref, g_ref, gt_ref, *refs):
    block = 256
    refs = list(refs)
    sources = [[refs.pop(0) for _ in range(kind)] for kind in layout]
    if not first:
        out_in, back_in = refs.pop(0), refs.pop(0)
    out_ref, back_ref = refs.pop(0), refs.pop(0)
    made = [refs.pop(0) for _ in layout]
    hid, dga, dup = refs[:3]
    if first:
        out_ref[...] = jnp.zeros_like(out_ref)
        back_ref[...] = jnp.zeros_like(back_ref)
    else:
        out_ref[...] = out_in[...]
        back_ref[...] = back_in[...]
    width = n2_ref.shape[1]
    half = 3 * width // 2
    for source, dw_ref in zip(sources, made):
        if len(source) == 2:
            hold = refs[3]
            hold[meta_ref[3]] = source[0][...]
            hold[1 - meta_ref[3]] = source[1][...]

            def take(part, cols, hold=hold):
                if part == 0:
                    return hold[0, :width, cols]
                if part == 2:
                    return hold[1, half - width :, cols]
                return jnp.concatenate([hold[0, width:, cols], hold[1, : half - width, cols]], axis=0)
        else:

            def take(part, cols, hold=source[0]):
                return hold[part, :, cols]

        for part in range(2):
            cols = slice(part * block, (part + 1) * block)
            wg = take(0, cols)
            wu = take(1, cols)
            wl = take(2, cols)
            n2 = n2_ref[...]
            gate = nn(n2, wg)
            up = nn(n2, wu)
            grad = nn(g_ref[...], wl)
            sigma = 1.0 / (1.0 + jnp.exp(-gate))
            silu = gate * sigma
            hid[...] = (silu * up).astype(BF16)
            dup[...] = (grad * silu).astype(BF16)
            dga[...] = (grad * up * (sigma * (1.0 + gate * (1.0 - sigma)))).astype(BF16)
            out_ref[...] += nt(hid[...], wl)
            back_ref[...] += nt(dga[...], wg) + nt(dup[...], wu)
            dw_ref[0, :, cols] = nn(n2t_ref[...], dga[...]).astype(BF16)
            dw_ref[1, :, cols] = nn(n2t_ref[...], dup[...]).astype(BF16)
            dw_ref[2, :, cols] = nn(gt_ref[...], hid[...]).astype(BF16)


def mlp(meta, n2, n2t, g, gt, weights, before=()):
    width = n2.shape[1]
    units = 512
    layout = tuple(len(w) for w in weights)
    out = [struct((LEN, width), F32)] * 2 + [struct((3, width, units), BF16)] * len(weights)
    args = (meta, n2, n2t, g, gt, *[a for w in weights for a in w], *before)
    scratch = [pltpu.VMEM((LEN, 256), BF16)] * 3
    if 2 in layout:
        scratch.append(pltpu.VMEM((2, 3 * width // 2, units), BF16))
    aliases = {len(args) - 2: 0, len(args) - 1: 1} if before else {}
    return call(
        functools.partial(mlp_body, layout, not before),
        "mlp",
        out,
        args,
        24,
        in_specs=[SM] + [VM] * (len(args) - 1),
        out_specs=[VM] * len(out),
        scratch_shapes=scratch,
        input_output_aliases=aliases,
    )


def norm_back(grad, value, gain):
    scale = lax.rsqrt(jnp.mean(value * value, axis=-1, keepdims=True) + EPS)
    unit = value * scale
    gain_grad = jnp.sum(grad * unit, axis=0, keepdims=True)
    e = grad * gain
    return scale * (e - unit * jnp.mean(e * unit, axis=-1, keepdims=True)), gain_grad


def give(meta_ref, value, refs):
    slot = pl.program_id(0) ^ meta_ref[2]
    for which, ref in enumerate(refs[:2]):

        @pl.when(slot == which)
        def _():
            ref[...] = value

    for which in range(2):

        @pl.when(slot == 2 + which)
        def _():
            refs[2][which] = value


def middle_body(
    meta_ref, x_ref, after_ref, sum_ref, back_ref, g_ref, gain_ref, mta_ref, mtb_ref,
    w0, w1, w2, w3, e0, e1, e23, da_ref, do_ref, even_ref, odd_ref, gain_out, acc,
):
    step = pl.program_id(0)
    after = after_ref[...]
    delta = (after - x_ref[...].astype(F32) + sum_ref[...]).astype(BF16)
    give(meta_ref, delta, (e0, e1, e23))
    back, gain_grad = norm_back(back_ref[...], after, gain_ref[...])
    grad_after = g_ref[...].astype(F32) + back
    da_ref[...] = grad_after
    low = grad_after.astype(BF16)

    @pl.when(step == 0)
    def _():
        gain_out[...] = jnp.zeros_like(gain_out)
        acc[...] = jnp.zeros_like(acc)

    gain_out[...] += gain_grad
    weights = turn_rows((w0, w1, w2, w3))
    do_ref[...] = nt(weights, low).astype(BF16)
    for turn in range(3):
        for which, mt in enumerate((mta_ref, mtb_ref)):
            acc[turn, which] += nn(mt[turn], low)

    @pl.when(step == pl.num_programs(0) - 1)
    def _():
        for turn in range(3):
            for slot in range(4):
                at = (slot % 2) * HD
                ref = odd_ref if slot % 2 else even_ref
                ref[slot // 2, turn * HD : (turn + 1) * HD, :] = acc[turn, slot // 2, at : at + HD, :].astype(BF16)


def middle(meta, x, after, total, back, g, gain, mts, wo):
    width = x.shape[1]
    step = 256
    rows = pl.BlockSpec((step, width), lambda i: (i, 0))
    full = lambda a: pl.BlockSpec(a.shape, lambda i, n=a.ndim: (0,) * n)
    heads = pl.BlockSpec((3, 2 * HD, step), lambda i: (0, 0, i))
    args = (meta, x, after, total, back, g, gain, *mts, *wo)
    out = [struct((step, width), BF16)] * 2 + [
        struct((2, step, width), BF16),
        struct((LEN, width), F32),
        struct((12 * HD, LEN), BF16),
        struct((2, 3 * HD, width), BF16),
        struct((2, 3 * HD, width), BF16),
        struct((1, width), F32),
    ]
    return call(
        middle_body,
        "middle",
        out,
        args,
        14,
        grid=(LEN // step,),
        in_specs=[SM] + [rows] * 5 + [full(gain), heads, heads] + [full(w) for w in wo],
        out_specs=[full(o) for o in out[:3]]
        + [rows, pl.BlockSpec((12 * HD, step), lambda i: (0, i)), full(out[5]), full(out[6]), full(out[7])],
        scratch_shapes=[pltpu.VMEM((3, 2, 2 * HD, width), F32)],
    )


def token_grad_body(turns, last, meta_ref, *refs):
    dts = refs[: len(turns)]
    weights = refs[len(turns) : len(turns) + 4]
    rest = refs[len(turns) + 4 :]
    step = pl.program_id(0)
    total = None
    for turn, dt in zip(turns, dts):
        for part in range(3):
            w = jnp.concatenate([w[part, turn * HD : (turn + 1) * HD, :] for w in weights], axis=0)
            more = nn(dt[part].T, w)
            total = more if total is None else total + more
    if not last:
        rest[0][...] = total
        return
    before_ref, x_ref, da_ref, g_ref, gain_ref, e0, e1, e23, gain_out = rest
    total = total + before_ref[...]
    back, gain_grad = norm_back(total, x_ref[...].astype(F32), gain_ref[...])
    give(meta_ref, (da_ref[...] - g_ref[...].astype(F32) + back).astype(BF16), (e0, e1, e23))

    @pl.when(step == 0)
    def _():
        gain_out[...] = jnp.zeros_like(gain_out)

    gain_out[...] += gain_grad


def token_grad(meta, turns, dts, weights, rest=None):
    width = weights[0].shape[2]
    step = 256
    rows = pl.BlockSpec((step, width), lambda i: (i, 0))
    full = lambda a: pl.BlockSpec(a.shape, lambda i, n=a.ndim: (0,) * n)
    cols = pl.BlockSpec((3, 4 * HD, step), lambda i: (0, 0, i))
    specs = [SM] + [cols] * len(dts) + [full(w) for w in weights]
    args = (meta, *dts, *weights)
    if rest is None:
        out = [struct((LEN, width), F32)]
        out_specs = [rows]
    else:
        out = [struct((step, width), BF16)] * 2 + [struct((2, step, width), BF16), struct((1, width), F32)]
        out_specs = [full(o) for o in out]
        specs = specs + [rows] * 4 + [full(rest[4])]
        args = args + tuple(rest)
    return call(
        functools.partial(token_grad_body, turns, rest is not None),
        "token_grad",
        out,
        args,
        12,
        grid=(LEN // step,),
        in_specs=specs,
        out_specs=out_specs,
    )


def rope_tables(length, width):
    halfway = width // 2
    inverse = 10000.0 ** (-jnp.arange(halfway, dtype=F32) * 2.0 / width)
    angles = inverse[:, None] * jnp.arange(length, dtype=F32)[None, :]
    return jnp.cos(angles), jnp.sin(angles)


def swap(value, axis, size, mask):
    return lax.ppermute(value, axis, [(i, i ^ mask) for i in range(size)])


def added(*refs):
    total = refs[0].astype(F32)
    for ref in refs[1:]:
        total = total + ref.astype(F32)
    return total.astype(BF16)


def put(cond, ref, at, value):
    @pl.when(cond)
    def _():
        if at is None:
            ref[...] = value
        else:
            ref[at] = value


def start_body(meta_ref, a0, b0, a2, b2, keep_p, send_p, keep_q, send_q):
    step = pl.program_id(0)
    bit = meta_ref[3]
    two = meta_ref[4]
    for slot, (a, b) in enumerate(((a0, b0), (a2, b2))):
        value = added(a[0], b[0])
        put(step == bit, keep_p, slot, value)
        put(step == 1 - bit, send_p, slot, value)
        put(step == 2 + two, keep_q, slot, value)
        put(step == 3 - two, send_q, slot, value)


def start_sums(meta, dw0, in1, dw2, in3):
    rows = dw0.shape[0] * dw0.shape[1] // 4
    cols = dw0.shape[2]
    parts = [a.reshape(4, rows, cols) for a in (dw0, in1, dw2, in3)]
    out = [struct((2, rows, cols), BF16)] * 4
    return call(
        start_body,
        "start_sums",
        out,
        (meta, *parts),
        16,
        grid=(4,),
        in_specs=[SM] + [pl.BlockSpec((1, rows, cols), lambda i: (i, 0, 0))] * 4,
        out_specs=[pl.BlockSpec((2, rows, cols), lambda i: (0, 0, 0))] * 4,
    )


def second_body(meta_ref, kp, rp, kq, rq, keep, send_p, send_q):
    step = pl.program_id(0)
    for which, (k, r, send, bit) in enumerate(((kp, rp, send_p, meta_ref[4]), (kq, rq, send_q, meta_ref[3]))):
        for slot in range(2):
            value = added(k[slot, 0], r[slot, 0])
            put(step == bit, keep, (which, slot), value)
            put(step == 1 - bit, send, slot, value)


def second_sums(meta, *pieces):
    _, rows, cols = pieces[0].shape
    half = rows // 2
    full = lambda n: pl.BlockSpec((2,) * n + (half, cols), lambda i: (0,) * (n + 2))
    return call(
        second_body,
        "second_sums",
        [struct((2, 2, half, cols), BF16)] + [struct((2, half, cols), BF16)] * 2,
        (meta, *[p.reshape(2, 2, half, cols) for p in pieces]),
        20,
        grid=(2,),
        in_specs=[SM] + [pl.BlockSpec((2, 1, half, cols), lambda i: (0, i, 0, 0))] * 4,
        out_specs=[full(2), full(1), full(1)],
    )


def third_body(meta_ref, a, bp, bq, keep, send):
    which = pl.program_id(0)
    for part, b in enumerate((bp, bq)):

        @pl.when(which == part)
        def _():
            keep[0] = added(a[0, 0], b[0])
            send[0] = added(a[0, 1], b[1])


def third_sums(meta, a, bp, bq):
    _, _, rows, cols = a.shape
    whole = pl.BlockSpec((2, rows, cols), lambda i: (0, 0, 0))
    block = pl.BlockSpec((1, rows, cols), lambda i: (i, 0, 0))
    return call(
        third_body,
        "third_sums",
        [struct((2, rows, cols), BF16)] * 2,
        (meta, a, bp, bq),
        12,
        grid=(2,),
        in_specs=[SM, pl.BlockSpec((1, 2, rows, cols), lambda i: (i, 0, 0, 0)), whole, whole],
        out_specs=[block, block],
    )


def halve_body(bit_ref, a, b, keep, send):
    bit = bit_ref[0]
    step = pl.program_id(0)
    for which in range(2):
        value = added(a[which, 0], b[which, 0])
        put(step == bit, keep, which, value)
        put(step != bit, send, which, value)


def halve_sums(bit, a, b):
    _, rows, cols = a.shape
    half = rows // 2
    return call(
        halve_body,
        "halve_sums",
        [struct((2, half, cols), BF16)] * 2,
        (bit.reshape(1), a.reshape(2, 2, half, cols), b.reshape(2, 2, half, cols)),
        12,
        grid=(2,),
        in_specs=[SM] + [pl.BlockSpec((2, 1, half, cols), lambda i: (0, i, 0, 0))] * 2,
        out_specs=[pl.BlockSpec((2, half, cols), lambda i: (0, 0, 0))] * 2,
    )


def plain_body(tie_ref, a, b, out):
    out[...] = added(a[...], b[...])


def plain_sum(tie, a, b):
    return call(plain_body, "plain_sum", [struct(a.shape, BF16)], (tie, a, b), 12, in_specs=[SM, VM, VM], out_specs=[VM])[0]


def split_body(bit_ref, a, b, keep, send):
    bit = bit_ref[0]
    step = pl.program_id(0)
    value = added(a[0], b[0])
    put(step == bit, keep, None, value)
    put(step != bit, send, None, value)


def split_sums(bit, a, b):
    rows, cols = a.shape
    half = rows // 2
    return call(
        split_body,
        "split_sums",
        [struct((half, cols), BF16)] * 2,
        (bit.reshape(1), a.reshape(2, half, cols), b.reshape(2, half, cols)),
        12,
        grid=(2,),
        in_specs=[SM] + [pl.BlockSpec((1, half, cols), lambda i: (i, 0, 0))] * 2,
        out_specs=[pl.BlockSpec((half, cols), lambda i: (0, 0))] * 2,
    )


def merge_body(bit_ref, a, b, out):
    bit = bit_ref[0]
    out[bit] = a[...]
    out[1 - bit] = b[...]


def merge(bit, a, b):
    rows, cols = a.shape
    made = call(
        merge_body,
        "merge",
        [struct((2, rows, cols), BF16)],
        (bit.reshape(1), a, b),
        12,
        in_specs=[SM, VM, VM],
        out_specs=[VM],
    )[0]
    return made.reshape(2 * rows, cols)


def pair_body(bit_ref, a, b, out):
    bit = bit_ref[0]
    for which in range(2):
        out[which, bit] = a[which]
        out[which, 1 - bit] = b[which]


def pair_join(bit, a, b):
    _, rows, cols = a.shape
    made = call(
        pair_body,
        "pair_join",
        [struct((2, 2, rows, cols), BF16)],
        (bit.reshape(1), a, b),
        12,
        in_specs=[SM, VM, VM],
        out_specs=[VM],
    )[0]
    return made.reshape(2, 2 * rows, cols)


def cross_body(meta_ref, a, bp, bq, out_p, out_q):
    two = meta_ref[4]
    bit = meta_ref[3]
    out_p[two] = a[0]
    out_p[1 - two] = bp[...]
    out_q[bit] = a[1]
    out_q[1 - bit] = bq[...]


def cross_join(meta, a, bp, bq):
    _, rows, cols = a.shape
    made = call(
        cross_body,
        "cross_join",
        [struct((2, rows, cols), BF16)] * 2,
        (meta, a, bp, bq),
        12,
        in_specs=[SM, VM, VM, VM],
        out_specs=[VM, VM],
    )
    return [m.reshape(2 * rows, cols) for m in made]


def mlp_out_body(meta_ref, p, rp, q, rq, gu_ref, wd_ref, hold):
    bit = meta_ref[3]
    two = meta_ref[4]
    hold[bit] = p[...]
    hold[1 - bit] = rp[...]
    hold[2 + two] = q[...]
    hold[3 - two] = rq[...]
    rows = hold.shape[1]
    pair = gu_ref.shape[0]
    for which in range(2):
        gu_ref[which * rows : (which + 1) * rows, :] = hold[which].astype(F32)
    rest = pair - 2 * rows
    gu_ref[2 * rows :, :] = hold[2, :rest, :].astype(F32)
    wd_ref[:, : rows - rest] = hold[2, rest:, :].astype(F32).T
    wd_ref[:, rows - rest :] = hold[3].astype(F32).T


def mlp_out(meta, p, rp, q, rq, width):
    rows, units = p.shape
    return call(
        mlp_out_body,
        "mlp_out",
        [struct((2 * width, units), F32), struct((units, width), F32)],
        (meta, p, rp, q, rq),
        24,
        in_specs=[SM] + [VM] * 4,
        out_specs=[VM] * 2,
        scratch_shapes=[pltpu.VMEM((4, rows, units), BF16)],
    )


def core_body(count, meta_ref, *refs):
    evens, ins = refs[:count], refs[count : 2 * count]
    keep, send = refs[2 * count :]
    rows = evens[0].shape[1]
    for which, (a, b) in enumerate(zip(evens, ins)):
        keep[which * rows : (which + 1) * rows, :] = added(a[0], b[0])
        send[which * rows : (which + 1) * rows, :] = added(a[1], b[1])


def core_sums(meta, evens, ins):
    count = len(evens)
    _, rows, cols = evens[0].shape
    args = (meta, *evens, *ins)
    return call(
        functools.partial(core_body, count),
        "core_sums",
        [struct((count * rows, cols), BF16)] * 2,
        args,
        16,
        in_specs=[SM] + [VM] * (2 * count),
        out_specs=[VM] * 2,
    )


def spread_body(tie_ref, in_ref, out_ref):
    total = in_ref[0].astype(F32)
    for which in range(1, in_ref.shape[0]):
        total = total + in_ref[which].astype(F32)
    total = total.astype(BF16)
    for which in range(in_ref.shape[0]):
        out_ref[which] = total


def spread_sum(tie, pieces):
    return call(spread_body, "spread_sum", [struct(pieces.shape, BF16)], (tie, pieces), 16, in_specs=[SM, VM], out_specs=[VM])[0]


GAIN_ROWS = 8


def spread_gain_body(tie_ref, in_ref, gain_ref, out_ref):
    count, rows, width = in_ref.shape
    total = in_ref[0].astype(F32)
    for which in range(1, count):
        total = total + in_ref[which].astype(F32)
    total = total.astype(BF16)
    gains = gain_ref[...]
    high = gains.astype(BF16)
    low = (gains - high.astype(F32)).astype(BF16)
    head = jnp.concatenate([high, low, jnp.zeros((GAIN_ROWS - 4, width), BF16)], axis=0)
    for which in range(count):
        out_ref[which, :GAIN_ROWS, :] = head
        out_ref[which, GAIN_ROWS:, :] = total


def spread_gain_sum(tie, pieces, gains):
    count, rows, width = pieces.shape
    return call(
        spread_gain_body,
        "spread_sum",
        [struct((count, rows + GAIN_ROWS, width), BF16)],
        (tie, pieces, gains),
        16,
        in_specs=[SM, VM, VM],
        out_specs=[VM],
    )[0]


def exchange(value):
    return lax.all_to_all(value, "dp", 0, 0)


def attn_out_body(meta_ref, own_ref, other_ref, late_ref, qkv_ref, wo_ref, gain_ref, hold, hold_early):
    bit = meta_ref[3]
    hold_early[bit] = own_ref[...]
    hold_early[1 - bit] = other_ref[...]
    early = hold_early[...].reshape(9 * HD, hold.shape[1])
    wo_ref[...] = early[: 3 * HD, :].astype(F32)
    count = late_ref.shape[0]
    rows = late_ref.shape[1] - GAIN_ROWS
    gains = None
    for which in range(count):
        head = late_ref[which, :GAIN_ROWS, :].astype(F32)
        gains = head if gains is None else gains + head
        hold[which * rows : (which + 1) * rows, :] = late_ref[which, GAIN_ROWS:, :].astype(F32)
    gain_ref[...] = gains[0:2] + gains[2:4]
    for part in range(3):
        at = part * HD
        parts = [early[3 * HD + at : 3 * HD + at + HD, :], early[6 * HD + at : 6 * HD + at + HD, :]]
        parts = [p.astype(F32) for p in parts] + [hold[at : at + HD, :]]
        qkv_ref[part] = jnp.concatenate(parts, axis=0).T


def attn_out(meta, own, other, late):
    width = own.shape[1]
    return call(
        attn_out_body,
        "attn_out",
        [struct((3, width, 3 * HD), F32), struct((3 * HD, width), F32), struct((2, width), F32)],
        (meta, own, other, late),
        20,
        in_specs=[SM, VM, VM, VM],
        out_specs=[VM, VM, VM],
        scratch_shapes=[pltpu.VMEM((3 * HD, width), F32), pltpu.VMEM((2,) + own.shape, BF16)],
    )


def add_home_body(meta_ref, in_ref, p0, p1, p23, p3, out_ref):
    slot = pl.program_id(0) ^ meta_ref[2]
    for which, piece in enumerate((p0, p1, p23.at[0], p3)):

        @pl.when(slot == which)
        def _():
            out_ref[0] = in_ref[0] + piece[...].astype(F32)


def add_home(meta, base, pieces):
    count, rows, width = base.shape
    block = pl.BlockSpec((1, rows, width), lambda i: (i, 0, 0))
    full = lambda a: pl.BlockSpec(a.shape, lambda i, n=a.ndim: (0,) * n)
    return call(
        add_home_body,
        "add_home",
        [struct(base.shape, F32)],
        (meta, base, *pieces),
        16,
        grid=(count,),
        in_specs=[SM, block] + [full(p) for p in pieces],
        out_specs=[block],
    )[0]


def tie(value, *after):
    return lax.optimization_barrier((value, *after))[0]


def local(n_dp, inputs, w_qkv, w_out, w_gate_up, w_down, gain_attn, gain_mlp, piece_starts, out_grad):
    width = inputs.shape[2]
    units = w_down.shape[0]
    here = lax.axis_index("tensor").astype(jnp.int32)
    row = lax.axis_index("dp").astype(jnp.int32)
    bit = row & 1
    bits = [(row >> s) & 1 for s in range(n_dp.bit_length() - 1)]
    mine = lax.dynamic_index_in_dim(piece_starts, here, 0, keepdims=False)[0]
    meta = jnp.concatenate([mine, jnp.stack([here, bits[0], bits[1]])])
    one = gain_attn[None]
    two = gain_mlp[None]
    cosine, sine = rope_tables(LEN, HD)
    tensor = functools.partial(swap, axis="tensor", size=4)
    dp = functools.partial(swap, axis="dp", size=n_dp)

    def picks(whole):
        return [lax.dynamic_index_in_dim(whole, here ^ k, 0, keepdims=False).astype(BF16) for k in range(4)]

    def around(pieces):
        return [pieces[0]] + [tensor(pieces[k], mask=k) for k in range(1, 4)]

    def homeward(own, core, far):
        received = tensor(far, mask=2)
        return own, tensor(core, mask=1), received, tensor(received[1], mask=1)

    def far(half):
        direct = tensor(half, mask=2)
        other = dp(direct, mask=1)
        return direct, other, tensor(direct, mask=1), tensor(other, mask=1)

    x_mine = picks(inputs)
    xs = around(x_mine)
    wa0 = jnp.concatenate([jnp.swapaxes(w_qkv, 1, 2), w_out[None]]).astype(BF16)
    wa1 = tensor(wa0, mask=1)
    wa_far = far(tie(lax.dynamic_slice_in_dim(wa0, 2 * bit, 2, 0), xs[1]))
    wm0 = jnp.concatenate([w_gate_up, w_down.T[None]]).astype(BF16)
    wm1 = tensor(wm0, mask=1)
    wm_far = far(lax.dynamic_slice_in_dim(wm0.reshape(3 * width, units), 3 * width // 2 * bit, 3 * width // 2, 0))
    gs = around(picks(out_grad))

    last = [meta]

    def run(kernel, first, *args, **kw):
        out = kernel(tie(first, last[0]), *args, **kw)
        last[0] = out[0] if isinstance(out, (list, tuple)) else out
        return out

    x, n1, qa, ka, va = run(project_first, meta, xs, one, wa0, wa1, cosine, sine)
    mta, ma, la = run(attend, meta, qa, ka, va)
    qb, kb, vb, wa2, wa3 = run(project_next, meta, n1, wa_far, cosine, sine)
    wa = (wa0, wa1, wa2, wa3)
    mtb, mb, lb = run(attend, meta, qb, kb, vb)
    after, n2, n2t, g, gt = run(after_attention, meta, x, ma, mb, wa, two, gs)
    acc_out, acc_back, dw1, dw0 = run(mlp, meta, n2, n2t, g, gt, ((wm1,), (wm0,)))
    in1 = tensor(dw1, mask=1)
    acc_out, acc_back, dw3, dw2 = run(mlp, meta, n2, n2t, g, gt, (wm_far[2:], wm_far[:2]), (acc_out, acc_back))
    in3 = tensor(dw3, mask=1)
    middle_out = run(middle, meta, x, after, acc_out, acc_back, g, two, (mta, mtb), wa)
    home = homeward(*middle_out[:3])
    da, do, even_o, odd_o, gain_two = middle_out[3:]
    in_o = tensor(odd_o, mask=1)
    keep_p, send_p, keep_q, send_q = run(start_sums, meta, dw0, in1, dw2, in3)
    recv_p = dp(send_p, mask=1)
    recv_q = dp(send_q, mask=2)
    sets = ((qa, ka, va, mta, la), (qb, kb, vb, mtb, lb))
    back = lambda turn: run(lambda m: attend_back(turn, m, cosine, sine, n1, sets, do), meta)
    dt0, even0, odd0 = back(0)
    in0 = tensor(odd0, mask=1)
    dt1, even1, odd1 = back(1)
    in1_ = tensor(odd1, mask=1)
    keep, send_p, send_q = run(second_sums, tie(meta, home[2]), keep_p, recv_p, keep_q, recv_q)
    recv_p = dp(send_p, mask=2)
    recv_q = dp(send_q, mask=1)
    early, early_send = run(core_sums, meta, (even_o, even0, even1), (in_o, in0, in1_))
    early_recv = tensor(early_send, mask=2)
    dt2, even2, odd2 = back(2)
    in2 = tensor(odd2, mask=1)
    keep, send = run(third_sums, tie(meta, home[3]), keep, recv_p, recv_q)
    pieces = tensor(send, mask=2)
    late, late_send = run(core_sums, meta, (even2,), (in2,))
    late_recv = tensor(late_send, mask=2)
    (before,) = run(lambda m: token_grad(m, (0, 1), (dt0, dt1), wa), meta)
    early, early_send = run(split_sums, bits[0], early, early_recv)
    early_recv = dp(early_send, mask=1)
    *grads, gain_one = run(lambda m: token_grad(m, (2,), (dt2,), wa, (before, x, da, g, one)), meta)
    for shift in range(2, len(bits)):
        keep, send = run(halve_sums, bits[shift], keep, pieces)
        pieces = dp(send, mask=1 << shift)
    late = run(plain_sum, meta, late, late_recv)
    late = exchange(late.reshape(n_dp, -1, width))
    grads = homeward(grads[0], grads[1], tie(grads[2], late_recv))
    early, early_send = run(split_sums, bits[1], early, early_recv)
    early_recv = dp(early_send, mask=2)
    gains = jnp.concatenate([gain_one, gain_two])
    gains = gains + tensor(gains, mask=1)
    gains = gains + tensor(gains, mask=2)
    for shift in range(2, len(bits)):
        early, early_send = run(split_sums, bits[shift], early, early_recv)
        early_recv = dp(early_send, mask=1 << shift)
    piece = run(plain_sum, meta, keep, pieces)
    other = dp(piece, mask=1 << (len(bits) - 1))
    early = run(plain_sum, meta, early, early_recv)
    early_recv = dp(early, mask=1 << (len(bits) - 1))
    late = exchange(run(spread_gain_sum, meta, late, gains))
    for shift in reversed(range(2, len(bits))):
        piece = run(pair_join, bits[shift], piece, other)
        if shift > 2:
            other = dp(piece, mask=1 << (shift - 1))
    recv_p = dp(piece[0], mask=2)
    recv_q = dp(piece[1], mask=1)
    for shift in reversed(range(2, len(bits))):
        early = run(merge, bits[shift], early, early_recv)
        early_recv = dp(early, mask=1 << (shift - 1))
    early = run(merge, bits[1], early, early_recv)
    early_recv = dp(early, mask=1)
    p, q = run(cross_join, meta, piece, recv_p, recv_q)
    recv_p = dp(p, mask=1)
    recv_q = dp(q, mask=2)
    outputs = run(add_home, meta, inputs, home)
    input_grad = run(add_home, meta, out_grad, grads)
    grad_qkv, grad_out, gains = run(attn_out, meta, early, early_recv, late)
    grad_pair, grad_down = run(mlp_out, meta, p, recv_p, q, recv_q, width)
    return (
        outputs,
        input_grad,
        grad_qkv,
        grad_out,
        grad_pair.reshape(2, width, units),
        grad_down,
        gains[0],
        gains[1],
    )


def solution(mesh):
    rows = P(None, ("dp", "tensor"), None)
    weights = (P(None, None, "tensor"), P("tensor", None), P(None, None, "tensor"), P("tensor", None))
    return jax.shard_map(
        functools.partial(local, mesh.shape["dp"]),
        mesh=mesh,
        in_specs=(rows, *weights, P(), P(), P(None, "dp", None), rows),
        out_specs=(rows, rows, *weights, P(), P()),
        check_vma=False,
    )
```

```python
import functools
import jax
import jax.numpy as jnp
import numpy as np
from jax import lax
from jax.experimental import pallas as pl
from jax.experimental.pallas import tpu as pltpu
from jax.sharding import PartitionSpec as P

HD = 64
LEN = 1024
PIECE = 256
HALF = 512
EPS = 1e-06
F32 = jnp.float32
BF16 = jnp.bfloat16
MIB = 1024 * 1024


def nn(a, b):
    return lax.dot_general(a, b, (((1,), (0,)), ((), ())), preferred_element_type=F32)


def nt(a, b):
    return lax.dot_general(a, b, (((1,), (1,)), ((), ())), preferred_element_type=F32)


COST = {
    "project_first": 5,
    "project_next": 5,
    "attend": 10,
    "after_attention": 5,
    "mlp": 15,
    "middle": 3,
    "attend_back": 2,
    "token_grad": 0.5,
    "start_sums": 1,
    "add_home": 0.1,
    "mlp_out": 0.1,
}
RATE = 1e9


def call(body, name, out_shape, args, vmem, **kw):
    return pl.pallas_call(
        body,
        name=name,
        out_shape=out_shape,
        compiler_params=pltpu.CompilerParams(vmem_limit_bytes=vmem * MIB),
        cost_estimate=pl.CostEstimate(flops=int(COST.get(name, 0.3) * RATE), bytes_accessed=0, transcendentals=0),
        **kw,
    )(*args)


def struct(shape, dtype):
    return jax.ShapeDtypeStruct(shape, dtype)


def project(n1_ref, weights, cos_ref, sin_ref, q_ref, k_ref, v_ref):
    step = 256
    for block in range(LEN // step):
        cols = slice(block * step, (block + 1) * step)
        rows = n1_ref[cols, :]
        cosine = cos_ref[:, cols]
        sine = sin_ref[:, cols]
        for slot, w_ref in enumerate(weights):
            for part, ref in ((0, q_ref), (1, k_ref), (2, v_ref)):
                made = nt(w_ref[part], rows)
                for head in range(3):
                    low = made[head * HD : head * HD + HD // 2]
                    high = made[head * HD + HD // 2 : (head + 1) * HD]
                    if part < 2:
                        low, high = low * cosine - high * sine, high * cosine + low * sine
                    if part == 0:
                        low, high = low * HD**-0.5, high * HD**-0.5
                    at = slot * HD
                    ref[head, at : at + HD // 2, cols] = low.astype(BF16)
                    ref[head, at + HD // 2 : at + HD, cols] = high.astype(BF16)


def in_order(here, pieces, ref):
    step = ref.shape[0] // 4
    for quarter in range(4):
        for slot, piece in enumerate(pieces):

            @pl.when((here ^ slot) == quarter)
            def _():
                ref[quarter * step : (quarter + 1) * step, :] = piece[...]


def project_first_body(meta_ref, p0, p1, p2, p3, gain_ref, w0, w1, cos_ref, sin_ref, x_ref, n1_ref, q_ref, k_ref, v_ref):
    step = 256
    gain = gain_ref[...]
    in_order(meta_ref[2], (p0, p1, p2, p3), x_ref)
    for block in range(LEN // step):
        rows = slice(block * step, (block + 1) * step)
        x = x_ref[rows, :].astype(F32)
        scale = lax.rsqrt(jnp.mean(x * x, axis=-1, keepdims=True) + EPS)
        n1_ref[rows, :] = (x * scale * gain).astype(BF16)
    project(n1_ref, (w0, w1), cos_ref, sin_ref, q_ref, k_ref, v_ref)


def project_next_body(
    meta_ref, n1_ref, d2, r2, d3, r3, cos_ref, sin_ref, q_ref, k_ref, v_ref, w2_ref, w3_ref
):
    bit = meta_ref[3]
    for direct, other, ref in ((d2, r2, w2_ref), (d3, r3, w3_ref)):
        for part in range(2):
            ref[2 * bit + part] = direct[part]
            ref[2 * (1 - bit) + part] = other[part]
    project(n1_ref, (w2_ref, w3_ref), cos_ref, sin_ref, q_ref, k_ref, v_ref)


HEADS3 = (3, 2 * HD, LEN)


VM = pl.BlockSpec(memory_space=pltpu.VMEM)
SM = pl.BlockSpec(memory_space=pltpu.SMEM)


def project_first(meta, pieces, gain, w0, w1, cosine, sine):
    width = gain.shape[1]
    out = [struct((LEN, width), BF16)] * 2 + [struct(HEADS3, BF16)] * 3
    args = (meta, *pieces, gain, w0, w1, cosine, sine)
    return call(
        project_first_body,
        "project_first",
        out,
        args,
        10,
        in_specs=[SM] + [VM] * (len(args) - 1),
        out_specs=[VM] * len(out),
    )


def project_next(meta, n1, far, cosine, sine):
    out = [struct(HEADS3, BF16)] * 3 + [struct((4,) + far[0].shape[1:], BF16)] * 2
    args = (meta, n1, *far, cosine, sine)
    return call(
        project_next_body,
        "project_next",
        out,
        args,
        10,
        in_specs=[SM] + [VM] * (len(args) - 1),
        out_specs=[VM] * len(out),
    )


def limits(starts_ref):
    pos = lax.broadcasted_iota(jnp.int32, (1, LEN), 1)
    lim = pos
    for piece in range(2):
        first = starts_ref[piece]
        lim = jnp.where((pos >= first) & (pos < first + PIECE), first + PIECE - 1, lim)
    return lim


def one_head(block, head):
    zero = jnp.zeros((HD, block.shape[1]), block.dtype)
    part = block[head * HD : (head + 1) * HD]
    return jnp.concatenate([part, zero] if head == 0 else [zero, part], axis=0)


NEG = -1e30


def attend_body(qb, starts_ref, q_ref, k_ref, v_ref, mt_ref, m_ref, lse_ref):
    lim = limits(starts_ref)
    k_rows = k_ref[0].T
    for head in range(2):
        q_one = one_head(q_ref[0], head)
        v_one = v_ref[0, head * HD : (head + 1) * HD, :]
        for block in range(LEN // qb):
            cols = slice(block * qb, (block + 1) * qb)
            keys = HALF if (block + 1) * qb <= HALF else LEN
            scores = nn(k_rows[:keys], q_one[:, cols])
            edge = scores[keys - HALF :]
            pos = lax.broadcasted_iota(jnp.int32, (HALF, qb), 0) + (keys - HALF)
            edge = jnp.where(pos <= lim[:, cols], edge, NEG)
            most = jnp.max(edge, axis=0, keepdims=True)
            if keys > HALF:
                body = scores[:HALF]
                most = jnp.maximum(most, jnp.max(body, axis=0, keepdims=True))
            soft = jnp.exp(edge - most)
            total = jnp.sum(soft, axis=0, keepdims=True)
            mixed = nn(v_one[:, keys - HALF : keys], soft.astype(BF16))
            if keys > HALF:
                soft = jnp.exp(body - most)
                total = total + jnp.sum(soft, axis=0, keepdims=True)
                mixed = mixed + nn(v_one[:, :HALF], soft.astype(BF16))
            mt_ref[0, head * HD : (head + 1) * HD, cols] = (mixed * (1.0 / total)).astype(BF16)
            lse_ref[0, head : head + 1, cols] = most + jnp.log(total)
    m_ref[...] = mt_ref[0].T


def attend(starts, q, k, v, qb=512):
    block = pl.BlockSpec((1, 2 * HD, LEN), lambda i: (i, 0, 0))
    out = [struct(HEADS3, BF16), struct((LEN, 6 * HD), BF16), struct((3, 2, LEN), F32)]
    return call(
        functools.partial(attend_body, qb),
        "attend",
        out,
        (starts, q, k, v),
        10,
        grid=(3,),
        in_specs=[pl.BlockSpec(memory_space=pltpu.SMEM), block, block, block],
        out_specs=[
            block,
            pl.BlockSpec((LEN, 2 * HD), lambda i: (0, i)),
            pl.BlockSpec((1, 2, LEN), lambda i: (i, 0, 0)),
        ],
    )


def attend_back_body(qb, starts_ref, cos_ref, sin_ref, n1_ref, *refs):
    sets = (refs[0:5], refs[5:10])
    do_ref = refs[10]
    dt_ref, even_ref, odd_ref, acc_ref = refs[11:]
    lim = limits(starts_ref)
    for which, (q_ref, k_ref, v_ref, mt_ref, lse_ref) in enumerate(sets):
        q = q_ref[0]
        k = k_ref[0]
        v = v_ref[0]
        do = do_ref[which * 2 * HD : (which + 1) * 2 * HD, :]
        k_rows = k.T
        v_rows = v.T
        both = do.astype(F32) * mt_ref[0].astype(F32)
        for head in range(2):
            mine = slice(head * HD, (head + 1) * HD)
            inner = jnp.sum(both[mine], axis=0, keepdims=True)
            q_one = one_head(q, head)
            do_one = one_head(do, head)
            lse = lse_ref[0, head : head + 1, :]
            for block in range(LEN // qb):
                cols = slice(block * qb, (block + 1) * qb)
                wide = (block + 1) * qb > HALF
                dq = None
                for part in range(2 if wide else 1):
                    keys = slice(part * HALF, (part + 1) * HALF)
                    scores = nn(k_rows[keys], q_one[:, cols])
                    if part == (1 if wide else 0):
                        pos = lax.broadcasted_iota(jnp.int32, (HALF, qb), 0) + part * HALF
                        scores = jnp.where(pos <= lim[:, cols], scores, NEG)
                    soft = jnp.exp(scores - lse[:, cols])
                    grad = nn(v_rows[keys], do_one[:, cols])
                    grad = (soft * (grad - inner[:, cols])).astype(BF16)
                    more = nn(k[mine, keys], grad)
                    dq = more if dq is None else dq + more
                    dk = nt(q[mine, cols], grad)
                    dv = nt(do[mine, cols], soft.astype(BF16))
                    fresh = block == (0 if part == 0 else HALF // qb)
                    if fresh:
                        acc_ref[1, mine, keys] = dk
                        acc_ref[2, mine, keys] = dv
                    else:
                        acc_ref[1, mine, keys] += dk
                        acc_ref[2, mine, keys] += dv
                acc_ref[0, mine, cols] = dq * HD**-0.5
        cosine = cos_ref[...]
        sine = sin_ref[...]
        for part in range(3):
            for head in range(2):
                at = head * HD
                low = acc_ref[part, at : at + HD // 2, :]
                high = acc_ref[part, at + HD // 2 : at + HD, :]
                if part < 2:
                    low, high = low * cosine + high * sine, high * cosine - low * sine
                to = which * 2 * HD + at
                dt_ref[part, to : to + HD // 2, :] = low.astype(BF16)
                dt_ref[part, to + HD // 2 : to + HD, :] = high.astype(BF16)
    for part in range(3):
        made = nn(dt_ref[part], n1_ref[...])
        for slot in range(4):
            ref = odd_ref if slot % 2 else even_ref
            ref[slot // 2, part * HD : (part + 1) * HD, :] = made[slot * HD : (slot + 1) * HD].astype(BF16)


def attend_back(turn, starts, cosine, sine, n1, sets, do, qb=512):
    width = n1.shape[1]
    head = pl.BlockSpec((1, 2 * HD, LEN), lambda i: (turn, 0, 0))
    full = lambda a: pl.BlockSpec(a.shape, lambda i, n=a.ndim: (0,) * n)
    lse = pl.BlockSpec((1, 2, LEN), lambda i: (turn, 0, 0))
    args = (starts, cosine, sine, n1, *sets[0], *sets[1], do)
    out = [struct((3, 4 * HD, LEN), BF16)] + [struct((2, 3 * HD, width), BF16)] * 2
    return call(
        functools.partial(attend_back_body, qb),
        "attend_back",
        out,
        args,
        16,
        grid=(1,),
        in_specs=[pl.BlockSpec(memory_space=pltpu.SMEM), full(cosine), full(sine), full(n1)]
        + [head, head, head, head, lse] * 2
        + [pl.BlockSpec((4 * HD, LEN), lambda i: (turn, 0))],
        out_specs=[full(o) for o in out],
        scratch_shapes=[pltpu.VMEM((3, 2 * HD, LEN), F32)],
    )


def turn_rows(w_refs):
    return jnp.concatenate(
        [w[3, turn * HD : (turn + 1) * HD, :] for turn in range(3) for w in w_refs], axis=0
    )


def after_body(
    meta_ref, x_ref, ma_ref, mb_ref, w0, w1, w2, w3, gain_ref, g0, g1, g2, g3,
    after_ref, n2_ref, n2t_ref, g_ref, gt_ref,
):
    slot = pl.program_id(0) ^ meta_ref[2]
    for which, piece in enumerate((g0, g1, g2, g3)):

        @pl.when(slot == which)
        def _():
            g_ref[...] = piece[...]

    first = turn_rows((w0, w1))
    second = turn_rows((w2, w3))
    after = x_ref[...].astype(F32) + nn(ma_ref[...], first) + nn(mb_ref[...], second)
    after_ref[...] = after
    scale = lax.rsqrt(jnp.mean(after * after, axis=-1, keepdims=True) + EPS)
    normed = (after * scale * gain_ref[...]).astype(BF16)
    n2_ref[...] = normed
    n2t_ref[...] = normed.T
    gt_ref[...] = g_ref[...].T


def after_attention(meta, x, mixed_a, mixed_b, wo, gain, g):
    width = x.shape[1]
    step = 256
    rows = lambda n: pl.BlockSpec((step, n), lambda i: (i, 0))
    cols = pl.BlockSpec((width, step), lambda i: (0, i))
    full = lambda a: pl.BlockSpec(a.shape, lambda i, n=a.ndim: (0,) * n)
    args = (meta, x, mixed_a, mixed_b, *wo, gain, *g)
    out = [
        struct((LEN, width), F32),
        struct((LEN, width), BF16),
        struct((width, LEN), BF16),
        struct((LEN, width), BF16),
        struct((width, LEN), BF16),
    ]
    return call(
        after_body,
        "after_attention",
        out,
        args,
        12,
        grid=(LEN // step,),
        in_specs=[SM, rows(width), rows(6 * HD), rows(6 * HD)]
        + [full(w) for w in wo]
        + [full(gain)]
        + [full(p) for p in g],
        out_specs=[rows(width), rows(width), cols, rows(width), cols],
    )


def mlp_body(layout, first, meta_ref, n2_ref, n2t_ref, g_ref, gt_ref, *refs):
    block = 256
    refs = list(refs)
    sources = [[refs.pop(0) for _ in range(kind)] for kind in layout]
    if not first:
        out_in, back_in = refs.pop(0), refs.pop(0)
    out_ref, back_ref = refs.pop(0), refs.pop(0)
    made = [refs.pop(0) for _ in layout]
    hid, dga, dup = refs[:3]
    if first:
        out_ref[...] = jnp.zeros_like(out_ref)
        back_ref[...] = jnp.zeros_like(back_ref)
    else:
        out_ref[...] = out_in[...]
        back_ref[...] = back_in[...]
    width = n2_ref.shape[1]
    half = 3 * width // 2
    for source, dw_ref in zip(sources, made):
        if len(source) == 2:
            hold = refs[3]
            hold[meta_ref[3]] = source[0][...]
            hold[1 - meta_ref[3]] = source[1][...]

            def take(part, cols, hold=hold):
                if part == 0:
                    return hold[0, :width, cols]
                if part == 2:
                    return hold[1, half - width :, cols]
                return jnp.concatenate([hold[0, width:, cols], hold[1, : half - width, cols]], axis=0)
        else:

            def take(part, cols, hold=source[0]):
                return hold[part, :, cols]

        for part in range(2):
            cols = slice(part * block, (part + 1) * block)
            wg = take(0, cols)
            wu = take(1, cols)
            wl = take(2, cols)
            n2 = n2_ref[...]
            gate = nn(n2, wg)
            up = nn(n2, wu)
            grad = nn(g_ref[...], wl)
            sigma = 1.0 / (1.0 + jnp.exp(-gate))
            silu = gate * sigma
            hid[...] = (silu * up).astype(BF16)
            dup[...] = (grad * silu).astype(BF16)
            dga[...] = (grad * up * (sigma * (1.0 + gate * (1.0 - sigma)))).astype(BF16)
            out_ref[...] += nt(hid[...], wl)
            back_ref[...] += nt(dga[...], wg) + nt(dup[...], wu)
            dw_ref[0, :, cols] = nn(n2t_ref[...], dga[...]).astype(BF16)
            dw_ref[1, :, cols] = nn(n2t_ref[...], dup[...]).astype(BF16)
            dw_ref[2, :, cols] = nn(gt_ref[...], hid[...]).astype(BF16)


def mlp(meta, n2, n2t, g, gt, weights, before=()):
    width = n2.shape[1]
    units = 512
    layout = tuple(len(w) for w in weights)
    out = [struct((LEN, width), F32)] * 2 + [struct((3, width, units), BF16)] * len(weights)
    args = (meta, n2, n2t, g, gt, *[a for w in weights for a in w], *before)
    scratch = [pltpu.VMEM((LEN, 256), BF16)] * 3
    if 2 in layout:
        scratch.append(pltpu.VMEM((2, 3 * width // 2, units), BF16))
    aliases = {len(args) - 2: 0, len(args) - 1: 1} if before else {}
    return call(
        functools.partial(mlp_body, layout, not before),
        "mlp",
        out,
        args,
        24,
        in_specs=[SM] + [VM] * (len(args) - 1),
        out_specs=[VM] * len(out),
        scratch_shapes=scratch,
        input_output_aliases=aliases,
    )


def norm_back(grad, value, gain):
    scale = lax.rsqrt(jnp.mean(value * value, axis=-1, keepdims=True) + EPS)
    unit = value * scale
    gain_grad = jnp.sum(grad * unit, axis=0, keepdims=True)
    e = grad * gain
    return scale * (e - unit * jnp.mean(e * unit, axis=-1, keepdims=True)), gain_grad


def give(meta_ref, value, refs):
    slot = pl.program_id(0) ^ meta_ref[2]
    for which, ref in enumerate(refs[:2]):

        @pl.when(slot == which)
        def _():
            ref[...] = value

    for which in range(2):

        @pl.when(slot == 2 + which)
        def _():
            refs[2][which] = value


def middle_body(
    meta_ref, x_ref, after_ref, sum_ref, back_ref, g_ref, gain_ref, mta_ref, mtb_ref,
    w0, w1, w2, w3, e0, e1, e23, da_ref, do_ref, even_ref, odd_ref, gain_out, acc,
):
    step = pl.program_id(0)
    after = after_ref[...]
    delta = (after - x_ref[...].astype(F32) + sum_ref[...]).astype(BF16)
    give(meta_ref, delta, (e0, e1, e23))
    back, gain_grad = norm_back(back_ref[...], after, gain_ref[...])
    grad_after = g_ref[...].astype(F32) + back
    da_ref[...] = grad_after
    low = grad_after.astype(BF16)

    @pl.when(step == 0)
    def _():
        gain_out[...] = jnp.zeros_like(gain_out)
        acc[...] = jnp.zeros_like(acc)

    gain_out[...] += gain_grad
    weights = turn_rows((w0, w1, w2, w3))
    do_ref[...] = nt(weights, low).astype(BF16)
    for turn in range(3):
        for which, mt in enumerate((mta_ref, mtb_ref)):
            acc[turn, which] += nn(mt[turn], low)

    @pl.when(step == pl.num_programs(0) - 1)
    def _():
        for turn in range(3):
            for slot in range(4):
                at = (slot % 2) * HD
                ref = odd_ref if slot % 2 else even_ref
                ref[slot // 2, turn * HD : (turn + 1) * HD, :] = acc[turn, slot // 2, at : at + HD, :].astype(BF16)


def middle(meta, x, after, total, back, g, gain, mts, wo):
    width = x.shape[1]
    step = 256
    rows = pl.BlockSpec((step, width), lambda i: (i, 0))
    full = lambda a: pl.BlockSpec(a.shape, lambda i, n=a.ndim: (0,) * n)
    heads = pl.BlockSpec((3, 2 * HD, step), lambda i: (0, 0, i))
    args = (meta, x, after, total, back, g, gain, *mts, *wo)
    out = [struct((step, width), BF16)] * 2 + [
        struct((2, step, width), BF16),
        struct((LEN, width), F32),
        struct((12 * HD, LEN), BF16),
        struct((2, 3 * HD, width), BF16),
        struct((2, 3 * HD, width), BF16),
        struct((1, width), F32),
    ]
    return call(
        middle_body,
        "middle",
        out,
        args,
        14,
        grid=(LEN // step,),
        in_specs=[SM] + [rows] * 5 + [full(gain), heads, heads] + [full(w) for w in wo],
        out_specs=[full(o) for o in out[:3]]
        + [rows, pl.BlockSpec((12 * HD, step), lambda i: (0, i)), full(out[5]), full(out[6]), full(out[7])],
        scratch_shapes=[pltpu.VMEM((3, 2, 2 * HD, width), F32)],
    )


def token_grad_body(turns, meta_ref, *refs):
    dts = refs[: len(turns)]
    weights = refs[len(turns) : len(turns) + 4]
    rest = refs[len(turns) + 4 :]
    step = pl.program_id(0)
    total = None
    for turn, dt in zip(turns, dts):
        for part in range(3):
            w = jnp.concatenate([w[part, turn * HD : (turn + 1) * HD, :] for w in weights], axis=0)
            more = nn(dt[part].T, w)
            total = more if total is None else total + more
    x_ref, da_ref, g_ref, gain_ref, e0, e1, e23, gain_out = rest
    back, gain_grad = norm_back(total, x_ref[...].astype(F32), gain_ref[...])
    give(meta_ref, (da_ref[...] - g_ref[...].astype(F32) + back).astype(BF16), (e0, e1, e23))

    @pl.when(step == 0)
    def _():
        gain_out[...] = jnp.zeros_like(gain_out)

    gain_out[...] += gain_grad


def token_grad(meta, turns, dts, weights, rest):
    width = weights[0].shape[2]
    step = 256
    rows = pl.BlockSpec((step, width), lambda i: (i, 0))
    full = lambda a: pl.BlockSpec(a.shape, lambda i, n=a.ndim: (0,) * n)
    cols = pl.BlockSpec((3, 4 * HD, step), lambda i: (0, 0, i))
    out = [struct((step, width), BF16)] * 2 + [struct((2, step, width), BF16), struct((1, width), F32)]
    return call(
        functools.partial(token_grad_body, turns),
        "token_grad",
        out,
        (meta, *dts, *weights, *rest),
        16,
        grid=(LEN // step,),
        in_specs=[SM] + [cols] * len(dts) + [full(w) for w in weights] + [rows] * 3 + [full(rest[3])],
        out_specs=[full(o) for o in out],
    )


def rope_tables(length, width):
    halfway = width // 2
    inverse = 10000.0 ** (-jnp.arange(halfway, dtype=F32) * 2.0 / width)
    angles = inverse[:, None] * jnp.arange(length, dtype=F32)[None, :]
    return jnp.cos(angles), jnp.sin(angles)


def swap(value, axis, size, mask):
    return lax.ppermute(value, axis, [(i, i ^ mask) for i in range(size)])


def added(*refs):
    total = refs[0].astype(F32)
    for ref in refs[1:]:
        total = total + ref.astype(F32)
    return total.astype(BF16)


def put(cond, ref, at, value):
    @pl.when(cond)
    def _():
        if at is None:
            ref[...] = value
        else:
            ref[at] = value


def start_body(meta_ref, a0, b0, a2, b2, keep_p, send_p, keep_q, send_q):
    step = pl.program_id(0)
    bit = meta_ref[3]
    two = meta_ref[4]
    for slot, (a, b) in enumerate(((a0, b0), (a2, b2))):
        value = added(a[0], b[0])
        put(step == bit, keep_p, slot, value)
        put(step == 1 - bit, send_p, slot, value)
        put(step == 2 + two, keep_q, slot, value)
        put(step == 3 - two, send_q, slot, value)


def start_sums(meta, dw0, in1, dw2, in3):
    rows = dw0.shape[0] * dw0.shape[1] // 4
    cols = dw0.shape[2]
    parts = [a.reshape(4, rows, cols) for a in (dw0, in1, dw2, in3)]
    out = [struct((2, rows, cols), BF16)] * 4
    return call(
        start_body,
        "start_sums",
        out,
        (meta, *parts),
        10,
        grid=(4,),
        in_specs=[SM] + [pl.BlockSpec((1, rows, cols), lambda i: (i, 0, 0))] * 4,
        out_specs=[pl.BlockSpec((2, rows, cols), lambda i: (0, 0, 0))] * 4,
    )


def second_body(meta_ref, kp, rp, kq, rq, keep, send_p, send_q):
    step = pl.program_id(0)
    for which, (k, r, send, bit) in enumerate(((kp, rp, send_p, meta_ref[4]), (kq, rq, send_q, meta_ref[3]))):
        for slot in range(2):
            value = added(k[slot, 0], r[slot, 0])
            put(step == bit, keep, (which, slot), value)
            put(step == 1 - bit, send, slot, value)


def second_sums(meta, *pieces):
    _, rows, cols = pieces[0].shape
    half = rows // 2
    full = lambda n: pl.BlockSpec((2,) * n + (half, cols), lambda i: (0,) * (n + 2))
    return call(
        second_body,
        "second_sums",
        [struct((2, 2, half, cols), BF16)] + [struct((2, half, cols), BF16)] * 2,
        (meta, *[p.reshape(2, 2, half, cols) for p in pieces]),
        10,
        grid=(2,),
        in_specs=[SM] + [pl.BlockSpec((2, 1, half, cols), lambda i: (0, i, 0, 0))] * 4,
        out_specs=[full(2), full(1), full(1)],
    )


def third_body(meta_ref, a, bp, bq, keep, send):
    which = pl.program_id(0)
    for part, b in enumerate((bp, bq)):

        @pl.when(which == part)
        def _():
            keep[0] = added(a[0, 0], b[0])
            send[0] = added(a[0, 1], b[1])


def third_sums(meta, a, bp, bq):
    _, _, rows, cols = a.shape
    whole = pl.BlockSpec((2, rows, cols), lambda i: (0, 0, 0))
    block = pl.BlockSpec((1, rows, cols), lambda i: (i, 0, 0))
    return call(
        third_body,
        "third_sums",
        [struct((2, rows, cols), BF16)] * 2,
        (meta, a, bp, bq),
        8,
        grid=(2,),
        in_specs=[SM, pl.BlockSpec((1, 2, rows, cols), lambda i: (i, 0, 0, 0)), whole, whole],
        out_specs=[block, block],
    )


def halve_body(bit_ref, a, b, keep, send):
    bit = bit_ref[0]
    step = pl.program_id(0)
    for which in range(2):
        value = added(a[which, 0], b[which, 0])
        put(step == bit, keep, which, value)
        put(step != bit, send, which, value)


def halve_sums(bit, a, b):
    _, rows, cols = a.shape
    half = rows // 2
    return call(
        halve_body,
        "halve_sums",
        [struct((2, half, cols), BF16)] * 2,
        (bit.reshape(1), a.reshape(2, 2, half, cols), b.reshape(2, 2, half, cols)),
        8,
        grid=(2,),
        in_specs=[SM] + [pl.BlockSpec((2, 1, half, cols), lambda i: (0, i, 0, 0))] * 2,
        out_specs=[pl.BlockSpec((2, half, cols), lambda i: (0, 0, 0))] * 2,
    )


def plain_body(tie_ref, a, b, out):
    out[...] = added(a[...], b[...])


def plain_sum(tie, a, b):
    return call(plain_body, "plain_sum", [struct(a.shape, BF16)], (tie, a, b), 6, in_specs=[SM, VM, VM], out_specs=[VM])[0]


def split_body(bit_ref, a, b, keep, send):
    bit = bit_ref[0]
    step = pl.program_id(0)
    value = added(a[0], b[0])
    put(step == bit, keep, None, value)
    put(step != bit, send, None, value)


def split_sums(bit, a, b):
    rows, cols = a.shape
    half = rows // 2
    return call(
        split_body,
        "split_sums",
        [struct((half, cols), BF16)] * 2,
        (bit.reshape(1), a.reshape(2, half, cols), b.reshape(2, half, cols)),
        6,
        grid=(2,),
        in_specs=[SM] + [pl.BlockSpec((1, half, cols), lambda i: (i, 0, 0))] * 2,
        out_specs=[pl.BlockSpec((half, cols), lambda i: (0, 0))] * 2,
    )


def merge_body(bit_ref, a, b, out):
    bit = bit_ref[0]
    out[bit] = a[...]
    out[1 - bit] = b[...]


def merge(bit, a, b):
    rows, cols = a.shape
    made = call(
        merge_body,
        "merge",
        [struct((2, rows, cols), BF16)],
        (bit.reshape(1), a, b),
        6,
        in_specs=[SM, VM, VM],
        out_specs=[VM],
    )[0]
    return made.reshape(2 * rows, cols)


def pair_body(bit_ref, a, b, out):
    bit = bit_ref[0]
    for which in range(2):
        out[which, bit] = a[which]
        out[which, 1 - bit] = b[which]


def pair_join(bit, a, b):
    _, rows, cols = a.shape
    made = call(
        pair_body,
        "pair_join",
        [struct((2, 2, rows, cols), BF16)],
        (bit.reshape(1), a, b),
        6,
        in_specs=[SM, VM, VM],
        out_specs=[VM],
    )[0]
    return made.reshape(2, 2 * rows, cols)


def cross_body(meta_ref, a, bp, bq, out_p, out_q):
    two = meta_ref[4]
    bit = meta_ref[3]
    out_p[two] = a[0]
    out_p[1 - two] = bp[...]
    out_q[bit] = a[1]
    out_q[1 - bit] = bq[...]


def cross_join(meta, a, bp, bq):
    _, rows, cols = a.shape
    made = call(
        cross_body,
        "cross_join",
        [struct((2, rows, cols), BF16)] * 2,
        (meta, a, bp, bq),
        6,
        in_specs=[SM, VM, VM, VM],
        out_specs=[VM, VM],
    )
    return [m.reshape(2 * rows, cols) for m in made]


def mlp_out_body(meta_ref, p, rp, q, rq, gu_ref, wd_ref, hold):
    bit = meta_ref[3]
    two = meta_ref[4]
    hold[bit] = p[...]
    hold[1 - bit] = rp[...]
    hold[2 + two] = q[...]
    hold[3 - two] = rq[...]
    rows = hold.shape[1]
    pair = gu_ref.shape[0]
    for which in range(2):
        gu_ref[which * rows : (which + 1) * rows, :] = hold[which].astype(F32)
    rest = pair - 2 * rows
    gu_ref[2 * rows :, :] = hold[2, :rest, :].astype(F32)
    wd_ref[:, : rows - rest] = hold[2, rest:, :].astype(F32).T
    wd_ref[:, rows - rest :] = hold[3].astype(F32).T


def mlp_out(meta, p, rp, q, rq, width):
    rows, units = p.shape
    return call(
        mlp_out_body,
        "mlp_out",
        [struct((2 * width, units), F32), struct((units, width), F32)],
        (meta, p, rp, q, rq),
        14,
        in_specs=[SM] + [VM] * 4,
        out_specs=[VM] * 2,
        scratch_shapes=[pltpu.VMEM((4, rows, units), BF16)],
    )


def core_body(count, meta_ref, *refs):
    evens, ins = refs[:count], refs[count : 2 * count]
    keep, send = refs[2 * count :]
    rows = evens[0].shape[1]
    for which, (a, b) in enumerate(zip(evens, ins)):
        keep[which * rows : (which + 1) * rows, :] = added(a[0], b[0])
        send[which * rows : (which + 1) * rows, :] = added(a[1], b[1])


def core_sums(meta, evens, ins):
    count = len(evens)
    _, rows, cols = evens[0].shape
    args = (meta, *evens, *ins)
    return call(
        functools.partial(core_body, count),
        "core_sums",
        [struct((count * rows, cols), BF16)] * 2,
        args,
        8,
        in_specs=[SM] + [VM] * (2 * count),
        out_specs=[VM] * 2,
    )


def spread_body(tie_ref, in_ref, out_ref):
    total = in_ref[0].astype(F32)
    for which in range(1, in_ref.shape[0]):
        total = total + in_ref[which].astype(F32)
    total = total.astype(BF16)
    for which in range(in_ref.shape[0]):
        out_ref[which] = total


def spread_sum(tie, pieces):
    return call(spread_body, "spread_sum", [struct(pieces.shape, BF16)], (tie, pieces), 16, in_specs=[SM, VM], out_specs=[VM])[0]


GAIN_ROWS = 8


def spread_gain_body(tie_ref, in_ref, gain_ref, out_ref):
    count, rows, width = in_ref.shape
    total = in_ref[0].astype(F32)
    for which in range(1, count):
        total = total + in_ref[which].astype(F32)
    total = total.astype(BF16)
    gains = gain_ref[...]
    high = gains.astype(BF16)
    low = (gains - high.astype(F32)).astype(BF16)
    head = jnp.concatenate([high, low, jnp.zeros((GAIN_ROWS - 4, width), BF16)], axis=0)
    for which in range(count):
        out_ref[which, :GAIN_ROWS, :] = head
        out_ref[which, GAIN_ROWS:, :] = total


def spread_gain_sum(tie, pieces, gains):
    count, rows, width = pieces.shape
    return call(
        spread_gain_body,
        "spread_sum",
        [struct((count, rows + GAIN_ROWS, width), BF16)],
        (tie, pieces, gains),
        16,
        in_specs=[SM, VM, VM],
        out_specs=[VM],
    )[0]


def exchange(value):
    return lax.all_to_all(value, "dp", 0, 0)


def attn_out_body(meta_ref, own_ref, other_ref, late_ref, qkv_ref, wo_ref, gain_ref, hold, hold_early):
    bit = meta_ref[3]
    hold_early[bit] = own_ref[...]
    hold_early[1 - bit] = other_ref[...]
    early = hold_early[...].reshape(9 * HD, hold.shape[1])
    wo_ref[...] = early[: 3 * HD, :].astype(F32)
    count = late_ref.shape[0]
    rows = late_ref.shape[1] - GAIN_ROWS
    gains = None
    for which in range(count):
        head = late_ref[which, :GAIN_ROWS, :].astype(F32)
        gains = head if gains is None else gains + head
        hold[which * rows : (which + 1) * rows, :] = late_ref[which, GAIN_ROWS:, :].astype(F32)
    gain_ref[...] = gains[0:2] + gains[2:4]
    for part in range(3):
        at = part * HD
        parts = [early[3 * HD + at : 3 * HD + at + HD, :], early[6 * HD + at : 6 * HD + at + HD, :]]
        parts = [p.astype(F32) for p in parts] + [hold[at : at + HD, :]]
        qkv_ref[part] = jnp.concatenate(parts, axis=0).T


def attn_out(meta, own, other, late):
    width = own.shape[1]
    return call(
        attn_out_body,
        "attn_out",
        [struct((3, width, 3 * HD), F32), struct((3 * HD, width), F32), struct((2, width), F32)],
        (meta, own, other, late),
        12,
        in_specs=[SM, VM, VM, VM],
        out_specs=[VM, VM, VM],
        scratch_shapes=[pltpu.VMEM((3 * HD, width), F32), pltpu.VMEM((2,) + own.shape, BF16)],
    )


def add_home_body(meta_ref, in_ref, p0, p1, p23, p3, out_ref):
    slot = pl.program_id(0) ^ meta_ref[2]
    for which, piece in enumerate((p0, p1, p23.at[0], p3)):

        @pl.when(slot == which)
        def _():
            out_ref[0] = in_ref[0] + piece[...].astype(F32)


def add_home(meta, base, pieces):
    count, rows, width = base.shape
    block = pl.BlockSpec((1, rows, width), lambda i: (i, 0, 0))
    full = lambda a: pl.BlockSpec(a.shape, lambda i, n=a.ndim: (0,) * n)
    return call(
        add_home_body,
        "add_home",
        [struct(base.shape, F32)],
        (meta, base, *pieces),
        8,
        grid=(count,),
        in_specs=[SM, block] + [full(p) for p in pieces],
        out_specs=[block],
    )[0]


def tie(value, *after):
    return lax.optimization_barrier((value, *after))[0]


def local(n_dp, inputs, w_qkv, w_out, w_gate_up, w_down, gain_attn, gain_mlp, piece_starts, out_grad):
    width = inputs.shape[2]
    units = w_down.shape[0]
    here = lax.axis_index("tensor").astype(jnp.int32)
    row = lax.axis_index("dp").astype(jnp.int32)
    bit = row & 1
    bits = [(row >> s) & 1 for s in range(n_dp.bit_length() - 1)]
    mine = lax.dynamic_index_in_dim(piece_starts, here, 0, keepdims=False)[0]
    meta = jnp.concatenate([mine, jnp.stack([here, bits[0], bits[1]])])
    one = gain_attn[None]
    two = gain_mlp[None]
    cosine, sine = rope_tables(LEN, HD)
    tensor = functools.partial(swap, axis="tensor", size=4)
    dp = functools.partial(swap, axis="dp", size=n_dp)

    def picks(whole):
        return [lax.dynamic_index_in_dim(whole, here ^ k, 0, keepdims=False).astype(BF16) for k in range(4)]

    def around(pieces):
        return [pieces[0]] + [tensor(pieces[k], mask=k) for k in range(1, 4)]

    def homeward(own, core, far):
        received = tensor(far, mask=2)
        return own, tensor(core, mask=1), received, tensor(received[1], mask=1)

    def far(half):
        direct = tensor(half, mask=2)
        other = dp(direct, mask=1)
        return direct, other, tensor(direct, mask=1), tensor(other, mask=1)

    x_mine = picks(inputs)
    xs = around(x_mine)
    wa0 = jnp.concatenate([jnp.swapaxes(w_qkv, 1, 2), w_out[None]]).astype(BF16)
    wa1 = tensor(wa0, mask=1)
    wa_far = far(tie(lax.dynamic_slice_in_dim(wa0, 2 * bit, 2, 0), xs[1]))
    wm0 = jnp.concatenate([w_gate_up, w_down.T[None]]).astype(BF16)
    wm1 = tensor(wm0, mask=1)
    wm_far = far(lax.dynamic_slice_in_dim(wm0.reshape(3 * width, units), 3 * width // 2 * bit, 3 * width // 2, 0))
    gs = around(picks(out_grad))

    last = [meta]

    def run(kernel, first, *args, **kw):
        out = kernel(tie(first, last[0]), *args, **kw)
        last[0] = out[0] if isinstance(out, (list, tuple)) else out
        return out

    x, n1, qa, ka, va = run(project_first, meta, xs, one, wa0, wa1, cosine, sine)
    mta, ma, la = run(attend, meta, qa, ka, va)
    qb, kb, vb, wa2, wa3 = run(project_next, meta, n1, wa_far, cosine, sine)
    wa = (wa0, wa1, wa2, wa3)
    mtb, mb, lb = run(attend, meta, qb, kb, vb)
    after, n2, n2t, g, gt = run(after_attention, meta, x, ma, mb, wa, two, gs)
    acc_out, acc_back, dw1, dw0 = run(mlp, meta, n2, n2t, g, gt, ((wm1,), (wm0,)))
    in1 = tensor(dw1, mask=1)
    acc_out, acc_back, dw3, dw2 = run(mlp, meta, n2, n2t, g, gt, (wm_far[2:], wm_far[:2]), (acc_out, acc_back))
    in3 = tensor(dw3, mask=1)
    middle_out = run(middle, meta, x, after, acc_out, acc_back, g, two, (mta, mtb), wa)
    home = homeward(*middle_out[:3])
    da, do, even_o, odd_o, gain_two = middle_out[3:]
    in_o = tensor(odd_o, mask=1)
    keep_p, send_p, keep_q, send_q = run(start_sums, meta, dw0, in1, dw2, in3)
    recv_p = dp(send_p, mask=1)
    recv_q = dp(send_q, mask=2)
    sets = ((qa, ka, va, mta, la), (qb, kb, vb, mtb, lb))
    back = lambda turn: run(lambda m: attend_back(turn, m, cosine, sine, n1, sets, do), meta)
    dt0, even0, odd0 = back(0)
    in0 = tensor(odd0, mask=1)
    dt1, even1, odd1 = back(1)
    in1_ = tensor(odd1, mask=1)
    keep, send_p, send_q = run(second_sums, tie(meta, home[2]), keep_p, recv_p, keep_q, recv_q)
    recv_p = dp(send_p, mask=2)
    recv_q = dp(send_q, mask=1)
    early, early_send = run(core_sums, meta, (even_o, even0, even1), (in_o, in0, in1_))
    early_recv = tensor(early_send, mask=2)
    dt2, even2, odd2 = back(2)
    in2 = tensor(odd2, mask=1)
    keep, send = run(third_sums, tie(meta, home[3]), keep, recv_p, recv_q)
    pieces = tensor(send, mask=2)
    late, late_send = run(core_sums, meta, (even2,), (in2,))
    late_recv = tensor(late_send, mask=2)
    early, early_send = run(split_sums, bits[0], early, early_recv)
    early_recv = dp(early_send, mask=1)
    *grads, gain_one = run(lambda m: token_grad(m, (0, 1, 2), (dt0, dt1, dt2), wa, (x, da, g, one)), meta)
    for shift in range(2, len(bits)):
        keep, send = run(halve_sums, bits[shift], keep, pieces)
        pieces = dp(send, mask=1 << shift)
    late = run(plain_sum, meta, late, late_recv)
    late = exchange(late.reshape(n_dp, -1, width))
    grads = homeward(grads[0], grads[1], tie(grads[2], late_recv))
    early, early_send = run(split_sums, bits[1], early, early_recv)
    early_recv = dp(early_send, mask=2)
    gains = jnp.concatenate([gain_one, gain_two])
    gains = gains + tensor(gains, mask=1)
    gains = gains + tensor(gains, mask=2)
    for shift in range(2, len(bits)):
        early, early_send = run(split_sums, bits[shift], early, early_recv)
        early_recv = dp(early_send, mask=1 << shift)
    piece = run(plain_sum, meta, keep, pieces)
    other = dp(piece, mask=1 << (len(bits) - 1))
    early = run(plain_sum, meta, early, early_recv)
    early_recv = dp(early, mask=1 << (len(bits) - 1))
    late = exchange(run(spread_gain_sum, meta, late, gains))
    for shift in reversed(range(2, len(bits))):
        piece = run(pair_join, bits[shift], piece, other)
        if shift > 2:
            other = dp(piece, mask=1 << (shift - 1))
    recv_p = dp(piece[0], mask=2)
    recv_q = dp(piece[1], mask=1)
    for shift in reversed(range(2, len(bits))):
        early = run(merge, bits[shift], early, early_recv)
        early_recv = dp(early, mask=1 << (shift - 1))
    early = run(merge, bits[1], early, early_recv)
    early_recv = dp(early, mask=1)
    p, q = run(cross_join, meta, piece, recv_p, recv_q)
    recv_p = dp(p, mask=1)
    recv_q = dp(q, mask=2)
    outputs = run(add_home, meta, inputs, home)
    input_grad = run(add_home, meta, out_grad, grads)
    grad_qkv, grad_out, gains = run(attn_out, meta, early, early_recv, late)
    grad_pair, grad_down = run(mlp_out, meta, p, recv_p, q, recv_q, width)
    return (
        outputs,
        input_grad,
        grad_qkv,
        grad_out,
        grad_pair.reshape(2, width, units),
        grad_down,
        gains[0],
        gains[1],
    )


def solution(mesh):
    rows = P(None, ("dp", "tensor"), None)
    weights = (P(None, None, "tensor"), P("tensor", None), P(None, None, "tensor"), P("tensor", None))
    return jax.shard_map(
        functools.partial(local, mesh.shape["dp"]),
        mesh=mesh,
        in_specs=(rows, *weights, P(), P(), P(None, "dp", None), rows),
        out_specs=(rows, rows, *weights, P(), P()),
        check_vma=False,
    )
```

```python
import functools
import jax
import jax.numpy as jnp
import numpy as np
from jax import lax
from jax.experimental import pallas as pl
from jax.experimental.pallas import tpu as pltpu
from jax.sharding import PartitionSpec as P

HD = 64
LEN = 1024
PIECE = 256
HALF = 512
EPS = 1e-06
F32 = jnp.float32
BF16 = jnp.bfloat16
MIB = 1024 * 1024


def nn(a, b):
    return lax.dot_general(a, b, (((1,), (0,)), ((), ())), preferred_element_type=F32)


def nt(a, b):
    return lax.dot_general(a, b, (((1,), (1,)), ((), ())), preferred_element_type=F32)


COST = {
    "project_first": 5,
    "project_next": 5,
    "attend": 10,
    "after_attention": 5,
    "mlp": 15,
    "middle": 3,
    "attend_back": 2,
    "token_grad": 0.5,
    "start_sums": 1,
    "add_home": 0.1,
    "mlp_out": 0.1,
}
RATE = 1e9


def call(body, name, out_shape, args, vmem, **kw):
    return pl.pallas_call(
        body,
        name=name,
        out_shape=out_shape,
        compiler_params=pltpu.CompilerParams(vmem_limit_bytes=vmem * MIB),
        cost_estimate=pl.CostEstimate(flops=int(COST.get(name, 0.3) * RATE), bytes_accessed=0, transcendentals=0),
        **kw,
    )(*args)


def struct(shape, dtype):
    return jax.ShapeDtypeStruct(shape, dtype)


def project(n1_ref, weights, cos_ref, sin_ref, q_ref, k_ref, v_ref):
    step = 256
    for block in range(LEN // step):
        cols = slice(block * step, (block + 1) * step)
        rows = n1_ref[cols, :]
        cosine = cos_ref[:, cols]
        sine = sin_ref[:, cols]
        for slot, w_ref in enumerate(weights):
            for part, ref in ((0, q_ref), (1, k_ref), (2, v_ref)):
                made = nt(w_ref[part], rows)
                for head in range(3):
                    low = made[head * HD : head * HD + HD // 2]
                    high = made[head * HD + HD // 2 : (head + 1) * HD]
                    if part < 2:
                        low, high = low * cosine - high * sine, high * cosine + low * sine
                    if part == 0:
                        low, high = low * HD**-0.5, high * HD**-0.5
                    at = slot * HD
                    ref[head, at : at + HD // 2, cols] = low.astype(BF16)
                    ref[head, at + HD // 2 : at + HD, cols] = high.astype(BF16)


def in_order(here, pieces, ref):
    step = ref.shape[0] // 4
    for quarter in range(4):
        for slot, piece in enumerate(pieces):

            @pl.when((here ^ slot) == quarter)
            def _():
                ref[quarter * step : (quarter + 1) * step, :] = piece[...]


def project_first_body(meta_ref, p0, p1, p2, p3, gain_ref, w0, w1, cos_ref, sin_ref, x_ref, n1_ref, q_ref, k_ref, v_ref):
    step = 256
    gain = gain_ref[...]
    in_order(meta_ref[2], (p0, p1, p2, p3), x_ref)
    for block in range(LEN // step):
        rows = slice(block * step, (block + 1) * step)
        x = x_ref[rows, :].astype(F32)
        scale = lax.rsqrt(jnp.mean(x * x, axis=-1, keepdims=True) + EPS)
        n1_ref[rows, :] = (x * scale * gain).astype(BF16)
    project(n1_ref, (w0, w1), cos_ref, sin_ref, q_ref, k_ref, v_ref)


def project_next_body(
    meta_ref, n1_ref, d2, r2, d3, r3, cos_ref, sin_ref, q_ref, k_ref, v_ref, w2_ref, w3_ref
):
    bit = meta_ref[3]
    for direct, other, ref in ((d2, r2, w2_ref), (d3, r3, w3_ref)):
        for part in range(2):
            ref[2 * bit + part] = direct[part]
            ref[2 * (1 - bit) + part] = other[part]
    project(n1_ref, (w2_ref, w3_ref), cos_ref, sin_ref, q_ref, k_ref, v_ref)


HEADS3 = (3, 2 * HD, LEN)


VM = pl.BlockSpec(memory_space=pltpu.VMEM)
SM = pl.BlockSpec(memory_space=pltpu.SMEM)


def project_first(meta, pieces, gain, w0, w1, cosine, sine):
    width = gain.shape[1]
    out = [struct((LEN, width), BF16)] * 2 + [struct(HEADS3, BF16)] * 3
    args = (meta, *pieces, gain, w0, w1, cosine, sine)
    return call(
        project_first_body,
        "project_first",
        out,
        args,
        10,
        in_specs=[SM] + [VM] * (len(args) - 1),
        out_specs=[VM] * len(out),
    )


def project_next(meta, n1, far, cosine, sine):
    out = [struct(HEADS3, BF16)] * 3 + [struct((4,) + far[0].shape[1:], BF16)] * 2
    args = (meta, n1, *far, cosine, sine)
    return call(
        project_next_body,
        "project_next",
        out,
        args,
        10,
        in_specs=[SM] + [VM] * (len(args) - 1),
        out_specs=[VM] * len(out),
    )


def limits(starts_ref):
    pos = lax.broadcasted_iota(jnp.int32, (1, LEN), 1)
    lim = pos
    for piece in range(2):
        first = starts_ref[piece]
        lim = jnp.where((pos >= first) & (pos < first + PIECE), first + PIECE - 1, lim)
    return lim


def one_head(block, head):
    zero = jnp.zeros((HD, block.shape[1]), block.dtype)
    part = block[head * HD : (head + 1) * HD]
    return jnp.concatenate([part, zero] if head == 0 else [zero, part], axis=0)


NEG = -1e30


def attend_body(qb, starts_ref, q_ref, k_ref, v_ref, mt_ref, m_ref, lse_ref):
    lim = limits(starts_ref)
    k_rows = k_ref[0].T
    for head in range(2):
        q_one = one_head(q_ref[0], head)
        v_one = v_ref[0, head * HD : (head + 1) * HD, :]
        for block in range(LEN // qb):
            cols = slice(block * qb, (block + 1) * qb)
            keys = HALF if (block + 1) * qb <= HALF else LEN
            scores = nn(k_rows[:keys], q_one[:, cols])
            edge = scores[keys - HALF :]
            pos = lax.broadcasted_iota(jnp.int32, (HALF, qb), 0) + (keys - HALF)
            edge = jnp.where(pos <= lim[:, cols], edge, NEG)
            most = jnp.max(edge, axis=0, keepdims=True)
            if keys > HALF:
                body = scores[:HALF]
                most = jnp.maximum(most, jnp.max(body, axis=0, keepdims=True))
            soft = jnp.exp(edge - most)
            total = jnp.sum(soft, axis=0, keepdims=True)
            mixed = nn(v_one[:, keys - HALF : keys], soft.astype(BF16))
            if keys > HALF:
                soft = jnp.exp(body - most)
                total = total + jnp.sum(soft, axis=0, keepdims=True)
                mixed = mixed + nn(v_one[:, :HALF], soft.astype(BF16))
            mt_ref[0, head * HD : (head + 1) * HD, cols] = (mixed * (1.0 / total)).astype(BF16)
            lse_ref[0, head : head + 1, cols] = most + jnp.log(total)
    m_ref[...] = mt_ref[0].T


def attend(starts, q, k, v, qb=512):
    block = pl.BlockSpec((1, 2 * HD, LEN), lambda i: (i, 0, 0))
    out = [struct(HEADS3, BF16), struct((LEN, 6 * HD), BF16), struct((3, 2, LEN), F32)]
    return call(
        functools.partial(attend_body, qb),
        "attend",
        out,
        (starts, q, k, v),
        10,
        grid=(3,),
        in_specs=[pl.BlockSpec(memory_space=pltpu.SMEM), block, block, block],
        out_specs=[
            block,
            pl.BlockSpec((LEN, 2 * HD), lambda i: (0, i)),
            pl.BlockSpec((1, 2, LEN), lambda i: (i, 0, 0)),
        ],
    )


def attend_back_body(qb, starts_ref, cos_ref, sin_ref, n1_ref, *refs):
    sets = (refs[0:5], refs[5:10])
    do_ref = refs[10]
    dt_ref, even_ref, odd_ref, acc_ref = refs[11:]
    lim = limits(starts_ref)
    for which, (q_ref, k_ref, v_ref, mt_ref, lse_ref) in enumerate(sets):
        q = q_ref[0]
        k = k_ref[0]
        v = v_ref[0]
        do = do_ref[which * 2 * HD : (which + 1) * 2 * HD, :]
        k_rows = k.T
        v_rows = v.T
        both = do.astype(F32) * mt_ref[0].astype(F32)
        for head in range(2):
            mine = slice(head * HD, (head + 1) * HD)
            inner = jnp.sum(both[mine], axis=0, keepdims=True)
            q_one = one_head(q, head)
            do_one = one_head(do, head)
            lse = lse_ref[0, head : head + 1, :]
            for block in range(LEN // qb):
                cols = slice(block * qb, (block + 1) * qb)
                wide = (block + 1) * qb > HALF
                dq = None
                for part in range(2 if wide else 1):
                    keys = slice(part * HALF, (part + 1) * HALF)
                    scores = nn(k_rows[keys], q_one[:, cols])
                    if part == (1 if wide else 0):
                        pos = lax.broadcasted_iota(jnp.int32, (HALF, qb), 0) + part * HALF
                        scores = jnp.where(pos <= lim[:, cols], scores, NEG)
                    soft = jnp.exp(scores - lse[:, cols])
                    grad = nn(v_rows[keys], do_one[:, cols])
                    grad = (soft * (grad - inner[:, cols])).astype(BF16)
                    more = nn(k[mine, keys], grad)
                    dq = more if dq is None else dq + more
                    dk = nt(q[mine, cols], grad)
                    dv = nt(do[mine, cols], soft.astype(BF16))
                    fresh = block == (0 if part == 0 else HALF // qb)
                    if fresh:
                        acc_ref[1, mine, keys] = dk
                        acc_ref[2, mine, keys] = dv
                    else:
                        acc_ref[1, mine, keys] += dk
                        acc_ref[2, mine, keys] += dv
                acc_ref[0, mine, cols] = dq * HD**-0.5
        cosine = cos_ref[...]
        sine = sin_ref[...]
        for part in range(3):
            for head in range(2):
                at = head * HD
                low = acc_ref[part, at : at + HD // 2, :]
                high = acc_ref[part, at + HD // 2 : at + HD, :]
                if part < 2:
                    low, high = low * cosine + high * sine, high * cosine - low * sine
                to = which * 2 * HD + at
                dt_ref[part, to : to + HD // 2, :] = low.astype(BF16)
                dt_ref[part, to + HD // 2 : to + HD, :] = high.astype(BF16)
    for part in range(3):
        made = nn(dt_ref[part], n1_ref[...])
        for slot in range(4):
            ref = odd_ref if slot % 2 else even_ref
            ref[slot // 2, part * HD : (part + 1) * HD, :] = made[slot * HD : (slot + 1) * HD].astype(BF16)


def attend_back(turn, starts, cosine, sine, n1, sets, do, qb=512):
    width = n1.shape[1]
    head = pl.BlockSpec((1, 2 * HD, LEN), lambda i: (turn, 0, 0))
    full = lambda a: pl.BlockSpec(a.shape, lambda i, n=a.ndim: (0,) * n)
    lse = pl.BlockSpec((1, 2, LEN), lambda i: (turn, 0, 0))
    args = (starts, cosine, sine, n1, *sets[0], *sets[1], do)
    out = [struct((3, 4 * HD, LEN), BF16)] + [struct((2, 3 * HD, width), BF16)] * 2
    return call(
        functools.partial(attend_back_body, qb),
        "attend_back",
        out,
        args,
        16,
        grid=(1,),
        in_specs=[pl.BlockSpec(memory_space=pltpu.SMEM), full(cosine), full(sine), full(n1)]
        + [head, head, head, head, lse] * 2
        + [pl.BlockSpec((4 * HD, LEN), lambda i: (turn, 0))],
        out_specs=[full(o) for o in out],
        scratch_shapes=[pltpu.VMEM((3, 2 * HD, LEN), F32)],
    )


def turn_rows(w_refs):
    return jnp.concatenate(
        [w[3, turn * HD : (turn + 1) * HD, :] for turn in range(3) for w in w_refs], axis=0
    )


def after_body(
    meta_ref, x_ref, ma_ref, mb_ref, w0, w1, w2, w3, gain_ref, g0, g1, g2, g3,
    after_ref, n2_ref, n2t_ref, g_ref, gt_ref,
):
    slot = pl.program_id(0) ^ meta_ref[2]
    for which, piece in enumerate((g0, g1, g2, g3)):

        @pl.when(slot == which)
        def _():
            g_ref[...] = piece[...]

    first = turn_rows((w0, w1))
    second = turn_rows((w2, w3))
    after = x_ref[...].astype(F32) + nn(ma_ref[...], first) + nn(mb_ref[...], second)
    after_ref[...] = after
    scale = lax.rsqrt(jnp.mean(after * after, axis=-1, keepdims=True) + EPS)
    normed = (after * scale * gain_ref[...]).astype(BF16)
    n2_ref[...] = normed
    n2t_ref[...] = normed.T
    gt_ref[...] = g_ref[...].T


def after_attention(meta, x, mixed_a, mixed_b, wo, gain, g):
    width = x.shape[1]
    step = 256
    rows = lambda n: pl.BlockSpec((step, n), lambda i: (i, 0))
    cols = pl.BlockSpec((width, step), lambda i: (0, i))
    full = lambda a: pl.BlockSpec(a.shape, lambda i, n=a.ndim: (0,) * n)
    args = (meta, x, mixed_a, mixed_b, *wo, gain, *g)
    out = [
        struct((LEN, width), F32),
        struct((LEN, width), BF16),
        struct((width, LEN), BF16),
        struct((LEN, width), BF16),
        struct((width, LEN), BF16),
    ]
    return call(
        after_body,
        "after_attention",
        out,
        args,
        12,
        grid=(LEN // step,),
        in_specs=[SM, rows(width), rows(6 * HD), rows(6 * HD)]
        + [full(w) for w in wo]
        + [full(gain)]
        + [full(p) for p in g],
        out_specs=[rows(width), rows(width), cols, rows(width), cols],
    )


def mlp_body(layout, first, meta_ref, n2_ref, n2t_ref, g_ref, gt_ref, *refs):
    block = 256
    refs = list(refs)
    sources = [[refs.pop(0) for _ in range(kind)] for kind in layout]
    if not first:
        out_in, back_in = refs.pop(0), refs.pop(0)
    out_ref, back_ref = refs.pop(0), refs.pop(0)
    made = [refs.pop(0) for _ in layout]
    hid, dga, dup = refs[:3]
    if first:
        out_ref[...] = jnp.zeros_like(out_ref)
        back_ref[...] = jnp.zeros_like(back_ref)
    else:
        out_ref[...] = out_in[...]
        back_ref[...] = back_in[...]
    width = n2_ref.shape[1]
    half = 3 * width // 2
    for source, dw_ref in zip(sources, made):
        if len(source) == 2:
            hold = refs[3]
            hold[meta_ref[3]] = source[0][...]
            hold[1 - meta_ref[3]] = source[1][...]

            def take(part, cols, hold=hold):
                if part == 0:
                    return hold[0, :width, cols]
                if part == 2:
                    return hold[1, half - width :, cols]
                return jnp.concatenate([hold[0, width:, cols], hold[1, : half - width, cols]], axis=0)
        else:

            def take(part, cols, hold=source[0]):
                return hold[part, :, cols]

        for part in range(2):
            cols = slice(part * block, (part + 1) * block)
            wg = take(0, cols)
            wu = take(1, cols)
            wl = take(2, cols)
            n2 = n2_ref[...]
            gate = nn(n2, wg)
            up = nn(n2, wu)
            grad = nn(g_ref[...], wl)
            sigma = 1.0 / (1.0 + jnp.exp(-gate))
            silu = gate * sigma
            hid[...] = (silu * up).astype(BF16)
            dup[...] = (grad * silu).astype(BF16)
            dga[...] = (grad * up * (sigma * (1.0 + gate * (1.0 - sigma)))).astype(BF16)
            out_ref[...] += nt(hid[...], wl)
            back_ref[...] += nt(dga[...], wg) + nt(dup[...], wu)
            dw_ref[0, :, cols] = nn(n2t_ref[...], dga[...]).astype(BF16)
            dw_ref[1, :, cols] = nn(n2t_ref[...], dup[...]).astype(BF16)
            dw_ref[2, :, cols] = nn(gt_ref[...], hid[...]).astype(BF16)


def mlp(meta, n2, n2t, g, gt, weights, before=()):
    width = n2.shape[1]
    units = 512
    layout = tuple(len(w) for w in weights)
    out = [struct((LEN, width), F32)] * 2 + [struct((3, width, units), BF16)] * len(weights)
    args = (meta, n2, n2t, g, gt, *[a for w in weights for a in w], *before)
    scratch = [pltpu.VMEM((LEN, 256), BF16)] * 3
    if 2 in layout:
        scratch.append(pltpu.VMEM((2, 3 * width // 2, units), BF16))
    aliases = {len(args) - 2: 0, len(args) - 1: 1} if before else {}
    return call(
        functools.partial(mlp_body, layout, not before),
        "mlp",
        out,
        args,
        24,
        in_specs=[SM] + [VM] * (len(args) - 1),
        out_specs=[VM] * len(out),
        scratch_shapes=scratch,
        input_output_aliases=aliases,
    )


def norm_back(grad, value, gain):
    scale = lax.rsqrt(jnp.mean(value * value, axis=-1, keepdims=True) + EPS)
    unit = value * scale
    gain_grad = jnp.sum(grad * unit, axis=0, keepdims=True)
    e = grad * gain
    return scale * (e - unit * jnp.mean(e * unit, axis=-1, keepdims=True)), gain_grad


def give(meta_ref, value, refs):
    slot = pl.program_id(0) ^ meta_ref[2]
    for which, ref in enumerate(refs[:2]):

        @pl.when(slot == which)
        def _():
            ref[...] = value

    for which in range(2):

        @pl.when(slot == 2 + which)
        def _():
            refs[2][which] = value


def middle_body(
    meta_ref, x_ref, after_ref, sum_ref, back_ref, g_ref, gain_ref, mta_ref, mtb_ref,
    w0, w1, w2, w3, e0, e1, e23, da_ref, do_ref, even_ref, odd_ref, gain_out, acc,
):
    step = pl.program_id(0)
    after = after_ref[...]
    delta = (after - x_ref[...].astype(F32) + sum_ref[...]).astype(BF16)
    give(meta_ref, delta, (e0, e1, e23))
    back, gain_grad = norm_back(back_ref[...], after, gain_ref[...])
    grad_after = g_ref[...].astype(F32) + back
    da_ref[...] = grad_after
    low = grad_after.astype(BF16)

    @pl.when(step == 0)
    def _():
        gain_out[...] = jnp.zeros_like(gain_out)
        acc[...] = jnp.zeros_like(acc)

    gain_out[...] += gain_grad
    weights = turn_rows((w0, w1, w2, w3))
    do_ref[...] = nt(weights, low).astype(BF16)
    for turn in range(3):
        for which, mt in enumerate((mta_ref, mtb_ref)):
            acc[turn, which] += nn(mt[turn], low)

    @pl.when(step == pl.num_programs(0) - 1)
    def _():
        for turn in range(3):
            for slot in range(4):
                at = (slot % 2) * HD
                ref = odd_ref if slot % 2 else even_ref
                ref[slot // 2, turn * HD : (turn + 1) * HD, :] = acc[turn, slot // 2, at : at + HD, :].astype(BF16)


def middle(meta, x, after, total, back, g, gain, mts, wo):
    width = x.shape[1]
    step = 256
    rows = pl.BlockSpec((step, width), lambda i: (i, 0))
    full = lambda a: pl.BlockSpec(a.shape, lambda i, n=a.ndim: (0,) * n)
    heads = pl.BlockSpec((3, 2 * HD, step), lambda i: (0, 0, i))
    args = (meta, x, after, total, back, g, gain, *mts, *wo)
    out = [struct((step, width), BF16)] * 2 + [
        struct((2, step, width), BF16),
        struct((LEN, width), F32),
        struct((12 * HD, LEN), BF16),
        struct((2, 3 * HD, width), BF16),
        struct((2, 3 * HD, width), BF16),
        struct((1, width), F32),
    ]
    return call(
        middle_body,
        "middle",
        out,
        args,
        14,
        grid=(LEN // step,),
        in_specs=[SM] + [rows] * 5 + [full(gain), heads, heads] + [full(w) for w in wo],
        out_specs=[full(o) for o in out[:3]]
        + [rows, pl.BlockSpec((12 * HD, step), lambda i: (0, i)), full(out[5]), full(out[6]), full(out[7])],
        scratch_shapes=[pltpu.VMEM((3, 2, 2 * HD, width), F32)],
    )


def token_grad_body(turns, meta_ref, *refs):
    dts = refs[: len(turns)]
    weights = refs[len(turns) : len(turns) + 4]
    rest = refs[len(turns) + 4 :]
    step = pl.program_id(0)
    total = None
    for turn, dt in zip(turns, dts):
        for part in range(3):
            w = jnp.concatenate([w[part, turn * HD : (turn + 1) * HD, :] for w in weights], axis=0)
            more = nn(dt[part].T, w)
            total = more if total is None else total + more
    x_ref, da_ref, g_ref, gain_ref, e0, e1, e23, gain_out = rest
    back, gain_grad = norm_back(total, x_ref[...].astype(F32), gain_ref[...])
    give(meta_ref, (da_ref[...] - g_ref[...].astype(F32) + back).astype(BF16), (e0, e1, e23))

    @pl.when(step == 0)
    def _():
        gain_out[...] = jnp.zeros_like(gain_out)

    gain_out[...] += gain_grad


def token_grad(meta, turns, dts, weights, rest):
    width = weights[0].shape[2]
    step = 256
    rows = pl.BlockSpec((step, width), lambda i: (i, 0))
    full = lambda a: pl.BlockSpec(a.shape, lambda i, n=a.ndim: (0,) * n)
    cols = pl.BlockSpec((3, 4 * HD, step), lambda i: (0, 0, i))
    out = [struct((step, width), BF16)] * 2 + [struct((2, step, width), BF16), struct((1, width), F32)]
    return call(
        functools.partial(token_grad_body, turns),
        "token_grad",
        out,
        (meta, *dts, *weights, *rest),
        16,
        grid=(LEN // step,),
        in_specs=[SM] + [cols] * len(dts) + [full(w) for w in weights] + [rows] * 3 + [full(rest[3])],
        out_specs=[full(o) for o in out],
    )


def rope_tables(length, width):
    halfway = width // 2
    inverse = 10000.0 ** (-jnp.arange(halfway, dtype=F32) * 2.0 / width)
    angles = inverse[:, None] * jnp.arange(length, dtype=F32)[None, :]
    return jnp.cos(angles), jnp.sin(angles)


def swap(value, axis, size, mask):
    return lax.ppermute(value, axis, [(i, i ^ mask) for i in range(size)])


def added(*refs):
    total = refs[0].astype(F32)
    for ref in refs[1:]:
        total = total + ref.astype(F32)
    return total.astype(BF16)


def put(cond, ref, at, value):
    @pl.when(cond)
    def _():
        if at is None:
            ref[...] = value
        else:
            ref[at] = value


def start_body(meta_ref, a0, b0, a2, b2, keep_p, send_p, keep_q, send_q):
    step = pl.program_id(0)
    bit = meta_ref[3]
    two = meta_ref[4]
    for slot, (a, b) in enumerate(((a0, b0), (a2, b2))):
        value = added(a[0], b[0])
        put(step == bit, keep_p, slot, value)
        put(step == 1 - bit, send_p, slot, value)
        put(step == 2 + two, keep_q, slot, value)
        put(step == 3 - two, send_q, slot, value)


def start_sums(meta, dw0, in1, dw2, in3):
    rows = dw0.shape[0] * dw0.shape[1] // 4
    cols = dw0.shape[2]
    parts = [a.reshape(4, rows, cols) for a in (dw0, in1, dw2, in3)]
    out = [struct((2, rows, cols), BF16)] * 4
    return call(
        start_body,
        "start_sums",
        out,
        (meta, *parts),
        10,
        grid=(4,),
        in_specs=[SM] + [pl.BlockSpec((1, rows, cols), lambda i: (i, 0, 0))] * 4,
        out_specs=[pl.BlockSpec((2, rows, cols), lambda i: (0, 0, 0))] * 4,
    )


def second_body(meta_ref, kp, rp, kq, rq, keep, send_p, send_q):
    step = pl.program_id(0)
    for which, (k, r, send, bit) in enumerate(((kp, rp, send_p, meta_ref[4]), (kq, rq, send_q, meta_ref[3]))):
        for slot in range(2):
            value = added(k[slot, 0], r[slot, 0])
            put(step == bit, keep, (which, slot), value)
            put(step == 1 - bit, send, slot, value)


def second_sums(meta, *pieces):
    _, rows, cols = pieces[0].shape
    half = rows // 2
    full = lambda n: pl.BlockSpec((2,) * n + (half, cols), lambda i: (0,) * (n + 2))
    return call(
        second_body,
        "second_sums",
        [struct((2, 2, half, cols), BF16)] + [struct((2, half, cols), BF16)] * 2,
        (meta, *[p.reshape(2, 2, half, cols) for p in pieces]),
        10,
        grid=(2,),
        in_specs=[SM] + [pl.BlockSpec((2, 1, half, cols), lambda i: (0, i, 0, 0))] * 4,
        out_specs=[full(2), full(1), full(1)],
    )


def third_body(meta_ref, a, bp, bq, keep, send):
    which = pl.program_id(0)
    for part, b in enumerate((bp, bq)):

        @pl.when(which == part)
        def _():
            keep[0] = added(a[0, 0], b[0])
            send[0] = added(a[0, 1], b[1])


def third_sums(meta, a, bp, bq):
    _, _, rows, cols = a.shape
    whole = pl.BlockSpec((2, rows, cols), lambda i: (0, 0, 0))
    block = pl.BlockSpec((1, rows, cols), lambda i: (i, 0, 0))
    return call(
        third_body,
        "third_sums",
        [struct((2, rows, cols), BF16)] * 2,
        (meta, a, bp, bq),
        8,
        grid=(2,),
        in_specs=[SM, pl.BlockSpec((1, 2, rows, cols), lambda i: (i, 0, 0, 0)), whole, whole],
        out_specs=[block, block],
    )


def halve_body(bit_ref, a, b, keep, send):
    bit = bit_ref[0]
    step = pl.program_id(0)
    for which in range(2):
        value = added(a[which, 0], b[which, 0])
        put(step == bit, keep, which, value)
        put(step != bit, send, which, value)


def halve_sums(bit, a, b):
    _, rows, cols = a.shape
    half = rows // 2
    return call(
        halve_body,
        "halve_sums",
        [struct((2, half, cols), BF16)] * 2,
        (bit.reshape(1), a.reshape(2, 2, half, cols), b.reshape(2, 2, half, cols)),
        8,
        grid=(2,),
        in_specs=[SM] + [pl.BlockSpec((2, 1, half, cols), lambda i: (0, i, 0, 0))] * 2,
        out_specs=[pl.BlockSpec((2, half, cols), lambda i: (0, 0, 0))] * 2,
    )


def plain_body(tie_ref, a, b, out):
    out[...] = added(a[...], b[...])


def plain_sum(tie, a, b):
    return call(plain_body, "plain_sum", [struct(a.shape, BF16)], (tie, a, b), 6, in_specs=[SM, VM, VM], out_specs=[VM])[0]


def split_body(bit_ref, a, b, keep, send):
    bit = bit_ref[0]
    step = pl.program_id(0)
    value = added(a[0], b[0])
    put(step == bit, keep, None, value)
    put(step != bit, send, None, value)


def split_sums(bit, a, b):
    rows, cols = a.shape
    half = rows // 2
    return call(
        split_body,
        "split_sums",
        [struct((half, cols), BF16)] * 2,
        (bit.reshape(1), a.reshape(2, half, cols), b.reshape(2, half, cols)),
        6,
        grid=(2,),
        in_specs=[SM] + [pl.BlockSpec((1, half, cols), lambda i: (i, 0, 0))] * 2,
        out_specs=[pl.BlockSpec((half, cols), lambda i: (0, 0))] * 2,
    )


def merge_body(bit_ref, a, b, out):
    bit = bit_ref[0]
    out[bit] = a[...]
    out[1 - bit] = b[...]


def merge(bit, a, b):
    rows, cols = a.shape
    made = call(
        merge_body,
        "merge",
        [struct((2, rows, cols), BF16)],
        (bit.reshape(1), a, b),
        6,
        in_specs=[SM, VM, VM],
        out_specs=[VM],
    )[0]
    return made.reshape(2 * rows, cols)


def pair_body(bit_ref, a, b, out):
    bit = bit_ref[0]
    for which in range(2):
        out[which, bit] = a[which]
        out[which, 1 - bit] = b[which]


def pair_join(bit, a, b):
    _, rows, cols = a.shape
    made = call(
        pair_body,
        "pair_join",
        [struct((2, 2, rows, cols), BF16)],
        (bit.reshape(1), a, b),
        6,
        in_specs=[SM, VM, VM],
        out_specs=[VM],
    )[0]
    return made.reshape(2, 2 * rows, cols)


def cross_body(meta_ref, a, bp, bq, out_p, out_q):
    two = meta_ref[4]
    bit = meta_ref[3]
    out_p[two] = a[0]
    out_p[1 - two] = bp[...]
    out_q[bit] = a[1]
    out_q[1 - bit] = bq[...]


def cross_join(meta, a, bp, bq):
    _, rows, cols = a.shape
    made = call(
        cross_body,
        "cross_join",
        [struct((2, rows, cols), BF16)] * 2,
        (meta, a, bp, bq),
        6,
        in_specs=[SM, VM, VM, VM],
        out_specs=[VM, VM],
    )
    return [m.reshape(2 * rows, cols) for m in made]


def mlp_out_body(meta_ref, p, rp, q, rq, gu_ref, wd_ref, hold):
    bit = meta_ref[3]
    two = meta_ref[4]
    hold[bit] = p[...]
    hold[1 - bit] = rp[...]
    hold[2 + two] = q[...]
    hold[3 - two] = rq[...]
    rows = hold.shape[1]
    pair = gu_ref.shape[0]
    for which in range(2):
        gu_ref[which * rows : (which + 1) * rows, :] = hold[which].astype(F32)
    rest = pair - 2 * rows
    gu_ref[2 * rows :, :] = hold[2, :rest, :].astype(F32)
    wd_ref[:, : rows - rest] = hold[2, rest:, :].astype(F32).T
    wd_ref[:, rows - rest :] = hold[3].astype(F32).T


def mlp_out(meta, p, rp, q, rq, width):
    rows, units = p.shape
    return call(
        mlp_out_body,
        "mlp_out",
        [struct((2 * width, units), F32), struct((units, width), F32)],
        (meta, p, rp, q, rq),
        14,
        in_specs=[SM] + [VM] * 4,
        out_specs=[VM] * 2,
        scratch_shapes=[pltpu.VMEM((4, rows, units), BF16)],
    )


def core_body(count, meta_ref, *refs):
    evens, ins = refs[:count], refs[count : 2 * count]
    keep, send = refs[2 * count :]
    rows = evens[0].shape[1]
    for which, (a, b) in enumerate(zip(evens, ins)):
        keep[which * rows : (which + 1) * rows, :] = added(a[0], b[0])
        send[which * rows : (which + 1) * rows, :] = added(a[1], b[1])


def core_sums(meta, evens, ins):
    count = len(evens)
    _, rows, cols = evens[0].shape
    args = (meta, *evens, *ins)
    return call(
        functools.partial(core_body, count),
        "core_sums",
        [struct((count * rows, cols), BF16)] * 2,
        args,
        8,
        in_specs=[SM] + [VM] * (2 * count),
        out_specs=[VM] * 2,
    )


def spread_body(tie_ref, in_ref, out_ref):
    total = in_ref[0].astype(F32)
    for which in range(1, in_ref.shape[0]):
        total = total + in_ref[which].astype(F32)
    total = total.astype(BF16)
    for which in range(in_ref.shape[0]):
        out_ref[which] = total


def spread_sum(tie, pieces):
    return call(spread_body, "spread_sum", [struct(pieces.shape, BF16)], (tie, pieces), 16, in_specs=[SM, VM], out_specs=[VM])[0]


GAIN_ROWS = 8


def spread_gain_body(tie_ref, in_ref, gain_ref, out_ref):
    count, rows, width = in_ref.shape
    total = in_ref[0].astype(F32)
    for which in range(1, count):
        total = total + in_ref[which].astype(F32)
    total = total.astype(BF16)
    gains = gain_ref[...]
    high = gains.astype(BF16)
    low = (gains - high.astype(F32)).astype(BF16)
    head = jnp.concatenate([high, low, jnp.zeros((GAIN_ROWS - 4, width), BF16)], axis=0)
    for which in range(count):
        out_ref[which, :GAIN_ROWS, :] = head
        out_ref[which, GAIN_ROWS:, :] = total


def spread_gain_sum(tie, pieces, gains):
    count, rows, width = pieces.shape
    return call(
        spread_gain_body,
        "spread_sum",
        [struct((count, rows + GAIN_ROWS, width), BF16)],
        (tie, pieces, gains),
        16,
        in_specs=[SM, VM, VM],
        out_specs=[VM],
    )[0]


def exchange(value):
    return lax.all_to_all(value, "dp", 0, 0)


def attn_out_body(meta_ref, own_ref, other_ref, late_ref, qkv_ref, wo_ref, gain_ref, hold, hold_early):
    bit = meta_ref[3]
    hold_early[bit] = own_ref[...]
    hold_early[1 - bit] = other_ref[...]
    early = hold_early[...].reshape(9 * HD, hold.shape[1])
    wo_ref[...] = early[: 3 * HD, :].astype(F32)
    count = late_ref.shape[0]
    rows = late_ref.shape[1] - GAIN_ROWS
    gains = None
    for which in range(count):
        head = late_ref[which, :GAIN_ROWS, :].astype(F32)
        gains = head if gains is None else gains + head
        hold[which * rows : (which + 1) * rows, :] = late_ref[which, GAIN_ROWS:, :].astype(F32)
    gain_ref[...] = gains[0:2] + gains[2:4]
    for part in range(3):
        at = part * HD
        parts = [early[3 * HD + at : 3 * HD + at + HD, :], early[6 * HD + at : 6 * HD + at + HD, :]]
        parts = [p.astype(F32) for p in parts] + [hold[at : at + HD, :]]
        qkv_ref[part] = jnp.concatenate(parts, axis=0).T


def attn_out(meta, own, other, late):
    width = own.shape[1]
    return call(
        attn_out_body,
        "attn_out",
        [struct((3, width, 3 * HD), F32), struct((3 * HD, width), F32), struct((2, width), F32)],
        (meta, own, other, late),
        12,
        in_specs=[SM, VM, VM, VM],
        out_specs=[VM, VM, VM],
        scratch_shapes=[pltpu.VMEM((3 * HD, width), F32), pltpu.VMEM((2,) + own.shape, BF16)],
    )


def add_home_body(meta_ref, in_ref, p0, p1, p23, p3, out_ref):
    slot = pl.program_id(0) ^ meta_ref[2]
    for which, piece in enumerate((p0, p1, p23.at[0], p3)):

        @pl.when(slot == which)
        def _():
            out_ref[0] = in_ref[0] + piece[...].astype(F32)


def add_home(meta, base, pieces):
    count, rows, width = base.shape
    block = pl.BlockSpec((1, rows, width), lambda i: (i, 0, 0))
    full = lambda a: pl.BlockSpec(a.shape, lambda i, n=a.ndim: (0,) * n)
    return call(
        add_home_body,
        "add_home",
        [struct(base.shape, F32)],
        (meta, base, *pieces),
        8,
        grid=(count,),
        in_specs=[SM, block] + [full(p) for p in pieces],
        out_specs=[block],
    )[0]


def tie(value, *after):
    return lax.optimization_barrier((value, *after))[0]


def local(n_dp, inputs, w_qkv, w_out, w_gate_up, w_down, gain_attn, gain_mlp, piece_starts, out_grad):
    width = inputs.shape[2]
    units = w_down.shape[0]
    here = lax.axis_index("tensor").astype(jnp.int32)
    row = lax.axis_index("dp").astype(jnp.int32)
    bit = row & 1
    bits = [(row >> s) & 1 for s in range(n_dp.bit_length() - 1)]
    mine = lax.dynamic_index_in_dim(piece_starts, here, 0, keepdims=False)[0]
    meta = jnp.concatenate([mine, jnp.stack([here, bits[0], bits[1]])])
    one = gain_attn[None]
    two = gain_mlp[None]
    cosine, sine = rope_tables(LEN, HD)
    tensor = functools.partial(swap, axis="tensor", size=4)
    dp = functools.partial(swap, axis="dp", size=n_dp)

    def picks(whole):
        return [lax.dynamic_index_in_dim(whole, here ^ k, 0, keepdims=False).astype(BF16) for k in range(4)]

    def around(pieces):
        return [pieces[0]] + [tensor(pieces[k], mask=k) for k in range(1, 4)]

    def homeward(own, core, far):
        received = tensor(far, mask=2)
        return own, tensor(core, mask=1), received, tensor(received[1], mask=1)

    def far(half):
        direct = tensor(half, mask=2)
        other = dp(direct, mask=1)
        return direct, other, tensor(direct, mask=1), tensor(other, mask=1)

    x_mine = picks(inputs)
    xs = around(x_mine)
    wa0 = jnp.concatenate([jnp.swapaxes(w_qkv, 1, 2), w_out[None]]).astype(BF16)
    wa1 = tensor(wa0, mask=1)
    wa_far = far(tie(lax.dynamic_slice_in_dim(wa0, 2 * bit, 2, 0), xs[1]))
    wm0 = jnp.concatenate([w_gate_up, w_down.T[None]]).astype(BF16)
    wm1 = tensor(wm0, mask=1)
    wm_far = far(lax.dynamic_slice_in_dim(wm0.reshape(3 * width, units), 3 * width // 2 * bit, 3 * width // 2, 0))
    gs = around(picks(out_grad))

    last = [meta]

    def run(kernel, first, *args, **kw):
        out = kernel(tie(first, last[0]), *args, **kw)
        last[0] = out[0] if isinstance(out, (list, tuple)) else out
        return out

    x, n1, qa, ka, va = run(project_first, meta, xs, one, wa0, wa1, cosine, sine)
    mta, ma, la = run(attend, meta, qa, ka, va)
    qb, kb, vb, wa2, wa3 = run(project_next, meta, n1, wa_far, cosine, sine)
    wa = (wa0, wa1, wa2, wa3)
    mtb, mb, lb = run(attend, meta, qb, kb, vb)
    after, n2, n2t, g, gt = run(after_attention, meta, x, ma, mb, wa, two, gs)
    acc_out, acc_back, dw1, dw0 = run(mlp, meta, n2, n2t, g, gt, ((wm1,), (wm0,)))
    in1 = tensor(dw1, mask=1)
    acc_out, acc_back, dw3, dw2 = run(mlp, meta, n2, n2t, g, gt, (wm_far[2:], wm_far[:2]), (acc_out, acc_back))
    in3 = tensor(dw3, mask=1)
    middle_out = run(middle, meta, x, after, acc_out, acc_back, g, two, (mta, mtb), wa)
    home = homeward(*middle_out[:3])
    da, do, even_o, odd_o, gain_two = middle_out[3:]
    in_o = tensor(odd_o, mask=1)
    keep_p, send_p, keep_q, send_q = run(start_sums, meta, dw0, in1, dw2, in3)
    recv_p = dp(send_p, mask=1)
    recv_q = dp(send_q, mask=2)
    sets = ((qa, ka, va, mta, la), (qb, kb, vb, mtb, lb))
    back = lambda turn: run(lambda m: attend_back(turn, m, cosine, sine, n1, sets, do), meta)
    dt0, even0, odd0 = back(0)
    in0 = tensor(odd0, mask=1)
    dt1, even1, odd1 = back(1)
    in1_ = tensor(odd1, mask=1)
    keep, send_p, send_q = run(second_sums, tie(meta, home[2]), keep_p, recv_p, keep_q, recv_q)
    recv_p = dp(send_p, mask=2)
    recv_q = dp(send_q, mask=1)
    early, early_send = run(core_sums, meta, (even_o, even0, even1), (in_o, in0, in1_))
    early_recv = tensor(early_send, mask=2)
    dt2, even2, odd2 = back(2)
    in2 = tensor(odd2, mask=1)
    keep, send = run(third_sums, tie(meta, home[3]), keep, recv_p, recv_q)
    pieces = tensor(send, mask=2)
    late, late_send = run(core_sums, meta, (even2,), (in2,))
    late_recv = tensor(late_send, mask=2)
    early, early_send = run(split_sums, bits[0], early, early_recv)
    early_recv = dp(early_send, mask=1)
    *grads, gain_one = run(lambda m: token_grad(m, (0, 1, 2), (dt0, dt1, dt2), wa, (x, da, g, one)), meta)
    for shift in range(2, len(bits)):
        keep, send = run(halve_sums, bits[shift], keep, pieces)
        pieces = dp(send, mask=1 << shift)
    grads = homeward(grads[0], grads[1], tie(grads[2], late_recv))
    early, early_send = run(split_sums, bits[1], early, early_recv)
    early_recv = dp(early_send, mask=2)
    gains = jnp.concatenate([gain_one, gain_two])
    gains = gains + tensor(gains, mask=1)
    gains = gains + tensor(gains, mask=2)
    outputs = run(add_home, meta, inputs, home)
    for shift in range(2, len(bits)):
        early, early_send = run(split_sums, bits[shift], early, early_recv)
        early_recv = dp(early_send, mask=1 << shift)
    late = run(plain_sum, meta, late, late_recv)
    late = exchange(late.reshape(n_dp, -1, width))
    piece = run(plain_sum, meta, keep, pieces)
    other = dp(piece, mask=1 << (len(bits) - 1))
    early = run(plain_sum, meta, early, early_recv)
    early_recv = dp(early, mask=1 << (len(bits) - 1))
    late = exchange(run(spread_gain_sum, meta, late, gains))
    for shift in reversed(range(2, len(bits))):
        piece = run(pair_join, bits[shift], piece, other)
        if shift > 2:
            other = dp(piece, mask=1 << (shift - 1))
    recv_p = dp(piece[0], mask=2)
    recv_q = dp(piece[1], mask=1)
    for shift in reversed(range(2, len(bits))):
        early = run(merge, bits[shift], early, early_recv)
        early_recv = dp(early, mask=1 << (shift - 1))
    early = run(merge, bits[1], early, early_recv)
    early_recv = dp(early, mask=1)
    p, q = run(cross_join, meta, piece, recv_p, recv_q)
    recv_p = dp(p, mask=1)
    recv_q = dp(q, mask=2)
    input_grad = run(add_home, meta, out_grad, grads)
    grad_qkv, grad_out, gains = run(attn_out, meta, early, early_recv, late)
    grad_pair, grad_down = run(mlp_out, meta, p, recv_p, q, recv_q, width)
    return (
        outputs,
        input_grad,
        grad_qkv,
        grad_out,
        grad_pair.reshape(2, width, units),
        grad_down,
        gains[0],
        gains[1],
    )


def solution(mesh):
    rows = P(None, ("dp", "tensor"), None)
    weights = (P(None, None, "tensor"), P("tensor", None), P(None, None, "tensor"), P("tensor", None))
    return jax.shard_map(
        functools.partial(local, mesh.shape["dp"]),
        mesh=mesh,
        in_specs=(rows, *weights, P(), P(), P(None, "dp", None), rows),
        out_specs=(rows, rows, *weights, P(), P()),
        check_vma=False,
    )
```
